32 devices in a mesh: wide: 8 (over y, x, core), narrow: 4 (over z).
Axes of the slice: x: 2, y: 2, z: 4, core: 2. Of those that a mesh axis runs over, the one named last changes fastest.
Arguments:
- hidden_in: bfloat16 [16, 1024, 768], P('wide', 'narrow'), may hold values from -6 to 6
- positions: int32 [16, 1024], P('wide', 'narrow'), may hold values from 0 to 1023, as said below
- time_index: int32 [16], P('wide'), may hold values from 0 to 1023
- cond_table: bfloat16 [1024, 128], replicated, may hold values from -5 to 5
- ada_weight: bfloat16 [128, 4608], replicated, may hold values from -0.5 to 0.5
- norm1_gain: bfloat16 [768], replicated, may hold values from 0.099609375 to 1.8984375
- qkv_weight: bfloat16 [768, 2304], replicated, may hold values from -0.21875 to 0.21875
- out_weight: bfloat16 [768, 768], replicated, may hold values from -0.875 to 0.875
- norm2_gain: bfloat16 [768], replicated, may hold values from 0.099609375 to 1.8984375
- up_weight: bfloat16 [768, 3072], replicated, may hold values from -0.21875 to 0.21875
- down_weight: bfloat16 [3072, 768], replicated, may hold values from -0.21875 to 0.21875
- cotangent: bfloat16 [16, 1024, 768], P('wide', 'narrow'), may hold values from -6 to 6
Outputs:
- hidden_out: bfloat16 [16, 1024, 768], P('wide', 'narrow')
- hidden_grad: bfloat16 [16, 1024, 768], P('wide', 'narrow')
- cond_table_grad: float32 [1024, 128], P('wide', 'narrow')
- ada_weight_grad: float32 [128, 4608], P('narrow', 'wide')
- norm1_gain_grad: float32 [768], P('wide')
- qkv_weight_grad: float32 [768, 2304], P('wide', 'narrow')
- out_weight_grad: float32 [768, 768], P('wide', 'narrow')
- norm2_gain_grad: float32 [768], P('wide')
- up_weight_grad: float32 [768, 3072], P('wide', 'narrow')
- down_weight_grad: float32 [3072, 768], P('wide', 'narrow')
The draws below stay inside these ranges and needn't reach their ends.
Inputs may be any that keep to these rules, and one draw needn't show every extreme that they name: positions count up by one from the start of each packed document, every row starts a document at its first token, and one row is a single document.
All inputs are finite; a program needn't handle non-finite values.
Results may differ from the reference program's by a relative error of at most 0.015.
The reference program's roundings to bfloat16 on the way count: a program that leaves them out, or rounds other values in their place, can miss the bound.
Values may be sent and summed in bfloat16 or wider, within the bound.
No kernel may reach another device: no remote copies, remote signals or barrier semaphores. Data moves between devices by JAX's collectives and lax.ppermute only.
A program may use at most 192 MiB of HBM per device.

```python
import jax
import jax.numpy as jnp
from jax import lax

D = 768
HEADS = 12
HEAD_DIM = 64
FF = 3072
COND = 128
TIMES = 1024
LENGTH = 1024
ROWS = 16


def draw_positions(key, part):
    start_key = jax.random.fold_in(key, 11)
    whole_key = jax.random.fold_in(key, 23)
    spacing = max(2, LENGTH // 4)
    starts = jax.random.randint(start_key, (ROWS, LENGTH), 0, spacing) == 0
    whole_row = jax.random.randint(whole_key, (), 0, ROWS)
    row_number = jnp.broadcast_to(jnp.arange(ROWS, dtype=jnp.int32)[:, None], (ROWS, LENGTH))
    starts = starts & (row_number != whole_row)
    index = jnp.broadcast_to(jnp.arange(LENGTH, dtype=jnp.int32)[None, :], (ROWS, LENGTH))
    begins = jnp.where(starts | (index == 0), index, 0)
    return (index - lax.cummax(begins, axis=1)).astype(jnp.int32)


def with_ends(entries, stream_key, least, largest):
    longest = entries.shape.index(max(entries.shape))
    spots = []
    for shift in (0, 1):
        where = [jax.random.randint(jax.random.fold_in(stream_key, axis), (), 0, length) for axis, length in enumerate(entries.shape)]
        where[longest] = (where[longest] + shift) % entries.shape[longest]
        spots.append(tuple(where))
    return entries.at[spots[0]].set(least).at[spots[1]].set(largest)


def with_spikes(entries, key, source, target, blocks, factor):
    def block_of(position):
        return (jnp.arange(entries.shape[position]) // (entries.shape[position] // blocks)).reshape((-1,) + (1,) * (entries.ndim - 1 - position))

    first = jax.random.permutation(key, blocks)[block_of(target)]
    second = (block_of(target) + blocks // 2) % blocks
    return jnp.where((block_of(source) == first) | (block_of(source) == second), factor * entries, entries)


def level_of(key, extent, shards, low, high):
    factor_of, own = 1.0, jax.random.fold_in(key, 6)
    for dim, shards_of in shards:
        draws = jnp.exp(jax.random.uniform(jax.random.fold_in(own, dim), (shards_of,), jnp.float32, low / len(shards), high / len(shards)))
        factor_of = factor_of * jnp.repeat(draws, extent[dim] // shards_of).reshape([-1 if axis == dim else 1 for axis in range(len(extent))])
    return factor_of


def scatter_about(rng, shape, width, limit, split=(), held_as=jnp.bfloat16):
    level = level_of(rng, shape, split, -0.22, 0.18) if split else 1.0
    values = jax.random.normal(rng, shape, jnp.float32) * width * level
    return jnp.minimum(jnp.maximum(values, -limit), limit).astype(held_as)


def heavy_noise(key, dims, width, most, shards, heavy, kind=jnp.bfloat16):
    array = width * jax.random.normal(key, dims, jnp.float32)
    if shards:
        array = array * level_of(key, dims, shards, -0.22, 0.18)
    return jnp.clip(with_spikes(array, jax.random.fold_in(key, 3), *heavy), -most, most).astype(kind)


def setup_inputs(seed: int = 0) -> dict:
    splits = jax.random.split(jax.random.key(seed), 13)
    hidden_in = scatter_about(splits[0], (ROWS, LENGTH, D), 1.0, 6.0, ((0, 8), (1, 4)))
    positions = draw_positions(jax.random.fold_in(splits[12], 71), 0)
    time_index = with_ends(jax.random.randint(splits[2], (ROWS,), 0, TIMES), jax.random.fold_in(splits[2], 1), 0, TIMES - 1).astype(jnp.int32)
    cond_table = scatter_about(splits[3], (TIMES, COND), 1.0, 5.0)
    ada_weight = scatter_about(splits[4], (COND, 6 * D), COND ** -0.5, 0.5)
    norm1_gain = jnp.clip(1.0 + 0.18 * jax.random.normal(splits[5], (D,), jnp.float32), 0.099609375, 1.8984375).astype(jnp.bfloat16)
    qkv_weight = scatter_about(splits[6], (D, 3 * D), D ** -0.5, 0.21875)
    out_weight = scatter_about(splits[7], (D, D), (D // 16) ** -0.5, 0.875)
    norm2_gain = jnp.clip(1.0 + 0.18 * jax.random.normal(splits[8], (D,), jnp.float32), 0.099609375, 1.8984375).astype(jnp.bfloat16)
    up_weight = scatter_about(splits[9], (D, FF), D ** -0.5, 0.21875)
    down_weight = scatter_about(splits[10], (FF, D), (FF // 4) ** -0.5, 0.21875)
    cotangent = heavy_noise(splits[11], (ROWS, LENGTH, D), 1.0, 6.0, ((0, 8), (1, 4)), (0, 2, 8, 2.0))
    return dict(hidden_in=hidden_in, positions=positions, time_index=time_index, cond_table=cond_table, ada_weight=ada_weight, norm1_gain=norm1_gain, qkv_weight=qkv_weight, out_weight=out_weight, norm2_gain=norm2_gain, up_weight=up_weight, down_weight=down_weight, cotangent=cotangent)


@jax.custom_vjp
def low(v):
    return lax.optimization_barrier(v.astype(jnp.bfloat16)).astype(jnp.float32)

@jax.custom_vjp
def low_back(v):
    return v

def low_keep(v):
    return (low(v), None)

def low_pass(kept, grad):
    return (grad,)

def back_keep(v):
    return (v, None)

def back_low(kept, grad):
    return (low(grad),)
low.defvjp(low_keep, low_pass)
low_back.defvjp(back_keep, back_low)
HIGHEST = lax.Precision.HIGHEST
norm_eps = 1e-05

def matmul(left, right):
    return jnp.dot(left, right, precision=HIGHEST, preferred_element_type=jnp.float32)

def norm_mod(hidden, gain, shift, scale):
    center = hidden - lax.optimization_barrier(jnp.mean(hidden, axis=-1, keepdims=True))
    variance = lax.optimization_barrier(jnp.mean(center * center, axis=-1, keepdims=True))
    return center * lax.rsqrt(variance + norm_eps) * gain * (1.0 + scale) + shift

def rotary(values, positions):
    half_dim = values.shape[-1] // 2
    frequency = 10000.0 ** (-jnp.arange(half_dim, dtype=jnp.float32) / half_dim)
    angles = positions.astype(jnp.float32)[..., None, None] * frequency
    cosine = jnp.cos(angles)
    sine = jnp.sin(angles)
    first_half = values[..., :half_dim]
    second_half = values[..., half_dim:]
    return jnp.concatenate([first_half * cosine - second_half * sine, second_half * cosine + first_half * sine], axis=-1)

def layer_row(hidden, positions, embedded, ada, gain_one, w_qkv, w_out, gain_two, w_up, w_down):
    length = hidden.shape[0]
    condition = low(jax.nn.silu(embedded))
    modulation = matmul(condition[None, :], ada)[0].reshape(6, D)
    shift_one, scale_one, gate_one = (modulation[0], modulation[1], modulation[2])
    shift_two, scale_two, gate_two = (modulation[3], modulation[4], modulation[5])
    norm_one = low(norm_mod(hidden, gain_one, shift_one, scale_one))
    qkv = low_back(matmul(norm_one, w_qkv)).reshape(length, 3, HEADS, HEAD_DIM)
    queries = low_back(low(rotary(qkv[:, 0], positions)))
    key_rows = low_back(low(rotary(qkv[:, 1], positions)))
    value_rows = low_back(low(qkv[:, 2]))
    scores = low_back(jnp.einsum('qhd,khd->hqk', queries, key_rows, precision=HIGHEST) * HEAD_DIM ** (-0.5))
    shifted = scores - lax.optimization_barrier(jnp.max(scores, axis=-1, keepdims=True))
    expo = jnp.exp(shifted)
    probs = expo / lax.optimization_barrier(jnp.sum(expo, axis=-1, keepdims=True))
    probs_low = low(probs)
    attended = low_back(low(jnp.einsum('hqk,khd->qhd', probs_low, value_rows, precision=HIGHEST))).reshape(length, D)
    projected = low_back(matmul(attended, w_out))
    middle = hidden + gate_one * projected
    norm_two = low(norm_mod(middle, gain_two, shift_two, scale_two))
    up_part = low_back(matmul(norm_two, w_up))
    activated = low(jax.nn.gelu(up_part, approximate=True))
    down_part = low_back(matmul(activated, w_down))
    return middle + gate_two * down_part

def reference(hidden_in, positions, time_index, cond_table, ada_weight, norm1_gain, qkv_weight, out_weight, norm2_gain, up_weight, down_weight, cotangent):
    weights = tuple((w_item.astype(jnp.float32) for w_item in (cond_table, ada_weight, norm1_gain, qkv_weight, out_weight, norm2_gain, up_weight, down_weight)))

    def one_row(totals, row_item):
        row_hidden, row_positions, row_time, row_cotangent = row_item

        def forward(hidden_row, table, ada, gain_one, w_qkv, w_out, gain_two, w_up, w_down):
            embedded = table[row_time]
            return layer_row(hidden_row, row_positions, embedded, ada, gain_one, w_qkv, w_out, gain_two, w_up, w_down)
        result, pull_back = jax.vjp(forward, row_hidden.astype(jnp.float32), *weights)
        grads = pull_back(row_cotangent.astype(jnp.float32))
        totals = tuple((acc + new for acc, new in zip(totals, grads[1:])))
        return (totals, (result.astype(jnp.bfloat16), grads[0].astype(jnp.bfloat16)))
    zeros = tuple((jnp.zeros(w_item.shape, jnp.float32) for w_item in weights))
    totals, (outputs, input_grads) = lax.scan(one_row, zeros, (hidden_in, positions, time_index, cotangent))
    return (outputs, input_grads, totals[0], totals[1], totals[2], totals[3], totals[4], totals[5], totals[6], totals[7])
```

```python
import jax
import jax.numpy as jnp
from jax import lax
from jax.sharding import PartitionSpec as P

HEAD_DIM = 64
HIGHEST = lax.Precision.HIGHEST
norm_eps = 1e-05
AXES = ("wide", "narrow")
F32 = jnp.float32
BF16 = jnp.bfloat16


def dot(left, right):
    return jnp.dot(left, right, preferred_element_type=F32)


def tdot(left, right):
    return lax.dot_general(left, right, (((0,), (0,)), ((), ())), preferred_element_type=F32)


def ndot(left, right):
    return lax.dot_general(left, right, (((1,), (1,)), ((), ())), preferred_element_type=F32)


def gelu_tanh(values):
    return jax.nn.gelu(values, approximate=True)


def pairs(wide, narrow, target):
    result = []
    for w in range(wide):
        for n in range(narrow):
            w_to, n_to = target(w, n)
            result.append((w * narrow + n, w_to * narrow + n_to))
    return result


def inverse(table):
    return [(target, source) for source, target in table]


def rotate(values, cosine, sine, sign):
    half = HEAD_DIM // 2
    first = values[..., :half]
    second = values[..., half:]
    return jnp.concatenate(
        [first * cosine - sign * second * sine, second * cosine + sign * first * sine], axis=-1
    )


def normalize(hidden):
    center = hidden - jnp.mean(hidden, axis=-1, keepdims=True)
    variance = jnp.mean(center * center, axis=-1, keepdims=True)
    inverse_std = lax.rsqrt(variance + norm_eps)
    return center * inverse_std, inverse_std


def normalize_back(grad, xhat, inverse_std):
    mean_grad = jnp.mean(grad, axis=-1, keepdims=True)
    mean_both = jnp.mean(grad * xhat, axis=-1, keepdims=True)
    return (grad - mean_grad - xhat * mean_both) * inverse_std


def make(wide, narrow):
    wide_bits = wide.bit_length() - 1

    def first_message(w, n):
        p, c = w // 2, w % 2
        return 2 * p + n // 2, 2 * c + n % 2

    def second_message(w, n):
        p, c = w // 2, w % 2
        return 2 * p + n // 2, 2 * c + 1 - n % 2

    message_one = pairs(wide, narrow, first_message)
    message_two = pairs(wide, narrow, second_message)
    flip = [pairs(wide, narrow, lambda w, n, b=b: (w ^ (1 << b), n)) for b in range(wide_bits)]
    narrow_near = pairs(wide, narrow, lambda w, n: (w, n ^ 1))
    narrow_far = pairs(wide, narrow, lambda w, n: (w, narrow - 1 - n))

    def on_device(
        hidden_in,
        positions,
        time_index,
        cond_table,
        ada_weight,
        norm1_gain,
        qkv_weight,
        out_weight,
        norm2_gain,
        up_weight,
        down_weight,
        cotangent,
    ):
        w = lax.axis_index("wide")
        n = lax.axis_index("narrow")
        core = w % 2
        part_len, width = hidden_in.shape[1:]
        heads = width // HEAD_DIM
        odd = n % 2

        def take(array, index):
            return lax.dynamic_index_in_dim(array, index, axis=0, keepdims=False)

        def spread(array):
            one = lax.ppermute(take(array, odd), AXES, message_one)
            two = lax.ppermute(take(array, 1 - odd), AXES, message_two)
            return jnp.concatenate([one, two], axis=0)

        def gather(array):
            one = lax.ppermute(array[:part_len], AXES, inverse(message_one))
            two = lax.ppermute(array[part_len:], AXES, inverse(message_two))
            return jnp.stack([jnp.where(odd == 0, one, two), jnp.where(odd == 0, two, one)])

        def reduce_blocks(array, order):
            block = array.shape[2:]
            current = array.reshape((2,) * wide_bits + (narrow,) + block)
            axes = list(range(wide_bits - 1, -1, -1))
            for bit in order:
                axis = axes.index(bit)
                mine = (w >> bit) & 1
                send = lax.dynamic_index_in_dim(current, 1 - mine, axis=axis, keepdims=False)
                keep = lax.dynamic_index_in_dim(current, mine, axis=axis, keepdims=False)
                received = lax.ppermute(send, AXES, flip[bit])
                current = (keep.astype(F32) + received.astype(F32)).astype(BF16)
                axes.pop(axis)
            near = n ^ 1
            send = jnp.stack([take(current, near), take(current, narrow - 1 - near)])
            keep = jnp.stack([take(current, n), take(current, narrow - 1 - n)])
            received = lax.ppermute(send, AXES, narrow_near)
            current = keep.astype(F32) + received.astype(F32)
            received = lax.ppermute(current[1].astype(BF16), AXES, narrow_far)
            return current[0] + received.astype(F32)

        hidden = spread(hidden_in).astype(F32)
        place = spread(positions)
        d_out = spread(cotangent).astype(F32)
        other_time = lax.ppermute(time_index, AXES, flip[0])
        row_time = jnp.where(n // 2 == core, time_index[n % 2], other_time[n % 2])
        embedded = lax.dynamic_slice_in_dim(cond_table, row_time, 1, axis=0).astype(F32)
        gate = jax.nn.sigmoid(embedded)
        condition = (embedded * gate).astype(BF16)
        modulation = dot(condition, ada_weight).reshape(6, 1, width)
        shift_one, scale_one, gate_one, shift_two, scale_two, gate_two = modulation
        gain_one = norm1_gain.astype(F32)
        gain_two = norm2_gain.astype(F32)
        tokens = hidden.shape[0]

        xhat_one, std_one = normalize(hidden)
        norm_one = (xhat_one * gain_one * (1.0 + scale_one) + shift_one).astype(BF16)
        qkv = dot(norm_one, qkv_weight)
        half = HEAD_DIM // 2
        frequency = 10000.0 ** (-jnp.arange(half, dtype=F32) / half)
        angles = place.astype(F32)[:, None, None] * frequency
        cosine, sine = jnp.cos(angles), jnp.sin(angles)

        def rotated(part, sign):
            return (
                rotate(part.reshape(tokens, heads, HEAD_DIM), cosine, sine, sign)
                .reshape(tokens, width)
                .astype(BF16)
            )

        queries = rotated(qkv[:, :width], 1.0)
        keys = rotated(qkv[:, width : 2 * width], 1.0)
        values = qkv[:, 2 * width :].astype(BF16)
        mine = jnp.concatenate([keys, values], axis=1)
        other = lax.ppermute(mine, AXES, flip[0])
        both = jnp.concatenate([mine, other], axis=0)

        group = 3

        def split_heads(array):
            return array.reshape(-1, heads // group, group, HEAD_DIM).transpose(1, 2, 0, 3)

        def join_heads(array):
            return array.transpose(2, 0, 1, 3).reshape(-1, width)

        q_heads = split_heads(queries)
        k_heads = split_heads(both[:, :width])
        v_heads = split_heads(both[:, width:])

        def attend(item):
            q, k, v = item
            scores = jnp.einsum("hqd,hkd->hqk", q, k, preferred_element_type=F32) * HEAD_DIM**-0.5
            row_max = jnp.max(scores, axis=-1, keepdims=True)
            expo = jnp.exp(scores - row_max)
            total = jnp.sum(expo, axis=-1, keepdims=True)
            probs = (expo / total).astype(BF16)
            result = jnp.einsum("hqk,hkd->hqd", probs, v, preferred_element_type=F32)
            return result.astype(BF16), row_max + jnp.log(total)

        attended_heads, log_total = lax.map(attend, (q_heads, k_heads, v_heads))
        attended = join_heads(attended_heads)
        projected = dot(attended, out_weight)
        middle = hidden + gate_one * projected
        xhat_two, std_two = normalize(middle)
        norm_two = (xhat_two * gain_two * (1.0 + scale_two) + shift_two).astype(BF16)
        up = dot(norm_two, up_weight)
        activated, gelu_back = jax.vjp(gelu_tanh, up)
        activated = activated.astype(BF16)
        down = dot(activated, down_weight)
        hidden_out = gather((middle + gate_two * down).astype(BF16))
        d_gate_two = jnp.sum(d_out * down, axis=0)
        d_down = (d_out * gate_two).astype(BF16)
        grad_down = tdot(activated, d_down)
        d_up = gelu_back(ndot(d_down, down_weight))[0].astype(BF16)
        grad_up = tdot(norm_two, d_up)
        d_norm_two = ndot(d_up, up_weight)
        d_shift_two = jnp.sum(d_norm_two, axis=0)
        sum_two = jnp.sum(d_norm_two * xhat_two, axis=0)
        grad_gain_two = sum_two * (1.0 + scale_two[0])
        d_scale_two = sum_two * gain_two
        d_middle = d_out + normalize_back(
            d_norm_two * (gain_two * (1.0 + scale_two)), xhat_two, std_two
        )
        d_gate_one = jnp.sum(d_middle * projected, axis=0)
        d_projected = (d_middle * gate_one).astype(BF16)
        grad_out = tdot(attended, d_projected)
        d_attended = ndot(d_projected, out_weight).astype(BF16)

        def attend_back(item):
            q, k, v, d_result, total = item
            scores = jnp.einsum("hqd,hkd->hqk", q, k, preferred_element_type=F32) * HEAD_DIM**-0.5
            probs = jnp.exp(scores - total)
            d_v = jnp.einsum("hqk,hqd->hkd", probs.astype(BF16), d_result, preferred_element_type=F32)
            d_probs = jnp.einsum("hqd,hkd->hqk", d_result, v, preferred_element_type=F32)
            d_scores = probs * (d_probs - jnp.sum(probs * d_probs, axis=-1, keepdims=True))
            d_low = d_scores.astype(BF16)
            d_q = jnp.einsum("hqk,hkd->hqd", d_low, k, preferred_element_type=F32) * HEAD_DIM**-0.5
            d_k = jnp.einsum("hqk,hqd->hkd", d_low, q, preferred_element_type=F32) * HEAD_DIM**-0.5
            return d_q.astype(BF16), d_k.astype(BF16), d_v.astype(BF16)

        d_q_heads, d_k_heads, d_v_heads = lax.map(
            attend_back, (q_heads, k_heads, v_heads, split_heads(d_attended), log_total)
        )
        d_query = join_heads(d_q_heads)
        d_both = jnp.concatenate([join_heads(d_k_heads), join_heads(d_v_heads)], axis=1)
        received = lax.ppermute(d_both[tokens:], AXES, flip[0])
        d_mine = (d_both[:tokens].astype(F32) + received.astype(F32)).astype(BF16)
        d_qkv = jnp.concatenate(
            [
                rotated(d_query.astype(F32), -1.0),
                rotated(d_mine[:, :width].astype(F32), -1.0),
                d_mine[:, width:],
            ],
            axis=1,
        )
        grad_qkv = tdot(norm_one, d_qkv)
        d_norm_one = ndot(d_qkv, qkv_weight)
        d_shift_one = jnp.sum(d_norm_one, axis=0)
        sum_one = jnp.sum(d_norm_one * xhat_one, axis=0)
        grad_gain_one = sum_one * (1.0 + scale_one[0])
        d_scale_one = sum_one * gain_one
        hidden_grad = d_middle + normalize_back(
            d_norm_one * (gain_one * (1.0 + scale_one)), xhat_one, std_one
        )
        hidden_grad = gather(hidden_grad.astype(BF16))

        d_modulation = jnp.concatenate(
            [d_shift_one, d_scale_one, d_gate_one, d_shift_two, d_scale_two, d_gate_two]
        )[None, :]
        d_condition = lax.dot_general(
            d_modulation,
            ada_weight.astype(F32),
            (((1,), (1,)), ((), ())),
            precision=HIGHEST,
            preferred_element_type=F32,
        )
        d_embedded = d_condition * gate * (1.0 + embedded * (1.0 - gate))
        times = cond_table.shape[0]
        grad_table = jnp.where(
            jnp.arange(times, dtype=jnp.int32)[:, None] == row_time, d_embedded, 0.0
        )
        grad_ada = condition.astype(F32).T * d_modulation

        def blocks(grad):
            rows, cols = grad.shape
            split = grad.astype(BF16).reshape(wide, rows // wide, narrow, cols // narrow)
            return split.transpose(0, 2, 1, 3).reshape(wide, narrow, -1, 128)

        def blocks_other(grad):
            rows, cols = grad.shape
            split = grad.astype(BF16).reshape(narrow, rows // narrow, wide, cols // wide)
            return split.transpose(2, 0, 1, 3).reshape(wide, narrow, -1)

        def blocks_gain(grad):
            split = grad.astype(BF16).reshape(wide, 1, -1)
            return jnp.broadcast_to(split, (wide, narrow, split.shape[2]))

        rest = jnp.concatenate(
            [
                blocks(grad_table).reshape(wide, narrow, -1),
                blocks_other(grad_ada),
                blocks_gain(grad_gain_one),
                blocks_gain(grad_gain_two),
            ],
            axis=2,
        )
        up_order = list(range(wide_bits))
        down_order = [0] + list(range(wide_bits - 1, 0, -1))
        sum_down = reduce_blocks(blocks(grad_down), down_order)
        sum_up = reduce_blocks(blocks(grad_up), up_order)
        sum_out = reduce_blocks(blocks(grad_out), up_order)
        sum_qkv = reduce_blocks(blocks(grad_qkv), down_order)
        sum_rest = reduce_blocks(rest, up_order)

        def block_shape(array):
            return array.shape[0] // wide, array.shape[1] // narrow

        table_count = times // wide * (cond_table.shape[1] // narrow)
        ada_shape = (ada_weight.shape[0] // narrow, ada_weight.shape[1] // wide)
        ada_count = ada_shape[0] * ada_shape[1]
        gain_count = width // wide
        at = table_count + ada_count
        return (
            hidden_out,
            hidden_grad,
            sum_rest[:table_count].reshape(block_shape(cond_table)),
            sum_rest[table_count:at].reshape(ada_shape),
            sum_rest[at : at + gain_count],
            sum_qkv.reshape(block_shape(qkv_weight)),
            sum_out.reshape(block_shape(out_weight)),
            sum_rest[at + gain_count :],
            sum_up.reshape(block_shape(up_weight)),
            sum_down.reshape(block_shape(down_weight)),
        )

    return on_device


def solution(mesh):
    in_specs = (
        P("wide", "narrow", None),
        P("wide", "narrow"),
        P("wide"),
        P(),
        P(),
        P(),
        P(),
        P(),
        P(),
        P(),
        P(),
        P("wide", "narrow", None),
    )
    out_specs = (
        P("wide", "narrow", None),
        P("wide", "narrow", None),
        P("wide", "narrow"),
        P("narrow", "wide"),
        P("wide"),
        P("wide", "narrow"),
        P("wide", "narrow"),
        P("wide"),
        P("wide", "narrow"),
        P("wide", "narrow"),
    )
    return jax.shard_map(
        make(mesh.shape["wide"], mesh.shape["narrow"]),
        mesh=mesh,
        in_specs=in_specs,
        out_specs=out_specs,
        check_vma=False,
    )
```

```python
import functools

import jax
import jax.numpy as jnp
from jax import lax
from jax.experimental import pallas as pl
from jax.experimental.pallas import tpu as pltpu
from jax.sharding import PartitionSpec as P

HEAD_DIM = 64
HALF = HEAD_DIM // 2
GROUP = 4
LOG2E = 1.4426950408889634
SCALE = HEAD_DIM**-0.5
HIGHEST = lax.Precision.HIGHEST
norm_eps = 1e-05
AXES = ("wide", "narrow")
EXTRA = 16
F32 = jnp.float32
BF16 = jnp.bfloat16
MIB = 1 << 20


def cost(us):
    return pl.CostEstimate(flops=int(us * 1.15e9), bytes_accessed=int(us * 3.7e6), transcendentals=0)


LIGHT = cost(0.01)
HEAVY = cost(100)


def dot(left, right):
    return jnp.dot(left, right, preferred_element_type=F32)


def ndot(left, right):
    return lax.dot_general(left, right, (((1,), (1,)), ((), ())), preferred_element_type=F32)


def pairs(wide, narrow, target):
    result = []
    for w in range(wide):
        for n in range(narrow):
            w_to, n_to = target(w, n)
            result.append((w * narrow + n, w_to * narrow + n_to))
    return result


def inverse(table):
    return [(target, source) for source, target in table]


def normalize(hidden):
    center = hidden - jnp.mean(hidden, axis=-1, keepdims=True)
    variance = jnp.mean(center * center, axis=-1, keepdims=True)
    inverse_std = lax.rsqrt(variance + norm_eps)
    return center * inverse_std, inverse_std


def normalize_back(grad, xhat, inverse_std):
    mean_grad = jnp.mean(grad, axis=-1, keepdims=True)
    mean_both = jnp.mean(grad * xhat, axis=-1, keepdims=True)
    return (grad - mean_grad - xhat * mean_both) * inverse_std


def rotate(values, cosine, sine):
    width = values.shape[1]
    lane = lax.broadcasted_iota(jnp.int32, values.shape, 1)
    ahead = pltpu.roll(values, width - HALF, 1)
    behind = pltpu.roll(values, HALF, 1)
    swapped = jnp.where(lane % HEAD_DIM < HALF, ahead, behind)
    repeat = width // cosine.shape[1]
    cosine = jnp.concatenate([cosine] * repeat, axis=1)
    sine = jnp.concatenate([sine] * repeat, axis=1)
    return values * cosine + swapped * sine


def whole(shape):
    return pl.BlockSpec(shape, lambda *index: (0,) * len(shape))


def params(mib):
    return pltpu.CompilerParams(vmem_limit_bytes=mib * MIB)


def shape_of(shape, dtype):
    return jax.ShapeDtypeStruct(shape, dtype)


def project_kernel(one, two, mod, gain, weight, cosine, sine, q_out, kv_out, norm_t, norm):
    step = pl.program_id(0)
    part = one.shape[0]

    @pl.when(step == 0)
    def first():
        for index, ref in enumerate((one, two)):
            xhat, unused = normalize(ref[...].astype(F32))
            value = xhat * gain[...].astype(F32) * (1.0 + mod[1:2, :]) + mod[0:1, :]
            norm[index * part : (index + 1) * part, :] = value.astype(BF16)
        norm_t[...] = norm[...].T

    result = dot(norm[...], weight[...])

    @pl.when(step == 0)
    def query():
        q_out[...] = (rotate(result, cosine[...], sine[...]).astype(BF16).astype(F32) * SCALE).astype(BF16)

    @pl.when(step == 1)
    def key():
        kv_out[0] = rotate(result, cosine[...], sine[...]).astype(BF16)

    @pl.when(step == 2)
    def value():
        kv_out[0] = result.astype(BF16)


def project(one, two, mod, gain, weight, cosine, sine):
    part, width = one.shape
    tokens = 2 * part
    return pl.pallas_call(
        project_kernel,
        grid=(3,),
        in_specs=[
            whole((part, width)),
            whole((part, width)),
            whole(mod.shape),
            whole((1, width)),
            pl.BlockSpec((width, width), lambda i: (0, i)),
            whole(cosine.shape),
            whole(sine.shape),
        ],
        out_specs=[
            whole((tokens, width)),
            pl.BlockSpec((1, tokens, width), lambda i: (jnp.maximum(i - 1, 0), 0, 0)),
            whole((width, tokens)),
        ],
        out_shape=[
            shape_of((tokens, width), BF16),
            shape_of((2, tokens, width), BF16),
            shape_of((width, tokens), BF16),
        ],
        scratch_shapes=[pltpu.VMEM((tokens, width), BF16)],
        compiler_params=params(28),
        cost_estimate=LIGHT,
        name="project",
    )(one, two, mod, gain, weight, cosine, sine)


def attend_kernel(q, kv, kv_other, out, out_t, log_total, keys, values_t):
    tokens, lanes = q.shape
    keys[:tokens, :] = kv[0]
    keys[tokens:, :] = kv_other[0]
    values_t[:, :tokens] = kv[1].T
    values_t[:, tokens:] = kv_other[1].T
    q_t = q[...].T
    row = lax.broadcasted_iota(jnp.int32, q_t.shape, 0) // HEAD_DIM
    log_total[...] = jnp.zeros_like(log_total)
    for head in range(GROUP):
        q_head = jnp.where(row == head, q_t, jnp.zeros_like(q_t))
        scores = dot(keys[...], q_head)
        top = jnp.max(scores, axis=0, keepdims=True)
        expo = jnp.exp2((scores - top) * LOG2E)
        total = jnp.sum(expo, axis=0, keepdims=True)
        rows = slice(head * HEAD_DIM, (head + 1) * HEAD_DIM)
        result = dot(values_t[rows, :], expo.astype(BF16)) / total
        out_t[rows, :] = result.astype(BF16)
        log_total[0, head : head + 1, :] = top + jnp.log(total)
    out[...] = out_t[...].T


def attend(q, kv, kv_other):
    tokens, width = q.shape
    lanes = GROUP * HEAD_DIM
    groups = width // lanes
    pair = pl.BlockSpec((2, tokens, lanes), lambda g: (0, 0, g))
    flat = pl.BlockSpec((tokens, lanes), lambda g: (0, g))
    return pl.pallas_call(
        attend_kernel,
        grid=(groups,),
        in_specs=[flat, pair, pair],
        out_specs=[
            flat,
            pl.BlockSpec((lanes, tokens), lambda g: (g, 0)),
            pl.BlockSpec((1, 8, tokens), lambda g: (g, 0, 0)),
        ],
        out_shape=[
            shape_of((tokens, width), BF16),
            shape_of((width, tokens), BF16),
            shape_of((groups, 8, tokens), F32),
        ],
        scratch_shapes=[
            pltpu.VMEM((2 * tokens, lanes), BF16),
            pltpu.VMEM((lanes, 2 * tokens), BF16),
        ],
        compiler_params=params(24),
        cost_estimate=LIGHT,
        name="attend",
    )(q, kv, kv_other)


def attend_back_kernel(
    q, kv, kv_other, d_out, out_t, log_total, dq, d_own, d_other, keys_t, low, grad_low, dq_t
):
    tokens, lanes = q.shape
    chunk = low.shape[0]
    keys_t[:, :tokens] = kv[0].T
    keys_t[:, tokens:] = kv_other[0].T
    q_all = q[...]
    d_all = d_out[...]
    q_t = q_all.T
    d_t = d_all.T
    row = lax.broadcasted_iota(jnp.int32, q_t.shape, 0) // HEAD_DIM
    lane = lax.broadcasted_iota(jnp.int32, q_all.shape, 1) // HEAD_DIM
    product = d_t.astype(F32) * out_t[...].astype(F32)
    q_rows, d_rows = [], []
    for head in range(GROUP):
        q_rows.append(jnp.where(lane == head, q_all, jnp.zeros_like(q_all)))
        d_rows.append(jnp.where(lane == head, d_all, jnp.zeros_like(d_all)))
    q_stack = jnp.concatenate(q_rows, axis=0)
    d_stack = jnp.concatenate(d_rows, axis=0)
    for index in range(2 * tokens // chunk):
        source = kv if index * chunk < tokens else kv_other
        at = index * chunk % tokens
        for head in range(GROUP):
            rows = slice(head * HEAD_DIM, (head + 1) * HEAD_DIM)
            columns = slice(head * tokens, (head + 1) * tokens)
            center = jnp.sum(product[rows, :], axis=0, keepdims=True)
            offset = log_total[0, head : head + 1, :] * LOG2E
            q_head = jnp.where(row == head, q_t, jnp.zeros_like(q_t))
            d_head = jnp.where(row == head, d_t, jnp.zeros_like(d_t))
            scores = dot(source[0, at : at + chunk, :], q_head)
            probs = jnp.exp2(scores * LOG2E - offset)
            low[:, columns] = probs.astype(BF16)
            d_probs = dot(source[1, at : at + chunk, :], d_head)
            d_scores = (probs * (d_probs - center)).astype(BF16)
            grad_low[:, columns] = d_scores
            update = dot(keys_t[rows, index * chunk : (index + 1) * chunk], d_scores)
            if index == 0:
                dq_t[rows, :] = update
            else:
                dq_t[rows, :] += update
        d_keys = dot(grad_low[...], q_stack)
        d_values = dot(low[...], d_stack)
        if index * chunk < tokens:
            d_own[0, at : at + chunk, :] = d_keys
            d_own[1, at : at + chunk, :] = d_values
        else:
            d_other[0, at : at + chunk, :] = d_keys.astype(BF16)
            d_other[1, at : at + chunk, :] = d_values.astype(BF16)
    dq[...] = (dq_t[...] * SCALE).T.astype(BF16)


def attend_back(q, kv, kv_other, d_out, out_t, log_total, group):
    tokens, width = q.shape
    lanes = GROUP * HEAD_DIM
    chunk = min(256, tokens)
    pair = pl.BlockSpec((2, tokens, lanes), lambda g: (0, 0, group))
    flat = pl.BlockSpec((tokens, lanes), lambda g: (0, group))
    pair_out = whole((2, tokens, lanes))
    return pl.pallas_call(
        attend_back_kernel,
        grid=(1,),
        in_specs=[
            flat,
            pair,
            pair,
            flat,
            pl.BlockSpec((lanes, tokens), lambda g: (group, 0)),
            pl.BlockSpec((1, 8, tokens), lambda g: (group, 0, 0)),
        ],
        out_specs=[whole((tokens, lanes)), pair_out, pair_out],
        out_shape=[
            shape_of((tokens, lanes), BF16),
            shape_of((2, tokens, lanes), F32),
            shape_of((2, tokens, lanes), BF16),
        ],
        scratch_shapes=[
            pltpu.VMEM((lanes, 2 * tokens), BF16),
            pltpu.VMEM((chunk, GROUP * tokens), BF16),
            pltpu.VMEM((chunk, GROUP * tokens), BF16),
            pltpu.VMEM((lanes, tokens), F32),
        ],
        compiler_params=params(24),
        cost_estimate=LIGHT,
        name="attend_back",
    )(q, kv, kv_other, d_out, out_t, log_total)


def gelu_both(up):
    factor = 0.7978845608028654
    square = up * up
    angle = up * (factor + factor * 0.044715 * square)
    tanh = jnp.tanh(angle)
    half = 0.5 * (1.0 + tanh)
    slope = half + 0.5 * up * (1.0 - tanh * tanh) * (factor + 3.0 * factor * 0.044715 * square)
    return up * half, slope


def store_rows(value, targets, held, core):
    if len(targets) == 1:
        targets[0][0] = value.astype(BF16)
        return
    blocks, rows = held.shape[0] * 2, held.shape[2]
    for block in range(blocks):
        held[block // 2, block % 2] = value[block * rows : (block + 1) * rows, :].astype(BF16)
    targets[0][0] = held[:, core]
    targets[1][0] = held[:, 1 - core]


def store_columns(value, targets, core):
    value = value.astype(BF16)
    if len(targets) == 1:
        targets[0][0] = value
        return
    parts, unused, rows, columns = targets[0].shape
    first, second = value[:, :columns], value[:, columns:]
    stay = jnp.where(core == 0, first, second)
    leave = jnp.where(core == 0, second, first)
    for index in range(parts):
        targets[0][index, 0] = stay[index * rows : (index + 1) * rows, :]
        targets[1][index, 0] = leave[index * rows : (index + 1) * rows, :]


def feed_kernel(
    core_ref,
    attended,
    attended_t,
    one,
    two,
    cot_one,
    cot_two,
    mod,
    gain_ref,
    w_out,
    w_up,
    w_down,
    out_one,
    out_two,
    d_attended,
    d_middle_out,
    sums,
    *rest,
):
    projected, middle, norm, norm_t, d_down, d_down_t, down, d_norm, held = rest[-9:]
    grads = rest[:-9]
    count = len(grads) // 2
    up_grad, down_grad = grads[:count], grads[count:]
    step = pl.program_id(0)
    last = pl.num_programs(0) - 1
    core = core_ref[0]
    part = one.shape[0]
    gate_one, shift, scale, gate_two = (mod[index : index + 1, :] for index in (2, 3, 4, 5))
    gain = gain_ref[...].astype(F32)

    @pl.when(step == 0)
    def begin():
        projected[...] = dot(attended[...], w_out[...])
        for index, (ref, cot) in enumerate(((one, cot_one), (two, cot_two))):
            rows = slice(index * part, (index + 1) * part)
            middle[rows, :] = ref[...].astype(F32) + gate_one * projected[rows, :]
            d_down[rows, :] = (cot[...].astype(F32) * gate_two).astype(BF16)
        xhat, unused = normalize(middle[...])
        norm[...] = (xhat * gain * (1.0 + scale) + shift).astype(BF16)
        norm_t[...] = norm[...].T
        d_down_t[...] = d_down[...].T

    @pl.when(step < last)
    def layer():
        up = dot(norm[...], w_up[...])
        activated, slope = gelu_both(up)
        activated = activated.astype(BF16)
        d_up = (ndot(d_down[...], w_down[...]) * slope).astype(BF16)
        down_step = dot(activated, w_down[...])
        norm_step = ndot(d_up, w_up[...])

        @pl.when(step == 0)
        def assign():
            down[...] = down_step
            d_norm[...] = norm_step

        @pl.when(step > 0)
        def add():
            down[...] += down_step
            d_norm[...] += norm_step

        store_rows(dot(norm_t[...], d_up), up_grad, held, core)
        store_columns(dot(d_down_t[...], activated), down_grad, core)

    @pl.when(step == last)
    def end():
        xhat, inverse_std = normalize(middle[...])
        grad = d_norm[...]
        back = normalize_back(grad * (gain * (1.0 + scale)), xhat, inverse_std)
        gate_sum = jnp.zeros_like(gate_two)
        for index, (cot, out) in enumerate(((cot_one, out_one), (cot_two, out_two))):
            rows = slice(index * part, (index + 1) * part)
            d_result = cot[...].astype(F32)
            out[...] = (middle[rows, :] + gate_two * down[rows, :]).astype(BF16)
            gate_sum += jnp.sum(d_result * down[rows, :], axis=0, keepdims=True)
            d_middle_out[rows, :] = d_result + back[rows, :]
        d_middle = d_middle_out[...]
        d_projected = (d_middle * gate_one).astype(BF16)
        both = jnp.sum(grad * xhat, axis=0, keepdims=True)
        sums[0:1, :] = jnp.sum(d_middle * projected[...], axis=0, keepdims=True)
        sums[1:2, :] = jnp.sum(grad, axis=0, keepdims=True)
        sums[2:3, :] = both * gain
        sums[3:4, :] = gate_sum
        sums[4:5, :] = both * (1.0 + scale)
        sums[5:8, :] = jnp.zeros((3, sums.shape[1]), F32)
        d_attended[...] = ndot(d_projected, w_out[...]).astype(BF16)
        store_rows(dot(attended_t[...], d_projected), up_grad, held, core)


def grad_rows(steps, width, wide, extra, split):
    half, rows = wide // 2, width // wide + extra
    if not split:
        return [pl.BlockSpec((1, width, width), lambda i: (i, 0, 0))], [shape_of((steps, width, width), BF16)]
    spec = pl.BlockSpec((1, half, rows, width), lambda i: (i, 0, 0, 0))
    return [spec] * 2, [shape_of((steps, half, rows, width), BF16)] * 2


def grad_columns(steps, width, narrow, split):
    at = lambda i: jnp.minimum(i, steps - 1)
    if not split:
        return [pl.BlockSpec((1, width, width), lambda i: (at(i), 0, 0))], [shape_of((steps, width, width), BF16)]
    spec = pl.BlockSpec((narrow, 1, width // narrow, width // 2), lambda i: (0, at(i), 0, 0))
    return [spec] * 2, [shape_of((narrow, steps, width // narrow, width // 2), BF16)] * 2


def feed(core, attended, attended_t, one, two, cot_one, cot_two, mod, gain, w_out, w_up, w_down, wide, narrow, split):
    tokens, width = attended.shape
    part = tokens // 2
    hidden = w_up.shape[1]
    steps = hidden // width
    half, rows = (wide // 2, width // wide) if split else (1, 16)
    up_specs, up_shapes = grad_rows(steps + 1, width, wide, 0, split)
    down_specs, down_shapes = grad_columns(steps, width, narrow, split)
    small = whole((part, width))
    full = whole((tokens, width))
    return pl.pallas_call(
        feed_kernel,
        grid=(steps + 1,),
        in_specs=[
            pl.BlockSpec(memory_space=pltpu.SMEM),
            full,
            whole((width, tokens)),
            small,
            small,
            small,
            small,
            whole(mod.shape),
            whole((1, width)),
            whole((width, width)),
            pl.BlockSpec((width, width), lambda i: (0, jnp.minimum(i, steps - 1))),
            pl.BlockSpec((width, width), lambda i: (jnp.minimum(i, steps - 1), 0)),
        ],
        out_specs=[small, small, full, full, whole((8, width))]
        + up_specs
        + down_specs,
        out_shape=[
            shape_of((part, width), BF16),
            shape_of((part, width), BF16),
            shape_of((tokens, width), BF16),
            shape_of((tokens, width), F32),
            shape_of((8, width), F32),
        ]
        + up_shapes
        + down_shapes,
        scratch_shapes=[
            pltpu.VMEM((tokens, width), F32),
            pltpu.VMEM((tokens, width), F32),
            pltpu.VMEM((tokens, width), BF16),
            pltpu.VMEM((width, tokens), BF16),
            pltpu.VMEM((tokens, width), BF16),
            pltpu.VMEM((width, tokens), BF16),
            pltpu.VMEM((tokens, width), F32),
            pltpu.VMEM((tokens, width), F32),
            pltpu.VMEM((half, 2, rows, width), BF16),
        ],
        compiler_params=params(44),
        cost_estimate=LIGHT,
        name="feed",
    )(core, attended, attended_t, one, two, cot_one, cot_two, mod, gain, w_out, w_up, w_down)


def project_back_kernel(groups, core_ref, *refs):
    dq, d_own, received = refs[:groups], refs[groups : 2 * groups], refs[2 * groups : 3 * groups]
    refs_in = refs[3 * groups : 3 * groups + 12]
    norm_t, one, two, mod, gain_ref, weight, cosine, sine, d_middle, early, ada, about = refs_in
    out_one, out_two, share = refs[3 * groups + 12 : 3 * groups + 15]
    grads = refs[3 * groups + 15 : -3]
    d_part, d_norm, held = refs[-3:]
    step = pl.program_id(0)
    part = one.shape[0]
    lanes = dq[0].shape[1]

    @pl.when(step == 0)
    def query():
        value = jnp.concatenate([ref[...] for ref in dq], axis=1).astype(F32)
        d_part[...] = rotate(value, cosine[...], -sine[...]).astype(BF16)

    @pl.when(step > 0)
    def other():
        for group in range(groups):
            total = d_own[group][0] + received[group][0].astype(F32)
            d_part[:, group * lanes : (group + 1) * lanes] = total.astype(BF16)

    @pl.when(step == 1)
    def key():
        d_part[...] = rotate(d_part[...].astype(F32), cosine[...], -sine[...]).astype(BF16)

    norm_step = ndot(d_part[...], weight[...])

    @pl.when(step == 0)
    def assign():
        d_norm[...] = norm_step

    @pl.when(step > 0)
    def add():
        d_norm[...] += norm_step

    @pl.when(step == 2)
    def end():
        gain = gain_ref[...].astype(F32)
        scale = mod[1:2, :]
        plain = jnp.zeros_like(gain)
        both = jnp.zeros_like(gain)
        for index, (ref, out) in enumerate(((one, out_one), (two, out_two))):
            rows = slice(index * part, (index + 1) * part)
            xhat, inverse_std = normalize(ref[...].astype(F32))
            grad = d_norm[rows, :]
            back = normalize_back(grad * (gain * (1.0 + scale)), xhat, inverse_std)
            out[...] = (d_middle[rows, :] + back).astype(BF16)
            plain += jnp.sum(grad, axis=0, keepdims=True)
            both += jnp.sum(grad * xhat, axis=0, keepdims=True)
        share[0:1, :] = plain
        share[1:2, :] = both * gain
        share[2:7, :] = early[0:5, :]
        share[7:8, :] = both * (1.0 + scale)

    if len(grads) == 1:
        store_rows(dot(norm_t[...], d_part[...]), grads, held, core_ref[0])
        return
    gradient = dot(norm_t[...], d_part[...])
    half, rows = held.shape[0], held.shape[2] - EXTRA
    width = gain_ref.shape[1]
    blocks = 2 * half
    for block in range(blocks):
        held[block // 2, block % 2, :rows, :] = gradient[block * rows : (block + 1) * rows, :].astype(BF16)
    place = lax.broadcasted_iota(jnp.int32, (EXTRA, width), 0)

    @pl.when(step == 0)
    def nothing():
        for block in range(blocks):
            held[block // 2, block % 2, rows:, :] = jnp.zeros((EXTRA, width), BF16)

    @pl.when(step == 1)
    def known():
        told = jnp.concatenate([about[...], jnp.zeros((1, width - about.shape[1]), F32)], axis=1)
        told = jnp.where(place == core_ref[1], told, 0.0).astype(BF16)
        for block in range(blocks):
            held[block // 2, block % 2, rows:, :] = told

    @pl.when(step == 2)
    def summed():
        flat = jnp.concatenate([share[index : index + 1, :] for index in range(6)], axis=1)
        depth = ada.shape[0]
        d_condition = jnp.sum(ada[...].astype(F32) * flat, axis=1, keepdims=True)
        embedded = about[:, :depth]
        gate = 1.0 / (1.0 + jnp.exp(-embedded))
        square = jnp.where(
            lax.broadcasted_iota(jnp.int32, (depth, depth), 0)
            == lax.broadcasted_iota(jnp.int32, (depth, depth), 1),
            d_condition,
            0.0,
        )
        d_embedded = jnp.sum(square, axis=0, keepdims=True) * gate * (1.0 + embedded * (1.0 - gate))
        count = flat.shape[1] // blocks
        rest = width - count - depth
        for block in range(blocks):
            row = jnp.concatenate(
                [flat[:, block * count : (block + 1) * count], d_embedded, jnp.zeros((1, rest), F32)], axis=1
            )
            gains = jnp.concatenate(
                [
                    share[7:8, block * rows : (block + 1) * rows],
                    share[6:7, block * rows : (block + 1) * rows],
                    jnp.zeros((1, width - 2 * rows), F32),
                ],
                axis=1,
            )
            value = jnp.where(place == core_ref[1], row, 0.0) + jnp.where(place == EXTRA - 1, gains, 0.0)
            held[block // 2, block % 2, rows:, :] = value.astype(BF16)

    core = core_ref[0]
    grads[0][0] = held[:, core]
    grads[1][0] = held[:, 1 - core]


def project_back(
    core, dq, d_own, received, norm_t, one, two, mod, gain, weight, cosine, sine, d_middle, early, ada, about, wide, split
):
    groups = len(dq)
    tokens, lanes = dq[0].shape
    width = groups * lanes
    part = tokens // 2
    half, rows = (wide // 2, width // wide + EXTRA) if split else (1, 16)
    small = whole((part, width))
    full = whole((tokens, width))
    later = pl.BlockSpec((1, tokens, lanes), lambda i: (jnp.maximum(i - 1, 0), 0, 0))
    specs, shapes = grad_rows(3, width, wide, EXTRA, split)
    return pl.pallas_call(
        functools.partial(project_back_kernel, groups),
        grid=(3,),
        in_specs=[pl.BlockSpec(memory_space=pltpu.SMEM)]
        + [whole((tokens, lanes))] * groups
        + [later] * (2 * groups)
        + [
            whole((width, tokens)),
            small,
            small,
            whole(mod.shape),
            whole((1, width)),
            pl.BlockSpec((width, width), lambda i: (0, i)),
            whole(cosine.shape),
            whole(sine.shape),
            full,
            whole(early.shape),
            whole(ada.shape),
            whole(about.shape),
        ],
        out_specs=[small, small, whole((8, width))] + specs,
        out_shape=[
            shape_of((part, width), BF16),
            shape_of((part, width), BF16),
            shape_of((8, width), F32),
        ]
        + shapes,
        scratch_shapes=[
            pltpu.VMEM((tokens, width), BF16),
            pltpu.VMEM((tokens, width), F32),
            pltpu.VMEM((half, 2, rows, width), BF16),
        ],
        compiler_params=params(60),
        cost_estimate=LIGHT,
        name="project_back",
    )(core, *dq, *d_own, *received, norm_t, one, two, mod, gain, weight, cosine, sine, d_middle, early, ada, about)


def stage_kernel(cuts, words, *refs):
    count = len(cuts)
    for item, (first, last, place) in enumerate(cuts):
        keep, received = refs[2 * item], refs[2 * item + 1]
        stay, leave = refs[2 * count + 2 * item], refs[2 * count + 2 * item + 1]
        mine = words[item]
        for index in range(stay.shape[1]):
            base = (index >> place << (place + 1)) | (index & ((1 << place) - 1))
            for target, bit in ((stay, mine), (leave, 1 - mine)):
                at = base + (bit << place)
                target[0, index] = keep[0, at, first:last, :] + received[0, at, first:last, :]


def stage(name, words, items):
    specs, outs, shapes, operands = [], [], [], []
    for keep, received, first, last, place in items:
        lead, blocks, rows, columns = keep.shape
        spec = pl.BlockSpec((1, blocks, rows, columns), lambda i: (i, 0, 0, 0))
        specs += [spec, spec]
        operands += [keep, received]
        outs += [pl.BlockSpec((1, blocks // 2, last - first, columns), lambda i: (i, 0, 0, 0))] * 2
        shapes += [shape_of((lead, blocks // 2, last - first, columns), BF16)] * 2
    return pl.pallas_call(
        functools.partial(stage_kernel, [item[2:] for item in items]),
        grid=(items[0][0].shape[0],),
        in_specs=[pl.BlockSpec(memory_space=pltpu.SMEM)] + specs,
        out_specs=outs,
        out_shape=shapes,
        compiler_params=params(10),
        cost_estimate=LIGHT if name.endswith("core") and not name.startswith("qkv") else HEAVY,
        name=name,
    )(jnp.stack(words), *operands)


def call(kernel, name, shapes, operands, scratch=()):
    vmem = pl.BlockSpec(memory_space=pltpu.VMEM)
    return pl.pallas_call(
        kernel,
        in_specs=[pl.BlockSpec(memory_space=pltpu.SMEM)] + [vmem] * (len(operands) - 1),
        out_specs=[vmem] * len(shapes),
        out_shape=shapes,
        scratch_shapes=list(scratch),
        compiler_params=params(10),
        cost_estimate=HEAVY,
        name=name,
    )(*operands)


def near_kernel(extra, words, keep, received, stay, leave, *rest):
    n = words[1]
    last = 3
    for target, index in ((stay, n), (leave, n ^ 1)):
        for slot, at in ((0, index), (1, last - index)):
            total = keep[at, 0].astype(F32) + received[at, 0].astype(F32)
            target[slot] = total.astype(target.dtype)
    if extra:
        rest[0][...] = keep[last + 1, 0] + received[last + 1, 0]


def near(name, words, keep, received):
    lead, unused, rows, columns = keep.shape
    shapes = [shape_of((2, rows, columns), F32), shape_of((2, rows, columns), BF16)]
    extra = lead > 4
    if extra:
        shapes.append(shape_of((rows, columns), BF16))
    return call(functools.partial(near_kernel, extra), name, shapes, (words, keep, received))


def far_kernel(words, keep, received, stay, leave):
    stay[...] = keep[0] + received[0].astype(F32)
    leave[...] = (keep[1] + received[1].astype(F32)).astype(BF16)


def far(name, words, keep, received):
    shape = keep.shape[1:]
    return call(far_kernel, name, [shape_of(shape, F32), shape_of(shape, BF16)], (words, keep, received))


def end_kernel(turn, words, keep, received, out):
    total = keep[...] + received[...].astype(F32)
    out[...] = total.T if turn else total


def end(name, turn, words, keep, received):
    rows, columns = keep.shape
    shape = (columns, rows) if turn else (rows, columns)
    return call(functools.partial(end_kernel, turn), name, [shape_of(shape, F32)], (words, keep, received))[0]


def mix_kernel(words, keep_a, got_a, keep_b, got_b, rest, own, near, middle, far, sums, blocks):
    n = words[1]
    lead, unused, first_rows, width = keep_a.shape
    rows = rest.shape[0]
    for index in range(lead):
        columns = slice(index * width, (index + 1) * width)
        sums[:first_rows, columns] = keep_a[index, 0].astype(F32) + got_a[index, 0].astype(F32)
        second = keep_b[index, 0].astype(F32) + got_b[index, 0].astype(F32)
        sums[first_rows:, columns] = second[: rows - first_rows, :]
        if index > 0:
            at = rows + (lead - 1 - index) * EXTRA
            extra = slice(at, at + EXTRA)
            for part in range(blocks.shape[0]):
                blocks[part, extra, :] = second[rows - first_rows :, :]
    parts = blocks.shape[0]
    first = sums.shape[1] // parts
    second = rest.shape[1] // parts
    for part in range(parts):
        blocks[part, :rows, :first] = sums[:, part * first : (part + 1) * first]
        blocks[part, :rows, first:] = rest[:, part * second : (part + 1) * second].astype(F32)
    for target, mask in ((own, 0), (near, 1), (middle, 2), (far, 3)):
        target[...] = blocks[n ^ mask].astype(target.dtype)


def mix(words, keep_a, got_a, keep_b, got_b, rest, narrow):
    lead, unused, first_rows, width = keep_a.shape
    rows, rest_columns = rest.shape
    columns = (lead * width + rest_columns) // narrow
    shape = (rows + 2 * EXTRA, columns)
    return call(
        mix_kernel,
        "qkv_line",
        [shape_of(shape, F32)] + [shape_of(shape, BF16)] * 3,
        (words, keep_a, got_a, keep_b, got_b, rest),
        [pltpu.VMEM((rows, lead * width), F32), pltpu.VMEM((narrow,) + shape, F32)],
    )


def last_kernel(words, own, near, middle, far, qkv, out, ada, table, gain_one, gain_two, mods, about, wide):
    w, n = words[0], words[1]
    rows, first = qkv.shape
    gains = jnp.zeros((1, own.shape[1]), F32)
    total = jnp.zeros((rows, own.shape[1]), F32)
    slots = mods.shape[0] // 4
    for index, ref in enumerate((own, near, middle, far)):
        value = ref[...].astype(F32)
        total += value[:rows, :]
        mods[index * slots : (index + 1) * slots, :] = value[rows : rows + slots, :]
        about[index * slots : (index + 1) * slots, :] = value[rows + EXTRA : rows + EXTRA + slots, :]
        gains += value[rows + EXTRA - 1 : rows + EXTRA, :]
    qkv[...] = total[:, :first]
    out[...] = total[:, first:]
    gain_one[...] = gains[:, :rows]
    gain_two[...] = gains[:, rows : 2 * rows]
    count = ada.shape[1]
    depth = wide.shape[0]
    part = ada.shape[0]
    embedded = about[:, :depth]
    condition = (embedded / (1.0 + jnp.exp(-embedded))).astype(BF16)
    used = (about[:, 2 * depth : 2 * depth + 1] > 0.5).astype(F32)
    condition = (condition.astype(F32) * used).astype(BF16)
    turned = (((0,), (0,)), ((), ()))
    wide[...] = lax.dot_general(
        condition, mods[:, :count].astype(BF16), turned, preferred_element_type=F32
    )
    ada[...] = wide[pl.ds(n * part, part), :]
    time = about[:, depth : depth + 1] * 32.0 + about[:, depth + 1 : depth + 2]
    times = table.shape[0]
    lane = lax.broadcasted_iota(jnp.int32, (mods.shape[0], times), 1) + w * times
    onehot = jnp.where(time.astype(jnp.int32) == lane, used, 0.0).astype(BF16)
    grad = lax.dot_general(
        onehot, mods[:, count : count + depth].astype(BF16), turned, preferred_element_type=F32
    )
    value = grad[:, :part]
    for index in range(1, depth // part):
        value = jnp.where(n == index, grad[:, index * part : (index + 1) * part], value)
    table[...] = value


def last(words, own, got, qkv_shape, out_shape, ada_shape, table_shape, depth, wide):
    rows = qkv_shape[0]
    return call(
        last_kernel,
        "qkv_end",
        [shape_of(qkv_shape, F32), shape_of(out_shape, F32), shape_of(ada_shape, F32), shape_of(table_shape, F32)]
        + [shape_of((1, rows), F32)] * 2,
        (words, own, *got),
        [
            pltpu.VMEM((4 * wide, own.shape[1]), F32),
            pltpu.VMEM((4 * wide, own.shape[1]), F32),
            pltpu.VMEM((depth, ada_shape[1]), F32),
        ],
    )


def make(wide, narrow):
    wide_bits = wide.bit_length() - 1

    def first_message(w, n):
        p, c = w // 2, w % 2
        return 2 * p + n // 2, 2 * c + n % 2

    def second_message(w, n):
        p, c = w // 2, w % 2
        return 2 * p + n // 2, 2 * c + 1 - n % 2

    message_one = pairs(wide, narrow, first_message)
    message_two = pairs(wide, narrow, second_message)
    flip = [pairs(wide, narrow, lambda w, n, b=b: (w ^ (1 << b), n)) for b in range(wide_bits)]
    line = [pairs(wide, narrow, lambda w, n, m=m: (w, n ^ m)) for m in range(1, narrow)]
    split = wide == 8

    def on_device(
        hidden_in,
        positions,
        time_index,
        cond_table,
        ada_weight,
        norm1_gain,
        qkv_weight,
        out_weight,
        norm2_gain,
        up_weight,
        down_weight,
        cotangent,
    ):
        w = lax.axis_index("wide")
        n = lax.axis_index("narrow")
        core = w % 2
        core_word = jnp.stack([core, w]).astype(jnp.int32)
        words = jnp.stack([w, n]).astype(jnp.int32)
        width = hidden_in.shape[2]
        odd = n % 2

        def take(array, index):
            return lax.dynamic_index_in_dim(array, index, axis=0, keepdims=False)

        def spread(array):
            one = lax.ppermute(take(array, odd), AXES, message_one)
            two = lax.ppermute(take(array, 1 - odd), AXES, message_two)
            return one, two

        def permute(array, table):
            return lax.ppermute(array, AXES, table)

        def across(sends):
            return [permute(send, line[index]) for index, send in enumerate(sends)]

        def reduce_blocks(current):
            for bit in range(wide_bits):
                mine = (w >> bit) & 1
                current = current.reshape((-1, 2) + current.shape[1:])
                send = lax.dynamic_index_in_dim(current, 1 - mine, axis=1, keepdims=False)
                keep = lax.dynamic_index_in_dim(current, mine, axis=1, keepdims=False)
                received = permute(send, flip[bit])
                current = (keep.astype(F32) + received.astype(F32)).astype(BF16)
            current = current[0]
            total = take(current, n).astype(F32)
            for mask in range(1, narrow):
                total += permute(take(current, n ^ mask), line[mask - 1]).astype(F32)
            return total

        place_one, place_two = spread(positions)
        hidden_one, hidden_two = spread(hidden_in)
        other_time = permute(time_index, flip[0])
        row_time = jnp.where(n // 2 == core, time_index[n % 2], other_time[n % 2])
        embedded = lax.dynamic_slice_in_dim(cond_table, row_time, 1, axis=0).astype(F32)
        condition = (embedded * jax.nn.sigmoid(embedded)).astype(BF16)
        modulation = dot(condition, ada_weight).reshape(6, width)
        mod = jnp.concatenate([modulation, jnp.zeros((2, width), F32)])
        gain_one = norm1_gain.reshape(1, width)
        gain_two = norm2_gain.reshape(1, width)
        depth = cond_table.shape[1]
        pair = jnp.stack([row_time // 32, row_time % 32]).astype(F32).reshape(1, 2)
        about = jnp.concatenate(
            [embedded, pair, jnp.zeros((1, depth - 2), F32), jnp.ones((1, depth), F32)], axis=1
        )

        place = jnp.concatenate([place_one, place_two]).astype(F32)
        lane = jnp.arange(128, dtype=jnp.int32)
        frequency = 10000.0 ** (-(lane % HALF).astype(F32) / HALF)
        angles = place[:, None] * frequency
        cosine = jnp.cos(angles)
        sine = jnp.sin(angles) * jnp.where(lane % HEAD_DIM < HALF, -1.0, 1.0)

        wait = lax.optimization_barrier
        hidden_one, hidden_two, cotangent = wait((hidden_one, hidden_two, cotangent))
        cot_one, cot_two = spread(cotangent)
        q, kv, norm_t = project(hidden_one, hidden_two, mod, gain_one, qkv_weight, cosine, sine)
        kv_other = permute(kv, flip[0])
        attended, attended_t, log_total = attend(q, kv, kv_other)
        out_one, out_two, d_attended, d_middle, sums_two, *grads = feed(
            core_word,
            attended,
            attended_t,
            hidden_one,
            hidden_two,
            cot_one,
            cot_two,
            mod,
            gain_two,
            out_weight,
            up_weight,
            down_weight,
            wide,
            narrow,
            split,
        )
        grads_feed = grads
        out_one = permute(out_one, inverse(message_one))
        out_two = permute(out_two, inverse(message_two))
        dq, d_own, received = [], [], []

        def back_group(group, q):
            first, second, third = attend_back(q, kv, kv_other, d_attended, attended_t, log_total, group)
            dq.append(first)
            d_own.append(second)
            received.append(permute(third, flip[0]))

        rows = width // wide
        if split:
            bits = [((w >> bit) & 1).astype(jnp.int32) for bit in range(wide_bits)]
            up_keep, up_send, down_keep, down_send = grads
            down_got = permute(down_send, flip[0])
            up_got = permute(up_send, flip[0])
            back_group(0, q)
            d_own[0], down_got = wait((d_own[0], down_got))
            down_keep, down_send = stage("down_core", [bits[2]], [(down_keep, down_got, 0, width // narrow, 1)])
            down_got = permute(down_send, flip[2])
            up_got, down_send = wait((up_got, down_send))
            up_keep, up_send = stage("up_core", [bits[1]], [(up_keep, up_got, 0, rows, 0)])
            up_got = permute(up_send, flip[1])
            q, up_send = wait((q, up_send))
            back_group(1, q)
            q, d_own[1], received[0] = wait((q, d_own[1], received[0]))
            back_group(2, q)
            dq[0], dq[2], received[1] = wait((dq[0], dq[2], received[1]))
        else:
            for group in range(width // (GROUP * HEAD_DIM)):
                back_group(group, q)

        grad_one, grad_two, share, *grads = project_back(
            core_word,
            dq,
            d_own,
            received,
            norm_t,
            hidden_one,
            hidden_two,
            mod,
            gain_one,
            qkv_weight,
            cosine,
            sine,
            d_middle,
            sums_two,
            ada_weight,
            about,
            wide,
            split,
        )

        def join(one, two):
            return jnp.stack([jnp.where(odd == 0, one, two), jnp.where(odd == 0, two, one)])

        grad_first = grad_one
        grad_one, grad_two, out_one, out_two = wait((grad_one, grad_two, out_one, out_two))
        grad_one = permute(grad_one, inverse(message_one))
        grad_two = permute(grad_two, inverse(message_two))
        row_count = depth // narrow
        column_count = 6 * width // wide
        time_count = cond_table.shape[0] // wide
        if split:
            qkv_keep, qkv_send = grads
            qkv_got = permute(qkv_send, flip[0])
            down_got, up_got, grad_first = wait((down_got, up_got, grad_first))
            down_keep, down_send = stage("down_plane", [bits[1]], [(down_keep, down_got, 0, width // narrow, 0)])
            down_got = permute(down_send, flip[1])
            up_got, up_keep, down_send = wait((up_got, up_keep, down_send))
            up_keep, up_send = stage("up_plane", [bits[2]], [(up_keep, up_got, 0, rows, 0)])
            up_got = permute(up_send, flip[2])
            qkv_got, up_send = wait((qkv_got, up_send))
            middle = rows // 2
            a_keep, a_send, b_keep, b_send = stage(
                "qkv_core",
                [bits[1], bits[2]],
                [(qkv_keep, qkv_got, 0, middle, 0), (qkv_keep, qkv_got, middle, rows + EXTRA, 1)],
            )
            a_got = permute(a_send, flip[1])
            b_send, down_got, a_send = wait((b_send, down_got, a_send))
            b_got = permute(b_send, flip[2])
            down_got, grad_one, grad_two = wait((down_got, grad_one, grad_two))
            hidden_grad = join(grad_one, grad_two)
            down_keep, down_send = near("down_near", words, down_keep, down_got)
            down_got = permute(down_send, line[0])
            up_got, down_send, hidden_grad = wait((up_got, down_send, hidden_grad))
            up_keep, up_send, out_sum = near("up_near", words, up_keep, up_got)
            up_got = permute(up_send, line[0])
            a_got, b_got, up_send = wait((a_got, b_got, up_send))
            a_keep, a_send, b_keep, b_send = stage(
                "qkv_plane",
                [bits[2], bits[1]],
                [(a_keep, a_got, 0, middle, 0), (b_keep, b_got, 0, middle + EXTRA, 0)],
            )
            a_got, b_got = permute(a_send, flip[2]), permute(b_send, flip[1])
            down_got, a_send, b_send = wait((down_got, a_send, b_send))
            down_keep, down_send = far("down_far", words, down_keep, down_got)
            down_got = permute(down_send, line[2])
            up_got, down_send = wait((up_got, down_send))
            up_keep, up_send = far("up_far", words, up_keep, up_got)
            up_got = permute(up_send, line[2])
            a_got, b_got, up_send = wait((a_got, b_got, up_send))
            own, *sends = mix(words, a_keep, a_got, b_keep, b_got, out_sum, narrow)
            got = across(sends)
            down_got, sends = wait((down_got, sends))
            grad_down = end("down_end", True, words, down_keep, down_got)
            up_got, grad_down = wait((up_got, grad_down))
            grad_up = end("up_end", False, words, up_keep, up_got)
            got, grad_up = wait((got, grad_up))
            grad_qkv, grad_out, grad_ada, grad_table, grad_gain_one, grad_gain_two = last(
                words,
                own,
                got,
                (rows, 3 * width // narrow),
                (rows, width // narrow),
                (row_count, column_count),
                (time_count, row_count),
                depth,
                wide,
            )
            gains = grad_gain_two.reshape(rows), grad_gain_one.reshape(rows)
        else:
            up_grad, down_grad = grads_feed
            (qkv_grad,) = grads
            hidden_grad = join(grad_one, grad_two)
            steps = down_grad.shape[0]
            grad_up = reduce_blocks(up_grad[:steps].reshape(narrow, wide, rows, width).transpose(1, 0, 2, 3))
            grad_down = reduce_blocks(
                down_grad.reshape(steps, narrow, width // narrow, wide // steps, -1)
                .transpose(0, 3, 1, 2, 4)
                .reshape(wide, narrow, width // narrow, -1)
            ).T

            def by_rows(grad):
                return reduce_blocks(
                    grad.transpose(1, 0, 2).reshape(wide, rows, narrow, -1).transpose(0, 2, 1, 3)
                )

            grad_out = by_rows(up_grad[steps:])
            grad_qkv = by_rows(qkv_grad)
            told = jnp.concatenate(
                [embedded, jnp.broadcast_to(row_time.astype(F32), (1, width - depth))], axis=1
            )
            share = jnp.concatenate([share, told])[None]
            for table in flip + [line[0], line[2]]:
                share = jnp.concatenate([share, permute(share, table)])
            all_mod = share[:, :6].reshape(-1, 6 * width)
            gains = jnp.sum(share[:, 6:8].reshape(-1, 2, wide, rows), axis=0)
            gains = lax.dynamic_index_in_dim(gains, w, axis=1, keepdims=False)
            my_embedded = lax.dynamic_slice_in_dim(share[:, 8, :depth], n * row_count, row_count, axis=1)
            times = share[:, 8, depth].astype(jnp.int32)
            my_gate = jax.nn.sigmoid(my_embedded)
            my_conditions = (my_embedded * my_gate).astype(BF16).astype(F32)
            my_mod = lax.dynamic_slice_in_dim(all_mod, w * column_count, column_count, axis=1)
            grad_ada = lax.dot_general(
                my_conditions,
                my_mod,
                (((0,), (0,)), ((), ())),
                precision=HIGHEST,
                preferred_element_type=F32,
            )
            my_ada = lax.dynamic_slice_in_dim(ada_weight, n * row_count, row_count, axis=0).astype(F32)
            d_condition = lax.dot_general(
                all_mod,
                my_ada,
                (((1,), (1,)), ((), ())),
                precision=HIGHEST,
                preferred_element_type=F32,
            )
            d_embedded = d_condition * my_gate * (1.0 + my_embedded * (1.0 - my_gate))
            my_times = w * time_count + jnp.arange(time_count, dtype=jnp.int32)
            onehot = (my_times[:, None] == times[None, :]).astype(F32)
            grad_table = jnp.dot(onehot, d_embedded, precision=HIGHEST, preferred_element_type=F32)
        return (
            join(out_one, out_two),
            hidden_grad,
            grad_table,
            grad_ada,
            gains[1],
            grad_qkv,
            grad_out,
            gains[0],
            grad_up,
            grad_down,
        )

    return on_device


def solution(mesh):
    in_specs = (
        P("wide", "narrow", None),
        P("wide", "narrow"),
        P("wide"),
        P(),
        P(),
        P(),
        P(),
        P(),
        P(),
        P(),
        P(),
        P("wide", "narrow", None),
    )
    out_specs = (
        P("wide", "narrow", None),
        P("wide", "narrow", None),
        P("wide", "narrow"),
        P("narrow", "wide"),
        P("wide"),
        P("wide", "narrow"),
        P("wide", "narrow"),
        P("wide"),
        P("wide", "narrow"),
        P("wide", "narrow"),
    )
    return jax.shard_map(
        make(mesh.shape["wide"], mesh.shape["narrow"]),
        mesh=mesh,
        in_specs=in_specs,
        out_specs=out_specs,
        check_vma=False,
    )
```

```python
import functools

import jax
import jax.numpy as jnp
from jax import lax
from jax.experimental import pallas as pl
from jax.experimental.pallas import tpu as pltpu
from jax.sharding import PartitionSpec as P

HEAD_DIM = 64
HALF = HEAD_DIM // 2
GROUP = 4
ONES = 16
LOG2E = 1.4426950408889634
SCALE = HEAD_DIM**-0.5
HIGHEST = lax.Precision.HIGHEST
norm_eps = 1e-05
AXES = ("wide", "narrow")
EXTRA = 32
SMALL = 32
THIRD = 32
F32 = jnp.float32
BF16 = jnp.bfloat16
MIB = 1 << 20


def cost(us):
    return pl.CostEstimate(flops=int(us * 1.15e9), bytes_accessed=int(us * 3.7e6), transcendentals=0)


LIGHT = cost(0.01)
HEAVY = cost(100)


def dot(left, right):
    return jnp.dot(left, right, preferred_element_type=F32)


def ndot(left, right):
    return lax.dot_general(left, right, (((1,), (1,)), ((), ())), preferred_element_type=F32)


def pairs(wide, narrow, target):
    result = []
    for w in range(wide):
        for n in range(narrow):
            w_to, n_to = target(w, n)
            result.append((w * narrow + n, w_to * narrow + n_to))
    return result


def inverse(table):
    return [(target, source) for source, target in table]


def normalize(hidden):
    center = hidden - jnp.mean(hidden, axis=-1, keepdims=True)
    variance = jnp.mean(center * center, axis=-1, keepdims=True)
    inverse_std = lax.rsqrt(variance + norm_eps)
    return center * inverse_std, inverse_std


def normalize_back(grad, xhat, inverse_std):
    mean_grad = jnp.mean(grad, axis=-1, keepdims=True)
    mean_both = jnp.mean(grad * xhat, axis=-1, keepdims=True)
    return (grad - mean_grad - xhat * mean_both) * inverse_std


def rotate(values, cosine, sine):
    width = values.shape[1]
    lane = lax.broadcasted_iota(jnp.int32, values.shape, 1)
    ahead = pltpu.roll(values, width - HALF, 1)
    behind = pltpu.roll(values, HALF, 1)
    swapped = jnp.where(lane % HEAD_DIM < HALF, ahead, behind)
    repeat = width // cosine.shape[1]
    cosine = jnp.concatenate([cosine] * repeat, axis=1)
    sine = jnp.concatenate([sine] * repeat, axis=1)
    return values * cosine + swapped * sine


def whole(shape):
    return pl.BlockSpec(shape, lambda *index: (0,) * len(shape))


def params(mib):
    return pltpu.CompilerParams(vmem_limit_bytes=mib * MIB)


def shape_of(shape, dtype):
    return jax.ShapeDtypeStruct(shape, dtype)


def project_kernel(one, two, mod, gain, weight, cosine, sine, q_out, kv_out, norm_t, norm):
    step = pl.program_id(0)
    part = one.shape[0]

    @pl.when(step == 0)
    def first():
        for index, ref in enumerate((one, two)):
            xhat, unused = normalize(ref[...].astype(F32))
            value = xhat * gain[...].astype(F32) * (1.0 + mod[1:2, :]) + mod[0:1, :]
            norm[index * part : (index + 1) * part, :] = value.astype(BF16)
        norm_t[...] = norm[...].T

    result = dot(norm[...], weight[...])

    @pl.when(step == 0)
    def query():
        q_out[...] = (rotate(result, cosine[...], sine[...]).astype(BF16).astype(F32) * SCALE).astype(BF16)

    @pl.when(step == 1)
    def key():
        kv_out[0] = rotate(result, cosine[...], sine[...]).astype(BF16)

    @pl.when(step == 2)
    def value():
        kv_out[0] = result.astype(BF16)


def project(one, two, mod, gain, weight, cosine, sine):
    part, width = one.shape
    tokens = 2 * part
    return pl.pallas_call(
        project_kernel,
        grid=(3,),
        in_specs=[
            whole((part, width)),
            whole((part, width)),
            whole(mod.shape),
            whole((1, width)),
            pl.BlockSpec((width, width), lambda i: (0, i)),
            whole(cosine.shape),
            whole(sine.shape),
        ],
        out_specs=[
            whole((tokens, width)),
            pl.BlockSpec((1, tokens, width), lambda i: (jnp.maximum(i - 1, 0), 0, 0)),
            whole((width, tokens)),
        ],
        out_shape=[
            shape_of((tokens, width), BF16),
            shape_of((2, tokens, width), BF16),
            shape_of((width, tokens), BF16),
        ],
        scratch_shapes=[pltpu.VMEM((tokens, width), BF16)],
        compiler_params=params(28),
        cost_estimate=LIGHT,
        name="project",
    )(one, two, mod, gain, weight, cosine, sine)


def attend_kernel(q, kv, kv_other, out, out_t, log_total, keys, values_t, scores):
    tokens, lanes = q.shape
    keys[:tokens, :] = kv[0]
    keys[tokens:, :] = kv_other[0]
    step = HEAD_DIM + ONES
    turned = kv[1].T, kv_other[1].T
    for head in range(GROUP):
        lane = slice(head * HEAD_DIM, (head + 1) * HEAD_DIM)
        rows = slice(head * step, head * step + HEAD_DIM)
        values_t[rows, :tokens] = turned[0][lane, :]
        values_t[rows, tokens:] = turned[1][lane, :]
        values_t[head * step + HEAD_DIM : (head + 1) * step, :] = jnp.ones((ONES, 2 * tokens), BF16)
    q_t = q[...].T
    row = lax.broadcasted_iota(jnp.int32, q_t.shape, 0) // HEAD_DIM
    log_total[...] = jnp.zeros_like(log_total)

    def score(head):
        scores[head % 2] = dot(keys[...], jnp.where(row == head, q_t, jnp.zeros_like(q_t)))

    score(0)
    for head in range(GROUP):
        if head + 1 < GROUP:
            score(head + 1)
        score_head = scores[head % 2]
        top = jnp.max(score_head, axis=0, keepdims=True)
        expo = jnp.exp2((score_head - top) * LOG2E).astype(BF16)
        rows = slice(head * HEAD_DIM, (head + 1) * HEAD_DIM)
        result = dot(values_t[head * step : (head + 1) * step, :], expo)
        total = result[HEAD_DIM : HEAD_DIM + 1, :]
        out_t[rows, :] = (result[:HEAD_DIM, :] / total).astype(BF16)
        log_total[0, head : head + 1, :] = top + jnp.log(total)
    out[...] = out_t[...].T


def attend(q, kv, kv_other):
    tokens, width = q.shape
    lanes = GROUP * HEAD_DIM
    groups = width // lanes
    pair = pl.BlockSpec((2, tokens, lanes), lambda g: (0, 0, g))
    flat = pl.BlockSpec((tokens, lanes), lambda g: (0, g))
    return pl.pallas_call(
        attend_kernel,
        grid=(groups,),
        in_specs=[flat, pair, pair],
        out_specs=[
            flat,
            pl.BlockSpec((lanes, tokens), lambda g: (g, 0)),
            pl.BlockSpec((1, 8, tokens), lambda g: (g, 0, 0)),
        ],
        out_shape=[
            shape_of((tokens, width), BF16),
            shape_of((width, tokens), BF16),
            shape_of((groups, 8, tokens), F32),
        ],
        scratch_shapes=[
            pltpu.VMEM((2 * tokens, lanes), BF16),
            pltpu.VMEM((lanes + GROUP * ONES, 2 * tokens), BF16),
            pltpu.VMEM((2, 2 * tokens, tokens), F32),
        ],
        compiler_params=params(28),
        cost_estimate=LIGHT,
        name="attend",
    )(q, kv, kv_other)


def attend_back_kernel(
    q, kv, kv_other, d_out, out_t, log_total, dq, d_own, d_other, keys_t, low, grad_low, dq_t, scores, grads
):
    tokens, lanes = q.shape
    chunk = low.shape[0]
    keys_t[:, :tokens] = kv[0].T
    keys_t[:, tokens:] = kv_other[0].T
    q_all = q[...]
    d_all = d_out[...]
    q_t = q_all.T
    d_t = d_all.T
    row = lax.broadcasted_iota(jnp.int32, q_t.shape, 0) // HEAD_DIM
    lane = lax.broadcasted_iota(jnp.int32, q_all.shape, 1) // HEAD_DIM
    product = d_t.astype(F32) * out_t[...].astype(F32)
    q_rows, d_rows = [], []
    for head in range(GROUP):
        q_rows.append(jnp.where(lane == head, q_all, jnp.zeros_like(q_all)))
        d_rows.append(jnp.where(lane == head, d_all, jnp.zeros_like(d_all)))
    q_stack = jnp.concatenate(q_rows, axis=0)
    d_stack = jnp.concatenate(d_rows, axis=0)
    items = [(index, head) for index in range(2 * tokens // chunk) for head in range(GROUP)]

    def products(item):
        index, head = items[item]
        source = kv if index * chunk < tokens else kv_other
        at = index * chunk % tokens
        q_head = jnp.where(row == head, q_t, jnp.zeros_like(q_t))
        d_head = jnp.where(row == head, d_t, jnp.zeros_like(d_t))
        scores[item % 2] = dot(source[0, at : at + chunk, :], q_head)
        grads[item % 2] = dot(source[1, at : at + chunk, :], d_head)

    products(0)
    for item, (index, head) in enumerate(items):
        if item + 1 < len(items):
            products(item + 1)
        rows = slice(head * HEAD_DIM, (head + 1) * HEAD_DIM)
        columns = slice(head * tokens, (head + 1) * tokens)
        center = jnp.sum(product[rows, :], axis=0, keepdims=True)
        offset = log_total[0, head : head + 1, :] * LOG2E
        probs = jnp.exp2(scores[item % 2] * LOG2E - offset)
        low[:, columns] = probs.astype(BF16)
        d_scores = (probs * (grads[item % 2] - center)).astype(BF16)
        grad_low[:, columns] = d_scores
        update = dot(keys_t[rows, index * chunk : (index + 1) * chunk], d_scores)
        if index == 0:
            dq_t[rows, :] = update
        else:
            dq_t[rows, :] += update
        if head < GROUP - 1:
            continue
        at = index * chunk % tokens
        d_keys = dot(grad_low[...], q_stack)
        d_values = dot(low[...], d_stack)
        if index * chunk < tokens:
            d_own[0, at : at + chunk, :] = d_keys
            d_own[1, at : at + chunk, :] = d_values
        else:
            d_other[0, at : at + chunk, :] = d_keys.astype(BF16)
            d_other[1, at : at + chunk, :] = d_values.astype(BF16)
    dq[...] = (dq_t[...] * SCALE).T.astype(BF16)


def attend_back(q, kv, kv_other, d_out, out_t, log_total, group):
    tokens, width = q.shape
    lanes = GROUP * HEAD_DIM
    chunk = min(256, tokens)
    pair = pl.BlockSpec((2, tokens, lanes), lambda g: (0, 0, group))
    flat = pl.BlockSpec((tokens, lanes), lambda g: (0, group))
    pair_out = whole((2, tokens, lanes))
    return pl.pallas_call(
        attend_back_kernel,
        grid=(1,),
        in_specs=[
            flat,
            pair,
            pair,
            flat,
            pl.BlockSpec((lanes, tokens), lambda g: (group, 0)),
            pl.BlockSpec((1, 8, tokens), lambda g: (group, 0, 0)),
        ],
        out_specs=[whole((tokens, lanes)), pair_out, pair_out],
        out_shape=[
            shape_of((tokens, lanes), BF16),
            shape_of((2, tokens, lanes), F32),
            shape_of((2, tokens, lanes), BF16),
        ],
        scratch_shapes=[
            pltpu.VMEM((lanes, 2 * tokens), BF16),
            pltpu.VMEM((chunk, GROUP * tokens), BF16),
            pltpu.VMEM((chunk, GROUP * tokens), BF16),
            pltpu.VMEM((lanes, tokens), F32),
            pltpu.VMEM((2, chunk, tokens), F32),
            pltpu.VMEM((2, chunk, tokens), F32),
        ],
        compiler_params=params(24),
        cost_estimate=LIGHT,
        name="attend_back",
    )(q, kv, kv_other, d_out, out_t, log_total)


def gelu_both(up):
    factor = 0.7978845608028654
    square = up * up
    angle = up * (factor + factor * 0.044715 * square)
    tanh = jnp.tanh(angle)
    half = 0.5 * (1.0 + tanh)
    slope = half + 0.5 * up * (1.0 - tanh * tanh) * (factor + 3.0 * factor * 0.044715 * square)
    return up * half, slope


def store_rows(value, targets, held, core):
    if len(targets) == 1:
        targets[0][0] = value.astype(BF16)
        return
    blocks, rows = held.shape[0] * 2, held.shape[2]
    for block in range(blocks):
        held[block // 2, block % 2] = value[block * rows : (block + 1) * rows, :].astype(BF16)
    targets[0][0] = held[:, core]
    targets[1][0] = held[:, 1 - core]


def store_columns(value, targets, core):
    value = value.astype(BF16)
    if len(targets) == 1:
        targets[0][0] = value
        return
    parts, unused, rows, columns = targets[0].shape
    columns = columns // 2
    first, second = value[:, :columns], value[:, columns:]
    stay = jnp.where(core == 0, first, second)
    leave = jnp.where(core == 0, second, first)
    for target, kept in zip(targets, (stay, leave)):
        for index in range(2 * parts):
            side = slice((index % 2) * columns, (index % 2 + 1) * columns)
            target[index // 2, 0, :, side] = kept[index * rows : (index + 1) * rows, :]


def feed_kernel(
    core_ref,
    attended,
    attended_t,
    one,
    two,
    cot_one,
    cot_two,
    mod,
    gain_ref,
    w_out,
    w_up,
    w_down,
    out_one,
    out_two,
    d_attended,
    d_middle_out,
    sums,
    out_grad,
    *rest,
):
    projected, middle, norm, norm_t, d_down, d_down_t, down, d_norm, held = rest[-9:]
    grads = rest[:-9]
    count = len(grads) // 2
    up_grad, down_grad = grads[:count], grads[count:]
    step = pl.program_id(0)
    last = pl.num_programs(0) - 1
    core = core_ref[0]
    part = one.shape[0]
    gate_one, shift, scale, gate_two = (mod[index : index + 1, :] for index in (2, 3, 4, 5))
    gain = gain_ref[...].astype(F32)

    @pl.when(step == 0)
    def begin():
        projected[...] = dot(attended[...], w_out[...])
        for index, (ref, cot) in enumerate(((one, cot_one), (two, cot_two))):
            rows = slice(index * part, (index + 1) * part)
            middle[rows, :] = ref[...].astype(F32) + gate_one * projected[rows, :]
            d_down[rows, :] = (cot[...].astype(F32) * gate_two).astype(BF16)
        xhat, unused = normalize(middle[...])
        norm[...] = (xhat * gain * (1.0 + scale) + shift).astype(BF16)
        norm_t[...] = norm[...].T
        d_down_t[...] = d_down[...].T

    @pl.when(step < last)
    def layer():
        up = dot(norm[...], w_up[...])
        activated, slope = gelu_both(up)
        activated = activated.astype(BF16)
        d_up = (ndot(d_down[...], w_down[...]) * slope).astype(BF16)
        down_step = dot(activated, w_down[...])
        norm_step = ndot(d_up, w_up[...])

        @pl.when(step == 0)
        def assign():
            down[...] = down_step
            d_norm[...] = norm_step

        @pl.when(step > 0)
        def add():
            down[...] += down_step
            d_norm[...] += norm_step

        store_rows(dot(norm_t[...], d_up), up_grad, held, core)
        store_columns(dot(d_down_t[...], activated), down_grad, core)

    @pl.when(step == last)
    def end():
        xhat, inverse_std = normalize(middle[...])
        grad = d_norm[...]
        back = normalize_back(grad * (gain * (1.0 + scale)), xhat, inverse_std)
        gate_sum = jnp.zeros_like(gate_two)
        for index, (cot, out) in enumerate(((cot_one, out_one), (cot_two, out_two))):
            rows = slice(index * part, (index + 1) * part)
            d_result = cot[...].astype(F32)
            out[...] = (middle[rows, :] + gate_two * down[rows, :]).astype(BF16)
            gate_sum += jnp.sum(d_result * down[rows, :], axis=0, keepdims=True)
            d_middle_out[rows, :] = d_result + back[rows, :]
        d_middle = d_middle_out[...]
        d_projected = (d_middle * gate_one).astype(BF16)
        both = jnp.sum(grad * xhat, axis=0, keepdims=True)
        sums[0:1, :] = jnp.sum(d_middle * projected[...], axis=0, keepdims=True)
        sums[1:2, :] = jnp.sum(grad, axis=0, keepdims=True)
        sums[2:3, :] = both * gain
        sums[3:4, :] = gate_sum
        sums[4:5, :] = both * (1.0 + scale)
        sums[5:8, :] = jnp.zeros((3, sums.shape[1]), F32)
        d_attended[...] = ndot(d_projected, w_out[...]).astype(BF16)
        out_grad[...] = dot(attended_t[...], d_projected).astype(BF16)


def grad_rows(steps, width, wide, split):
    at = lambda i: jnp.minimum(i, steps - 1)
    half, rows = wide // 2, width // wide
    if not split:
        return [pl.BlockSpec((1, width, width), lambda i: (at(i), 0, 0))], [shape_of((steps, width, width), BF16)]
    spec = pl.BlockSpec((1, half, rows, width), lambda i: (at(i), 0, 0, 0))
    return [spec] * 2, [shape_of((steps, half, rows, width), BF16)] * 2


def grad_columns(steps, width, narrow, split):
    at = lambda i: jnp.minimum(i, steps - 1)
    if not split:
        return [pl.BlockSpec((1, width, width), lambda i: (at(i), 0, 0))], [shape_of((steps, width, width), BF16)]
    rows = width // narrow // 2
    spec = pl.BlockSpec((narrow, 1, rows, width), lambda i: (0, at(i), 0, 0))
    return [spec] * 2, [shape_of((narrow, steps, rows, width), BF16)] * 2


def feed(core, attended, attended_t, one, two, cot_one, cot_two, mod, gain, w_out, w_up, w_down, wide, narrow, split):
    tokens, width = attended.shape
    part = tokens // 2
    hidden = w_up.shape[1]
    steps = hidden // width
    half, rows = (wide // 2, width // wide) if split else (1, 16)
    up_specs, up_shapes = grad_rows(steps, width, wide, split)
    down_specs, down_shapes = grad_columns(steps, width, narrow, split)
    small = whole((part, width))
    full = whole((tokens, width))
    return pl.pallas_call(
        feed_kernel,
        grid=(steps + 1,),
        in_specs=[
            pl.BlockSpec(memory_space=pltpu.SMEM),
            full,
            whole((width, tokens)),
            small,
            small,
            small,
            small,
            whole(mod.shape),
            whole((1, width)),
            whole((width, width)),
            pl.BlockSpec((width, width), lambda i: (0, jnp.minimum(i, steps - 1))),
            pl.BlockSpec((width, width), lambda i: (jnp.minimum(i, steps - 1), 0)),
        ],
        out_specs=[small, small, full, full, whole((8, width)), whole((width, width))]
        + up_specs
        + down_specs,
        out_shape=[
            shape_of((part, width), BF16),
            shape_of((part, width), BF16),
            shape_of((tokens, width), BF16),
            shape_of((tokens, width), F32),
            shape_of((8, width), F32),
            shape_of((width, width), BF16),
        ]
        + up_shapes
        + down_shapes,
        scratch_shapes=[
            pltpu.VMEM((tokens, width), F32),
            pltpu.VMEM((tokens, width), F32),
            pltpu.VMEM((tokens, width), BF16),
            pltpu.VMEM((width, tokens), BF16),
            pltpu.VMEM((tokens, width), BF16),
            pltpu.VMEM((width, tokens), BF16),
            pltpu.VMEM((tokens, width), F32),
            pltpu.VMEM((tokens, width), F32),
            pltpu.VMEM((half, 2, rows, width), BF16),
        ],
        compiler_params=params(44),
        cost_estimate=LIGHT,
        name="feed",
    )(core, attended, attended_t, one, two, cot_one, cot_two, mod, gain, w_out, w_up, w_down)


def project_back_kernel(groups, parts, core_ref, *refs):
    dq, d_own, received = refs[:groups], refs[groups : 2 * groups], refs[2 * groups : 3 * groups]
    refs_in = refs[3 * groups : 3 * groups + 13]
    norm_t, one, two, mod, gain_ref, weight, cosine, sine, d_middle, early, ada, about, out_grad = refs_in
    out_one, out_two, share = refs[3 * groups + 13 : 3 * groups + 16]
    grads = refs[3 * groups + 16 : -4]
    d_part, d_norm, whole_grad, held = refs[-4:]
    step = pl.program_id(0)
    part = one.shape[0]
    lanes = dq[0].shape[1]

    @pl.when(step == 0)
    def query():
        value = jnp.concatenate([ref[...] for ref in dq], axis=1).astype(F32)
        d_part[...] = rotate(value, cosine[...], -sine[...]).astype(BF16)

    @pl.when(step > 0)
    def other():
        for group in range(groups):
            total = d_own[group][0] + received[group][0].astype(F32)
            d_part[:, group * lanes : (group + 1) * lanes] = total.astype(BF16)

    @pl.when(step == 1)
    def key():
        d_part[...] = rotate(d_part[...].astype(F32), cosine[...], -sine[...]).astype(BF16)

    norm_step = ndot(d_part[...], weight[...])
    gradient = dot(norm_t[...], d_part[...]).astype(BF16)
    width = gradient.shape[1]
    if len(grads) == 1:
        grads[0][0] = gradient
    else:
        for index in range(3):

            @pl.when(step == index)
            def keep_gradient(index=index):
                whole_grad[:, index * width : (index + 1) * width] = gradient

    @pl.when(step == 0)
    def assign():
        d_norm[...] = norm_step

    @pl.when(step > 0)
    def add():
        d_norm[...] += norm_step

    @pl.when(step == 2)
    def end():
        gain = gain_ref[...].astype(F32)
        scale = mod[1:2, :]
        plain = jnp.zeros_like(gain)
        both = jnp.zeros_like(gain)
        for index, (ref, out) in enumerate(((one, out_one), (two, out_two))):
            rows = slice(index * part, (index + 1) * part)
            xhat, inverse_std = normalize(ref[...].astype(F32))
            grad = d_norm[rows, :]
            back = normalize_back(grad * (gain * (1.0 + scale)), xhat, inverse_std)
            out[...] = (d_middle[rows, :] + back).astype(BF16)
            plain += jnp.sum(grad, axis=0, keepdims=True)
            both += jnp.sum(grad * xhat, axis=0, keepdims=True)
        share[0:1, :] = plain
        share[1:2, :] = both * gain
        share[2:7, :] = early[0:5, :]
        share[7:8, :] = both * (1.0 + scale)

        if len(grads) == 1:
            return
        core = core_ref[0]
        half, rows = held.shape[0], held.shape[2]
        blocks = 2 * half
        count = 3 * width // parts
        rest = width // parts
        for index in range(parts):
            for block in range(blocks):
                at = slice(block * rows, (block + 1) * rows)
                held[block // 2, block % 2, :, :count] = whole_grad[at, index * count : (index + 1) * count]
                held[block // 2, block % 2, :, count:] = out_grad[at, index * rest : (index + 1) * rest]
            grads[0][index] = held[:, core]
            grads[1][index] = held[:, 1 - core]
        flat = jnp.concatenate([share[index : index + 1, :] for index in range(6)], axis=1)
        depth = ada.shape[0]
        d_condition = jnp.sum(ada[...].astype(F32) * flat, axis=1, keepdims=True)
        embedded = about[:, :depth]
        gate = 1.0 / (1.0 + jnp.exp(-embedded))
        square = jnp.where(
            lax.broadcasted_iota(jnp.int32, (depth, depth), 0)
            == lax.broadcasted_iota(jnp.int32, (depth, depth), 1),
            d_condition,
            0.0,
        )
        d_embedded = jnp.sum(square, axis=0, keepdims=True) * gate * (1.0 + embedded * (1.0 - gate))
        count = flat.shape[1] // blocks
        place = lax.broadcasted_iota(jnp.int32, (EXTRA, width), 0)
        told_rest = width - about.shape[1] - 2 * rows
        for block in range(blocks):
            row = jnp.concatenate(
                [
                    flat[:, block * count : (block + 1) * count],
                    d_embedded,
                    jnp.zeros((1, width - count - depth), F32),
                ],
                axis=1,
            )
            told = jnp.concatenate(
                [
                    about[...],
                    share[7:8, block * rows : (block + 1) * rows],
                    share[6:7, block * rows : (block + 1) * rows],
                    jnp.zeros((1, told_rest), F32),
                ],
                axis=1,
            )
            mine = core_ref[1]
            value = jnp.where(place == mine, row, 0.0) + jnp.where(place == mine + blocks, told, 0.0)
            held[block // 2, block % 2, :EXTRA, :] = value.astype(BF16)
        grads[0][parts] = held[:, core]
        grads[1][parts] = held[:, 1 - core]


def project_back(
    core, dq, d_own, received, norm_t, one, two, mod, gain, weight, cosine, sine, d_middle, early, ada, about, out_grad, wide, narrow, split
):
    groups = len(dq)
    tokens, lanes = dq[0].shape
    width = groups * lanes
    part = tokens // 2
    small = whole((part, width))
    full = whole((tokens, width))
    later = pl.BlockSpec((1, tokens, lanes), lambda i: (jnp.maximum(i - 1, 0), 0, 0))
    if split:
        half, rows = wide // 2, width // wide
        shape = (narrow + 1, half, rows, width)
        specs, shapes = [whole(shape)] * 2, [shape_of(shape, BF16)] * 2
        scratch = [pltpu.VMEM((width, 3 * width), BF16), pltpu.VMEM((half, 2, rows, width), BF16)]
    else:
        specs, shapes = grad_rows(3, width, wide, split)
        scratch = [pltpu.VMEM((16, 128), BF16)] * 2
    return pl.pallas_call(
        functools.partial(project_back_kernel, groups, narrow),
        grid=(3,),
        in_specs=[pl.BlockSpec(memory_space=pltpu.SMEM)]
        + [whole((tokens, lanes))] * groups
        + [later] * (2 * groups)
        + [
            whole((width, tokens)),
            small,
            small,
            whole(mod.shape),
            whole((1, width)),
            pl.BlockSpec((width, width), lambda i: (0, i)),
            whole(cosine.shape),
            whole(sine.shape),
            full,
            whole(early.shape),
            whole(ada.shape),
            whole(about.shape),
            whole(out_grad.shape),
        ],
        out_specs=[small, small, whole((8, width))] + specs,
        out_shape=[
            shape_of((part, width), BF16),
            shape_of((part, width), BF16),
            shape_of((8, width), F32),
        ]
        + shapes,
        scratch_shapes=[
            pltpu.VMEM((tokens, width), BF16),
            pltpu.VMEM((tokens, width), F32),
        ]
        + scratch,
        compiler_params=params(60),
        cost_estimate=LIGHT,
        name="project_back",
    )(core, *dq, *d_own, *received, norm_t, one, two, mod, gain, weight, cosine, sine, d_middle, early, ada, about, out_grad)


def add(target, to, keep, received, at):
    target[to] = keep[at] + received[at]


def halve(kind, words, keep, received, stay, leave):
    entries, blocks = keep.shape[:2]
    if kind == "near":
        n = words[2]
        for target, index in ((stay, n), (leave, n ^ 1)):
            for entry in range(entries // 4 * 2):
                at = entry // 2 * 4 + (index if entry % 2 == 0 else 3 - index)
                for block in range(blocks):
                    add(target, (entry, block), keep, received, (at, block))
        if entries % 4:
            for block in range(blocks):
                total = keep[entries - 1, block] + received[entries - 1, block]
                stay[entries // 4 * 2, block] = total
                leave[entries // 4 * 2, block] = total
        return
    bit = words[0 if kind == "x" else 1]
    for target, mine in ((stay, bit), (leave, 1 - bit)):
        for entry in range(entries):
            for block in range(blocks // 2):
                if blocks == 2:
                    at = mine
                elif kind == "x":
                    at = 2 * block + mine
                else:
                    at = 2 * mine + block
                add(target, (entry, block), keep, received, (entry, at))


def first_kernel(count, words, *refs):
    pairs_in = [(refs[2 * index], refs[2 * index + 1]) for index in range(count)]
    a_stay, a_leave, b_stay, b_leave, c_stay, c_leave = refs[2 * count :]
    step = pl.program_id(0)
    y, x = step // 2, step % 2
    n = words[2]

    def third(target, part, extra):
        entry = 0
        for keep, received in pairs_in:
            for index in range(keep.shape[0] if extra else keep.shape[0] // 4 * 4):
                rows = slice(part * THIRD, (part + 1) * THIRD)
                target[entry, 0] = keep[index, 0, rows, :] + received[index, 0, rows, :]
                entry += 1

    for target, match in ((a_stay, x == words[0]), (a_leave, x != words[0])):
        pl.when(match)(functools.partial(third, target, 0, True))
    for target, match in ((b_stay, y == words[1]), (b_leave, y != words[1])):
        pl.when(match)(functools.partial(third, target, 1, False))
    rows = slice(2 * THIRD, 3 * THIRD)
    for target, index in ((c_stay, n), (c_leave, n ^ 1)):
        for item, (keep, received) in enumerate(pairs_in):
            target[2 * item, 0] = keep[index, 0, rows, :] + received[index, 0, rows, :]
            target[2 * item + 1, 0] = keep[3 - index, 0, rows, :] + received[3 - index, 0, rows, :]


def first_stage(name, words, items):
    count = len(items)
    width = items[0][0].shape[3]
    entries = sum(keep.shape[0] for keep, unused in items)
    blocks_a = (entries, 2, THIRD, width)
    blocks_b = (4 * count, 2, THIRD, width)
    blocks_c = (2 * count, 4, THIRD, width)

    def spec(shape, index):
        return pl.BlockSpec((shape[0], 1, THIRD, width), index)

    def by_y(i, words):
        return (0, i // 2, 0, 0)

    def stay_x(i, words):
        return (0, jnp.clip(i - 2 * words[1], 0, 1), 0, 0)

    def leave_x(i, words):
        return (0, jnp.clip(i - 2 * (1 - words[1]), 0, 1), 0, 0)

    def each(i, words):
        return (0, i, 0, 0)

    in_specs, operands = [], []
    for keep, received in items:
        block = (keep.shape[0], 1) + keep.shape[2:]
        in_specs += [pl.BlockSpec(block, each)] * 2
        operands += [keep, received]
    return pl.pallas_call(
        functools.partial(first_kernel, count),
        grid_spec=pltpu.PrefetchScalarGridSpec(
            num_scalar_prefetch=1,
            grid=(4,),
            in_specs=in_specs,
            out_specs=[
                spec(blocks_a, by_y),
                spec(blocks_a, by_y),
                spec(blocks_b, stay_x),
                spec(blocks_b, leave_x),
                spec(blocks_c, each),
                spec(blocks_c, each),
            ],
        ),
        out_shape=[shape_of(shape, BF16) for shape in (blocks_a, blocks_b, blocks_c) for unused in range(2)],
        compiler_params=params(16),
        cost_estimate=LIGHT,
        name=name,
    )(words, *operands)


def call(kernel, name, shapes, operands, scratch=(), estimate=None):
    vmem = pl.BlockSpec(memory_space=pltpu.VMEM)
    return pl.pallas_call(
        kernel,
        in_specs=[pl.BlockSpec(memory_space=pltpu.SMEM)] + [vmem] * (len(operands) - 1),
        out_specs=[vmem] * len(shapes),
        out_shape=shapes,
        scratch_shapes=list(scratch),
        compiler_params=params(16),
        cost_estimate=estimate or LIGHT,
        name=name,
    )(*operands)


def next_kernel(kinds, words, *refs):
    for index, kind in enumerate(kinds):
        keep, received = refs[2 * index], refs[2 * index + 1]
        stay, leave = refs[2 * len(kinds) + 2 * index], refs[2 * len(kinds) + 2 * index + 1]
        halve(kind, words, keep, received, stay, leave)


def next_stage(name, kinds, words, kept, got, estimate=None):
    shapes, operands = [], [words]
    for kind, keep, received in zip(kinds, kept, got):
        entries, blocks, rows, columns = keep.shape
        if kind == "near":
            shape = (entries // 4 * 2 + entries % 4, blocks, rows, columns)
        else:
            shape = (entries, blocks // 2, rows, columns)
        shapes += [shape_of(shape, BF16)] * 2
        operands += [keep, received]
    outs = call(functools.partial(next_kernel, kinds), name, shapes, operands, estimate=estimate)
    return outs[::2], outs[1::2]


def far_kernel(words, *refs):
    keeps, gots, (stay, leave, *held) = refs[:3], refs[3:6], refs[6:]
    for third, (keep, received) in enumerate(zip(keeps, gots)):
        rows = slice(third * THIRD, (third + 1) * THIRD)
        for item in range(keep.shape[0] // 2):
            stay[item, rows, :] = keep[2 * item, 0].astype(F32) + received[2 * item, 0].astype(F32)
            leave[item, rows, :] = keep[2 * item + 1, 0] + received[2 * item + 1, 0]
    if held:
        for index, ref in enumerate((keeps[0], gots[0])):
            rows = slice(3 * THIRD + index * SMALL, 3 * THIRD + (index + 1) * SMALL)
            leave[0, rows, :] = ref[2, 0, :SMALL, :]
            held[0][index * SMALL : (index + 1) * SMALL, :] = ref[2, 0, :SMALL, :]


def far_stage(name, words, kept, got):
    count = kept[1].shape[0] // 2
    width = kept[0].shape[3]
    extra = kept[0].shape[0] % 2
    rows = 3 * THIRD
    shapes = [
        shape_of((count, rows, width), F32),
        shape_of((count, rows + extra * 2 * SMALL, width), BF16),
    ]
    if extra:
        shapes.append(shape_of((2 * SMALL, width), BF16))
    return call(far_kernel, name, shapes, (words, *kept, *got))


def end_kernel(words, keep, received, up, down):
    up[...] = keep[0] + received[0].astype(F32)
    total = keep[1] + received[1].astype(F32)
    rows, columns = total.shape
    down[:, :rows] = total[:, : columns // 2].T
    down[:, rows:] = total[:, columns // 2 :].T


def last_kernel(words, own, got, held, qkv, out, ada, table, gain_one, gain_two, mods, about, wide):
    n, w = words[2], words[3]
    rows, first = qkv.shape
    total = own[0] + got[0, :rows, :].astype(F32)
    qkv[...] = total[:, :first]
    out[...] = total[:, first:]
    slots = mods.shape[0] // 4
    count = ada.shape[1]
    depth = wide.shape[0]
    part = ada.shape[0]
    for index in range(4):
        ref, at = (held, index * SMALL) if index < 2 else (got.at[0], rows + (index - 2) * SMALL)
        value = ref[at : at + 2 * slots, :].astype(F32)
        mods[index * slots : (index + 1) * slots, :] = value[:slots, :]
        about[index * slots : (index + 1) * slots, :] = value[slots:, :]
    gains = jnp.sum(about[:, 3 * depth : 3 * depth + 2 * rows], axis=0, keepdims=True)
    gain_one[...] = gains[:, :rows]
    gain_two[...] = gains[:, rows : 2 * rows]
    embedded = about[:, :depth]
    condition = (embedded / (1.0 + jnp.exp(-embedded))).astype(BF16)
    turned = (((0,), (0,)), ((), ()))
    wide[...] = lax.dot_general(
        condition, mods[:, :count].astype(BF16), turned, preferred_element_type=F32
    )
    ada[...] = wide[pl.ds(n * part, part), :]
    time = about[:, depth : depth + 1] * 32.0 + about[:, depth + 1 : depth + 2]
    times = table.shape[0]
    lane = lax.broadcasted_iota(jnp.int32, (mods.shape[0], times), 1) + w * times
    onehot = jnp.where(time.astype(jnp.int32) == lane, 1.0, 0.0).astype(BF16)
    grad = lax.dot_general(
        onehot, mods[:, count : count + depth].astype(BF16), turned, preferred_element_type=F32
    )
    value = grad[:, :part]
    for index in range(1, depth // part):
        value = jnp.where(n == index, grad[:, index * part : (index + 1) * part], value)
    table[...] = value


def last(words, own, got, held, qkv_shape, out_shape, ada_shape, table_shape, depth, wide):
    rows = qkv_shape[0]
    width = own.shape[2]
    return call(
        last_kernel,
        "last",
        [shape_of(qkv_shape, F32), shape_of(out_shape, F32), shape_of(ada_shape, F32), shape_of(table_shape, F32)]
        + [shape_of((1, rows), F32)] * 2,
        (words, own, got, held),
        [
            pltpu.VMEM((4 * wide, width), F32),
            pltpu.VMEM((4 * wide, width), F32),
            pltpu.VMEM((depth, ada_shape[1]), F32),
        ],
    )


def make(wide, narrow):
    wide_bits = wide.bit_length() - 1

    def first_message(w, n):
        p, c = w // 2, w % 2
        return 2 * p + n // 2, 2 * c + n % 2

    def second_message(w, n):
        p, c = w // 2, w % 2
        return 2 * p + n // 2, 2 * c + 1 - n % 2

    message_one = pairs(wide, narrow, first_message)
    message_two = pairs(wide, narrow, second_message)
    flip = [pairs(wide, narrow, lambda w, n, b=b: (w ^ (1 << b), n)) for b in range(wide_bits)]
    line = [pairs(wide, narrow, lambda w, n, m=m: (w, n ^ m)) for m in range(1, narrow)]
    split = wide == 8

    def on_device(
        hidden_in,
        positions,
        time_index,
        cond_table,
        ada_weight,
        norm1_gain,
        qkv_weight,
        out_weight,
        norm2_gain,
        up_weight,
        down_weight,
        cotangent,
    ):
        w = lax.axis_index("wide")
        n = lax.axis_index("narrow")
        core = w % 2
        core_word = jnp.stack([core, w]).astype(jnp.int32)
        words = jnp.stack([(w >> 1) & 1, (w >> 2) & 1, n, w]).astype(jnp.int32)
        width = hidden_in.shape[2]
        odd = n % 2

        def take(array, index):
            return lax.dynamic_index_in_dim(array, index, axis=0, keepdims=False)

        def spread(array):
            one = lax.ppermute(take(array, odd), AXES, message_one)
            two = lax.ppermute(take(array, 1 - odd), AXES, message_two)
            return one, two

        def permute(array, table):
            return lax.ppermute(array, AXES, table)

        def across(sends):
            return [permute(send, line[index]) for index, send in enumerate(sends)]

        def reduce_blocks(current):
            for bit in range(wide_bits):
                mine = (w >> bit) & 1
                current = current.reshape((-1, 2) + current.shape[1:])
                send = lax.dynamic_index_in_dim(current, 1 - mine, axis=1, keepdims=False)
                keep = lax.dynamic_index_in_dim(current, mine, axis=1, keepdims=False)
                received = permute(send, flip[bit])
                current = (keep.astype(F32) + received.astype(F32)).astype(BF16)
            current = current[0]
            total = take(current, n).astype(F32)
            for mask in range(1, narrow):
                total += permute(take(current, n ^ mask), line[mask - 1]).astype(F32)
            return total

        wait = lax.optimization_barrier
        hidden_one, hidden_two = spread(hidden_in)
        other_time = permute(time_index, flip[0])
        positions, other_time = wait((positions, other_time))
        place_one, place_two = spread(positions)
        row_time = jnp.where(n // 2 == core, time_index[n % 2], other_time[n % 2])
        embedded = lax.dynamic_slice_in_dim(cond_table, row_time, 1, axis=0).astype(F32)
        condition = (embedded * jax.nn.sigmoid(embedded)).astype(BF16)
        modulation = dot(condition, ada_weight).reshape(6, width)
        mod = jnp.concatenate([modulation, jnp.zeros((2, width), F32)])
        gain_one = norm1_gain.reshape(1, width)
        gain_two = norm2_gain.reshape(1, width)
        depth = cond_table.shape[1]
        pair = jnp.stack([row_time // 32, row_time % 32]).astype(F32).reshape(1, 2)
        about = jnp.concatenate(
            [embedded, pair, jnp.zeros((1, 2 * depth - 2), F32)], axis=1
        )

        place = jnp.concatenate([place_one, place_two]).astype(F32)
        lane = jnp.arange(128, dtype=jnp.int32)
        frequency = 10000.0 ** (-(lane % HALF).astype(F32) / HALF)
        angles = place[:, None] * frequency
        cosine = jnp.cos(angles)
        sine = jnp.sin(angles) * jnp.where(lane % HEAD_DIM < HALF, -1.0, 1.0)

        hidden_one, hidden_two, cotangent = wait((hidden_one, hidden_two, cotangent))
        cot_one, cot_two = spread(cotangent)
        q, kv, norm_t = project(hidden_one, hidden_two, mod, gain_one, qkv_weight, cosine, sine)
        kv_other = permute(kv, flip[0])
        attended, attended_t, log_total = attend(q, kv, kv_other)
        out_one, out_two, d_attended, d_middle, sums_two, out_grad, *grads = feed(
            core_word,
            attended,
            attended_t,
            hidden_one,
            hidden_two,
            cot_one,
            cot_two,
            mod,
            gain_two,
            out_weight,
            up_weight,
            down_weight,
            wide,
            narrow,
            split,
        )
        grads_feed = grads
        dq, d_own, received = [], [], []

        def back_group(group, q):
            first, second, third = attend_back(q, kv, kv_other, d_attended, attended_t, log_total, group)
            dq.append(first)
            d_own.append(second)
            received.append(permute(third, flip[0]))

        rows = width // wide
        if split:
            axes = {"x": flip[1], "y": flip[2], "near": line[0], "far": line[2]}

            def exchange(kinds, sends):
                return [permute(send, axes[kind]) for kind, send in zip(kinds, sends)]

            turns = [("x", "y", "near"), ("y", "near", "x"), ("near", "x", "y")]
            up_keep, up_send, down_keep, down_send = grads
            down_got = permute(down_send, flip[0])
            up_got = permute(up_send, flip[0])
            back_group(0, q)
            d_own[0], up_got, down_got = wait((d_own[0], up_got, down_got))
            stages = first_stage("first_feed", words, [(up_keep, up_got), (down_keep, down_got)])
            kept, sends = stages[::2], stages[1::2]
            got = exchange(turns[0], sends)
            out_one, out_two, q, *sends = wait((out_one, out_two, q, *sends))
            out_one = permute(out_one, inverse(message_one))
            back_group(1, q)
            q, d_own[1], received[0] = wait((q, d_own[1], received[0]))
            back_group(2, q)
            dq[2], received[1], out_one, out_two, *got = wait((dq[2], received[1], out_one, out_two, *got))
            out_two = permute(out_two, inverse(message_two))
            kept, sends = next_stage("second_feed", turns[1], words, kept, got)
            got = exchange(turns[1], sends)
            dq[0], *sends = wait((dq[0], *sends))
        else:
            out_one = permute(out_one, inverse(message_one))
            out_two = permute(out_two, inverse(message_two))
            for group in range(width // (GROUP * HEAD_DIM)):
                back_group(group, q)

        grad_one, grad_two, share, *grads = project_back(
            core_word,
            dq,
            d_own,
            received,
            norm_t,
            hidden_one,
            hidden_two,
            mod,
            gain_one,
            qkv_weight,
            cosine,
            sine,
            d_middle,
            sums_two,
            ada_weight,
            about,
            out_grad,
            wide,
            narrow,
            split,
        )

        def join(one, two):
            return jnp.stack([jnp.where(odd == 0, one, two), jnp.where(odd == 0, two, one)])

        row_count = depth // narrow
        column_count = 6 * width // wide
        time_count = cond_table.shape[0] // wide
        if split:
            qkv_keep, qkv_send = grads
            qkv_got = permute(qkv_send, flip[0])
            out_two, grad_first = wait((out_two, grad_one))
            grad_one = permute(grad_one, inverse(message_one))
            grad_first, out_two, *got = wait((grad_first, out_two, *got))
            kept, sends = next_stage("third_feed", turns[2], words, kept, got, HEAVY)
            got = exchange(turns[2], sends)
            qkv_got, *sends = wait((qkv_got, *sends))
            stages = first_stage("first_qkv", words, [(qkv_keep, qkv_got)])
            kept_qkv, sends = stages[::2], stages[1::2]
            grad_one, grad_two, got[0], got[1], got[2], *sends = wait((grad_one, grad_two, *got, *sends))
            got_qkv = exchange(turns[0], sends)
            *got, sends[0] = wait((*got, sends[0]))
            own, send = far_stage("far_feed", words, kept, got)
            far_got = permute(send, axes["far"])
            *got_qkv, send = wait((*got_qkv, send))
            kept_qkv, sends = next_stage("second_qkv", turns[1], words, kept_qkv, got_qkv)
            got_qkv = exchange(turns[1], sends)
            far_got, grad_two, *sends = wait((far_got, grad_two, *sends))
            grad_two = permute(grad_two, inverse(message_two))
            grad_up, grad_down = call(
                end_kernel,
                "end_feed",
                [shape_of((rows, width), F32), shape_of((width // 2, width // narrow), F32)],
                (words, own, far_got),
            )
            *got_qkv, grad_up = wait((*got_qkv, grad_up))
            kept_qkv, sends = next_stage("third_qkv", turns[2], words, kept_qkv, got_qkv)
            got_qkv = exchange(turns[2], sends)
            own, send, held = far_stage("far_qkv", words, kept_qkv, got_qkv)
            far_got = permute(send, axes["far"])
            grad_one, grad_two, send = wait((grad_one, grad_two, send))
            hidden_grad = join(grad_one, grad_two)
            far_got, hidden_grad = wait((far_got, hidden_grad))
            grad_qkv, grad_out, grad_ada, grad_table, grad_gain_one, grad_gain_two = last(
                words,
                own,
                far_got,
                held,
                (rows, 3 * width // narrow),
                (rows, width // narrow),
                (row_count, column_count),
                (time_count, row_count),
                depth,
                wide,
            )
            gains = grad_gain_two.reshape(rows), grad_gain_one.reshape(rows)
        else:
            up_grad, down_grad = grads_feed
            (qkv_grad,) = grads
            grad_one = permute(grad_one, inverse(message_one))
            grad_two = permute(grad_two, inverse(message_two))
            hidden_grad = join(grad_one, grad_two)
            steps = down_grad.shape[0]
            grad_up = reduce_blocks(up_grad.reshape(narrow, wide, rows, width).transpose(1, 0, 2, 3))
            grad_down = reduce_blocks(
                down_grad.reshape(steps, narrow, width // narrow, wide // steps, -1)
                .transpose(0, 3, 1, 2, 4)
                .reshape(wide, narrow, width // narrow, -1)
            ).T

            def by_rows(grad):
                return reduce_blocks(
                    grad.transpose(1, 0, 2).reshape(wide, rows, narrow, -1).transpose(0, 2, 1, 3)
                )

            grad_out = by_rows(out_grad[None])
            grad_qkv = by_rows(qkv_grad)
            told = jnp.concatenate(
                [embedded, jnp.broadcast_to(row_time.astype(F32), (1, width - depth))], axis=1
            )
            share = jnp.concatenate([share, told])[None]
            for table in flip + [line[0], line[2]]:
                share = jnp.concatenate([share, permute(share, table)])
            all_mod = share[:, :6].reshape(-1, 6 * width)
            gains = jnp.sum(share[:, 6:8].reshape(-1, 2, wide, rows), axis=0)
            gains = lax.dynamic_index_in_dim(gains, w, axis=1, keepdims=False)
            my_embedded = lax.dynamic_slice_in_dim(share[:, 8, :depth], n * row_count, row_count, axis=1)
            times = share[:, 8, depth].astype(jnp.int32)
            my_gate = jax.nn.sigmoid(my_embedded)
            my_conditions = (my_embedded * my_gate).astype(BF16).astype(F32)
            my_mod = lax.dynamic_slice_in_dim(all_mod, w * column_count, column_count, axis=1)
            grad_ada = lax.dot_general(
                my_conditions,
                my_mod,
                (((0,), (0,)), ((), ())),
                precision=HIGHEST,
                preferred_element_type=F32,
            )
            my_ada = lax.dynamic_slice_in_dim(ada_weight, n * row_count, row_count, axis=0).astype(F32)
            d_condition = lax.dot_general(
                all_mod,
                my_ada,
                (((1,), (1,)), ((), ())),
                precision=HIGHEST,
                preferred_element_type=F32,
            )
            d_embedded = d_condition * my_gate * (1.0 + my_embedded * (1.0 - my_gate))
            my_times = w * time_count + jnp.arange(time_count, dtype=jnp.int32)
            onehot = (my_times[:, None] == times[None, :]).astype(F32)
            grad_table = jnp.dot(onehot, d_embedded, precision=HIGHEST, preferred_element_type=F32)
        return (
            join(out_one, out_two),
            hidden_grad,
            grad_table,
            grad_ada,
            gains[1],
            grad_qkv,
            grad_out,
            gains[0],
            grad_up,
            grad_down,
        )

    return on_device


def solution(mesh):
    in_specs = (
        P("wide", "narrow", None),
        P("wide", "narrow"),
        P("wide"),
        P(),
        P(),
        P(),
        P(),
        P(),
        P(),
        P(),
        P(),
        P("wide", "narrow", None),
    )
    out_specs = (
        P("wide", "narrow", None),
        P("wide", "narrow", None),
        P("wide", "narrow"),
        P("narrow", "wide"),
        P("wide"),
        P("wide", "narrow"),
        P("wide", "narrow"),
        P("wide"),
        P("wide", "narrow"),
        P("wide", "narrow"),
    )
    return jax.shard_map(
        make(mesh.shape["wide"], mesh.shape["narrow"]),
        mesh=mesh,
        in_specs=in_specs,
        out_specs=out_specs,
        check_vma=False,
    )
```

```python
import functools

import jax
import jax.numpy as jnp
from jax import lax
from jax.experimental import pallas as pl
from jax.experimental.pallas import tpu as pltpu
from jax.sharding import PartitionSpec as P

HEAD_DIM = 64
HALF = HEAD_DIM // 2
GROUP = 4
ONES = 16
LOG2E = 1.4426950408889634
SCALE = HEAD_DIM**-0.5
HIGHEST = lax.Precision.HIGHEST
norm_eps = 1e-05
AXES = ("wide", "narrow")
EXTRA = 32
SMALL = 32
THIRD = 32
F32 = jnp.float32
BF16 = jnp.bfloat16
MIB = 1 << 20


def cost(us):
    return pl.CostEstimate(flops=int(us * 1.15e9), bytes_accessed=int(us * 3.7e6), transcendentals=0)


LIGHT = cost(0.01)
HEAVY = cost(100)


def dot(left, right):
    return jnp.dot(left, right, preferred_element_type=F32)


def ndot(left, right):
    return lax.dot_general(left, right, (((1,), (1,)), ((), ())), preferred_element_type=F32)


def pairs(wide, narrow, target):
    result = []
    for w in range(wide):
        for n in range(narrow):
            w_to, n_to = target(w, n)
            result.append((w * narrow + n, w_to * narrow + n_to))
    return result


def inverse(table):
    return [(target, source) for source, target in table]


def normalize(hidden):
    center = hidden - jnp.mean(hidden, axis=-1, keepdims=True)
    variance = jnp.mean(center * center, axis=-1, keepdims=True)
    inverse_std = lax.rsqrt(variance + norm_eps)
    return center * inverse_std, inverse_std


def normalize_back(grad, xhat, inverse_std):
    mean_grad = jnp.mean(grad, axis=-1, keepdims=True)
    mean_both = jnp.mean(grad * xhat, axis=-1, keepdims=True)
    return (grad - mean_grad - xhat * mean_both) * inverse_std


def rotate(values, cosine, sine):
    width = values.shape[1]
    lane = lax.broadcasted_iota(jnp.int32, values.shape, 1)
    ahead = pltpu.roll(values, width - HALF, 1)
    behind = pltpu.roll(values, HALF, 1)
    swapped = jnp.where(lane % HEAD_DIM < HALF, ahead, behind)
    repeat = width // cosine.shape[1]
    cosine = jnp.concatenate([cosine] * repeat, axis=1)
    sine = jnp.concatenate([sine] * repeat, axis=1)
    return values * cosine + swapped * sine


def whole(shape):
    return pl.BlockSpec(shape, lambda *index: (0,) * len(shape))


def params(mib):
    return pltpu.CompilerParams(vmem_limit_bytes=mib * MIB)


def shape_of(shape, dtype):
    return jax.ShapeDtypeStruct(shape, dtype)


def project_kernel(one, two, mod, gain, weight, cosine, sine, q_out, kv_out, norm_t, norm):
    step = pl.program_id(0)
    part = one.shape[0]

    @pl.when(step == 0)
    def first():
        for index, ref in enumerate((one, two)):
            xhat, unused = normalize(ref[...].astype(F32))
            value = xhat * gain[...].astype(F32) * (1.0 + mod[1:2, :]) + mod[0:1, :]
            norm[index * part : (index + 1) * part, :] = value.astype(BF16)
        norm_t[...] = norm[...].T

    result = dot(norm[...], weight[...])

    @pl.when(step < 2)
    def turn():
        turned = rotate(result, cosine[...], sine[...]).astype(BF16)

        @pl.when(step == 0)
        def query():
            q_out[...] = (turned.astype(F32) * SCALE).astype(BF16)

        @pl.when(step == 1)
        def key():
            kv_out[0] = turned

    @pl.when(step == 2)
    def value():
        kv_out[0] = result.astype(BF16)


def project(one, two, mod, gain, weight, cosine, sine):
    part, width = one.shape
    tokens = 2 * part
    return pl.pallas_call(
        project_kernel,
        grid=(3,),
        in_specs=[
            whole((part, width)),
            whole((part, width)),
            whole(mod.shape),
            whole((1, width)),
            pl.BlockSpec((width, width), lambda i: (0, i)),
            whole(cosine.shape),
            whole(sine.shape),
        ],
        out_specs=[
            whole((tokens, width)),
            pl.BlockSpec((1, tokens, width), lambda i: (jnp.maximum(i - 1, 0), 0, 0)),
            whole((width, tokens)),
        ],
        out_shape=[
            shape_of((tokens, width), BF16),
            shape_of((2, tokens, width), BF16),
            shape_of((width, tokens), BF16),
        ],
        scratch_shapes=[pltpu.VMEM((tokens, width), BF16)],
        compiler_params=params(28),
        cost_estimate=LIGHT,
        name="project",
    )(one, two, mod, gain, weight, cosine, sine)


def attend_kernel(q, kv, kv_other, out, out_t, log_total, keys, values_t, scores):
    tokens, lanes = q.shape
    keys[:tokens, :] = kv[0]
    keys[tokens:, :] = kv_other[0]
    step = HEAD_DIM + ONES
    turned = kv[1].T, kv_other[1].T
    for head in range(GROUP):
        lane = slice(head * HEAD_DIM, (head + 1) * HEAD_DIM)
        rows = slice(head * step, head * step + HEAD_DIM)
        values_t[rows, :tokens] = turned[0][lane, :]
        values_t[rows, tokens:] = turned[1][lane, :]
        values_t[head * step + HEAD_DIM : (head + 1) * step, :] = jnp.ones((ONES, 2 * tokens), BF16)
    q_t = q[...].T
    row = lax.broadcasted_iota(jnp.int32, q_t.shape, 0) // HEAD_DIM
    log_total[...] = jnp.zeros_like(log_total)

    def score(head):
        scores[head % 2] = dot(keys[...], jnp.where(row == head, q_t, jnp.zeros_like(q_t)))

    score(0)
    for head in range(GROUP):
        if head + 1 < GROUP:
            score(head + 1)
        score_head = scores[head % 2]
        top = jnp.max(score_head, axis=0, keepdims=True)
        expo = jnp.exp2((score_head - top) * LOG2E).astype(BF16)
        rows = slice(head * HEAD_DIM, (head + 1) * HEAD_DIM)
        result = dot(values_t[head * step : (head + 1) * step, :], expo)
        total = result[HEAD_DIM : HEAD_DIM + 1, :]
        out_t[rows, :] = (result[:HEAD_DIM, :] / total).astype(BF16)
        log_total[0, head : head + 1, :] = top + jnp.log(total)
    out[...] = out_t[...].T


def attend(q, kv, kv_other):
    tokens, width = q.shape
    lanes = GROUP * HEAD_DIM
    groups = width // lanes
    pair = pl.BlockSpec((2, tokens, lanes), lambda g: (0, 0, g))
    flat = pl.BlockSpec((tokens, lanes), lambda g: (0, g))
    return pl.pallas_call(
        attend_kernel,
        grid=(groups,),
        in_specs=[flat, pair, pair],
        out_specs=[
            flat,
            pl.BlockSpec((lanes, tokens), lambda g: (g, 0)),
            pl.BlockSpec((1, 8, tokens), lambda g: (g, 0, 0)),
        ],
        out_shape=[
            shape_of((tokens, width), BF16),
            shape_of((width, tokens), BF16),
            shape_of((groups, 8, tokens), F32),
        ],
        scratch_shapes=[
            pltpu.VMEM((2 * tokens, lanes), BF16),
            pltpu.VMEM((lanes + GROUP * ONES, 2 * tokens), BF16),
            pltpu.VMEM((2, 2 * tokens, tokens), F32),
        ],
        compiler_params=params(28),
        cost_estimate=LIGHT,
        name="attend",
    )(q, kv, kv_other)


def attend_back_kernel(
    q, kv, kv_other, d_out, out_t, log_total, dq, d_own, dk_other, dv_other, keys_t, low, grad_low, dq_t, scores, grads
):
    tokens, lanes = q.shape
    chunk = low.shape[0]
    keys_t[:, :tokens] = kv[0].T
    keys_t[:, tokens:] = kv_other[0].T
    q_all = q[...]
    d_all = d_out[...]
    q_t = q_all.T
    d_t = d_all.T
    row = lax.broadcasted_iota(jnp.int32, q_t.shape, 0) // HEAD_DIM
    lane = lax.broadcasted_iota(jnp.int32, q_all.shape, 1) // HEAD_DIM
    product = d_t.astype(F32) * out_t[...].astype(F32)
    q_rows, d_rows = [], []
    for head in range(GROUP):
        q_rows.append(jnp.where(lane == head, q_all, jnp.zeros_like(q_all)))
        d_rows.append(jnp.where(lane == head, d_all, jnp.zeros_like(d_all)))
    q_stack = jnp.concatenate(q_rows, axis=0)
    d_stack = jnp.concatenate(d_rows, axis=0)
    items = [(index, head) for index in range(2 * tokens // chunk) for head in range(GROUP)]

    def products(item):
        index, head = items[item]
        source = kv if index * chunk < tokens else kv_other
        at = index * chunk % tokens
        q_head = jnp.where(row == head, q_t, jnp.zeros_like(q_t))
        d_head = jnp.where(row == head, d_t, jnp.zeros_like(d_t))
        scores[item % 2] = dot(source[0, at : at + chunk, :], q_head)
        grads[item % 2] = dot(source[1, at : at + chunk, :], d_head)

    products(0)
    for item, (index, head) in enumerate(items):
        if item + 1 < len(items):
            products(item + 1)
        rows = slice(head * HEAD_DIM, (head + 1) * HEAD_DIM)
        columns = slice(head * tokens, (head + 1) * tokens)
        center = jnp.sum(product[rows, :], axis=0, keepdims=True)
        offset = log_total[0, head : head + 1, :] * LOG2E
        probs = jnp.exp2(scores[item % 2] * LOG2E - offset)
        low[:, columns] = probs.astype(BF16)
        d_scores = (probs * (grads[item % 2] - center)).astype(BF16)
        grad_low[:, columns] = d_scores
        update = dot(keys_t[rows, index * chunk : (index + 1) * chunk], d_scores)
        if index == 0:
            dq_t[rows, :] = update
        else:
            dq_t[rows, :] += update
        if head < GROUP - 1:
            continue
        at = index * chunk % tokens
        d_keys = dot(grad_low[...], q_stack)
        d_values = dot(low[...], d_stack)
        if index * chunk < tokens:
            d_own[0, at : at + chunk, :] = d_keys
            d_own[1, at : at + chunk, :] = d_values
        else:
            dk_other[at : at + chunk, :] = d_keys.astype(BF16)
            dv_other[at : at + chunk, :] = d_values.astype(BF16)
    dq[...] = (dq_t[...] * SCALE).T.astype(BF16)


def attend_back(q, kv, kv_other, d_out, out_t, log_total, base, count):
    tokens, width = q.shape
    lanes = GROUP * HEAD_DIM
    chunk = min(256, tokens)
    pair = pl.BlockSpec((2, tokens, lanes), lambda g: (0, 0, base + g))
    flat = pl.BlockSpec((tokens, lanes), lambda g: (0, base + g))
    pair_out = pl.BlockSpec((2, tokens, lanes), lambda g: (0, 0, g))
    flat_out = pl.BlockSpec((tokens, lanes), lambda g: (0, g))
    return pl.pallas_call(
        attend_back_kernel,
        grid=(count,),
        in_specs=[
            flat,
            pair,
            pair,
            flat,
            pl.BlockSpec((lanes, tokens), lambda g: (base + g, 0)),
            pl.BlockSpec((1, 8, tokens), lambda g: (base + g, 0, 0)),
        ],
        out_specs=[flat_out, pair_out, flat_out, flat_out],
        out_shape=[
            shape_of((tokens, count * lanes), BF16),
            shape_of((2, tokens, count * lanes), F32),
            shape_of((tokens, count * lanes), BF16),
            shape_of((tokens, count * lanes), BF16),
        ],
        scratch_shapes=[
            pltpu.VMEM((lanes, 2 * tokens), BF16),
            pltpu.VMEM((chunk, GROUP * tokens), BF16),
            pltpu.VMEM((chunk, GROUP * tokens), BF16),
            pltpu.VMEM((lanes, tokens), F32),
            pltpu.VMEM((2, chunk, tokens), F32),
            pltpu.VMEM((2, chunk, tokens), F32),
        ],
        compiler_params=params(32),
        cost_estimate=LIGHT,
        name="attend_back",
    )(q, kv, kv_other, d_out, out_t, log_total)


def gelu_both(up):
    factor = 0.7978845608028654
    square = up * up
    angle = up * (factor + factor * 0.044715 * square)
    tanh = jnp.tanh(angle)
    half = 0.5 * (1.0 + tanh)
    slope = half + 0.5 * up * (1.0 - tanh * tanh) * (factor + 3.0 * factor * 0.044715 * square)
    return up * half, slope


def store_rows(value, targets, held, core):
    if len(targets) == 1:
        targets[0][0] = value.astype(BF16)
        return
    blocks, rows = held.shape[0] * 2, held.shape[2]
    for block in range(blocks):
        held[block // 2, block % 2] = value[block * rows : (block + 1) * rows, :].astype(BF16)
    targets[0][0] = held[:, core]
    targets[1][0] = held[:, 1 - core]


def store_columns(value, targets, core):
    value = value.astype(BF16)
    if len(targets) == 1:
        targets[0][0] = value
        return
    parts, unused, rows, columns = targets[0].shape
    columns = columns // 2
    first, second = value[:, :columns], value[:, columns:]
    stay = jnp.where(core == 0, first, second)
    leave = jnp.where(core == 0, second, first)
    for target, kept in zip(targets, (stay, leave)):
        for index in range(2 * parts):
            side = slice((index % 2) * columns, (index % 2 + 1) * columns)
            target[index // 2, 0, :, side] = kept[index * rows : (index + 1) * rows, :]


def feed_kernel(
    core_ref,
    attended,
    attended_t,
    one,
    two,
    cot_one,
    cot_two,
    mod,
    gain_ref,
    w_out,
    w_up,
    w_down,
    out_one,
    out_two,
    d_attended,
    d_middle_out,
    sums,
    out_grad,
    *rest,
):
    projected, middle, norm, norm_t, d_down, d_down_t, down, d_norm, held = rest[-9:]
    grads = rest[:-9]
    count = len(grads) // 2
    up_grad, down_grad = grads[:count], grads[count:]
    step = pl.program_id(0)
    last = pl.num_programs(0) - 1
    core = core_ref[0]
    part = one.shape[0]
    gate_one, shift, scale, gate_two = (mod[index : index + 1, :] for index in (2, 3, 4, 5))
    gain = gain_ref[...].astype(F32)

    @pl.when(step == 0)
    def begin():
        projected[...] = dot(attended[...], w_out[...])
        for index, (ref, cot) in enumerate(((one, cot_one), (two, cot_two))):
            rows = slice(index * part, (index + 1) * part)
            middle[rows, :] = ref[...].astype(F32) + gate_one * projected[rows, :]
            d_down[rows, :] = (cot[...].astype(F32) * gate_two).astype(BF16)
        xhat, unused = normalize(middle[...])
        norm[...] = (xhat * gain * (1.0 + scale) + shift).astype(BF16)
        norm_t[...] = norm[...].T
        d_down_t[...] = d_down[...].T

    @pl.when(step < last)
    def layer():
        up = dot(norm[...], w_up[...])
        activated, slope = gelu_both(up)
        activated = activated.astype(BF16)
        d_up = (ndot(d_down[...], w_down[...]) * slope).astype(BF16)
        down_step = dot(activated, w_down[...])
        norm_step = ndot(d_up, w_up[...])

        @pl.when(step == 0)
        def assign():
            down[...] = down_step
            d_norm[...] = norm_step

        @pl.when(step > 0)
        def add():
            down[...] += down_step
            d_norm[...] += norm_step

        store_rows(dot(norm_t[...], d_up), up_grad, held, core)
        store_columns(dot(d_down_t[...], activated), down_grad, core)

    @pl.when(step == last)
    def end():
        xhat, inverse_std = normalize(middle[...])
        grad = d_norm[...]
        back = normalize_back(grad * (gain * (1.0 + scale)), xhat, inverse_std)
        gate_sum = jnp.zeros_like(gate_two)
        for index, (cot, out) in enumerate(((cot_one, out_one), (cot_two, out_two))):
            rows = slice(index * part, (index + 1) * part)
            d_result = cot[...].astype(F32)
            out[...] = (middle[rows, :] + gate_two * down[rows, :]).astype(BF16)
            gate_sum += jnp.sum(d_result * down[rows, :], axis=0, keepdims=True)
            d_middle_out[rows, :] = d_result + back[rows, :]
        d_middle = d_middle_out[...]
        d_projected = (d_middle * gate_one).astype(BF16)
        both = jnp.sum(grad * xhat, axis=0, keepdims=True)
        sums[0:1, :] = jnp.sum(d_middle * projected[...], axis=0, keepdims=True)
        sums[1:2, :] = jnp.sum(grad, axis=0, keepdims=True)
        sums[2:3, :] = both * gain
        sums[3:4, :] = gate_sum
        sums[4:5, :] = both * (1.0 + scale)
        sums[5:8, :] = jnp.zeros((3, sums.shape[1]), F32)
        d_attended[...] = ndot(d_projected, w_out[...]).astype(BF16)
        out_grad[...] = dot(attended_t[...], d_projected).astype(BF16)


def grad_rows(steps, width, wide, split):
    at = lambda i: jnp.minimum(i, steps - 1)
    half, rows = wide // 2, width // wide
    if not split:
        return [pl.BlockSpec((1, width, width), lambda i: (at(i), 0, 0))], [shape_of((steps, width, width), BF16)]
    spec = pl.BlockSpec((1, half, rows, width), lambda i: (at(i), 0, 0, 0))
    return [spec] * 2, [shape_of((steps, half, rows, width), BF16)] * 2


def grad_columns(steps, width, narrow, split):
    at = lambda i: jnp.minimum(i, steps - 1)
    if not split:
        return [pl.BlockSpec((1, width, width), lambda i: (at(i), 0, 0))], [shape_of((steps, width, width), BF16)]
    rows = width // narrow // 2
    spec = pl.BlockSpec((narrow, 1, rows, width), lambda i: (0, at(i), 0, 0))
    return [spec] * 2, [shape_of((narrow, steps, rows, width), BF16)] * 2


def feed(core, attended, attended_t, one, two, cot_one, cot_two, mod, gain, w_out, w_up, w_down, wide, narrow, split):
    tokens, width = attended.shape
    part = tokens // 2
    hidden = w_up.shape[1]
    steps = hidden // width
    half, rows = (wide // 2, width // wide) if split else (1, 16)
    up_specs, up_shapes = grad_rows(steps, width, wide, split)
    down_specs, down_shapes = grad_columns(steps, width, narrow, split)
    small = whole((part, width))
    full = whole((tokens, width))
    return pl.pallas_call(
        feed_kernel,
        grid=(steps + 1,),
        in_specs=[
            pl.BlockSpec(memory_space=pltpu.SMEM),
            full,
            whole((width, tokens)),
            small,
            small,
            small,
            small,
            whole(mod.shape),
            whole((1, width)),
            whole((width, width)),
            pl.BlockSpec((width, width), lambda i: (0, jnp.minimum(i, steps - 1))),
            pl.BlockSpec((width, width), lambda i: (jnp.minimum(i, steps - 1), 0)),
        ],
        out_specs=[small, small, full, full, whole((8, width)), whole((width, width))]
        + up_specs
        + down_specs,
        out_shape=[
            shape_of((part, width), BF16),
            shape_of((part, width), BF16),
            shape_of((tokens, width), BF16),
            shape_of((tokens, width), F32),
            shape_of((8, width), F32),
            shape_of((width, width), BF16),
        ]
        + up_shapes
        + down_shapes,
        scratch_shapes=[
            pltpu.VMEM((tokens, width), F32),
            pltpu.VMEM((tokens, width), F32),
            pltpu.VMEM((tokens, width), BF16),
            pltpu.VMEM((width, tokens), BF16),
            pltpu.VMEM((tokens, width), BF16),
            pltpu.VMEM((width, tokens), BF16),
            pltpu.VMEM((tokens, width), F32),
            pltpu.VMEM((tokens, width), F32),
            pltpu.VMEM((half, 2, rows, width), BF16),
        ],
        compiler_params=params(50),
        cost_estimate=LIGHT,
        name="feed",
    )(core, attended, attended_t, one, two, cot_one, cot_two, mod, gain, w_out, w_up, w_down)


def project_back_kernel(groups, parts, core_ref, *refs):
    dq, d_own = refs[:groups], refs[groups : 2 * groups]
    dk, dv = refs[2 * groups : 3 * groups], refs[3 * groups : 4 * groups]
    refs = refs[groups:]
    refs_in = refs[3 * groups : 3 * groups + 13]
    norm_t, one, two, mod, gain_ref, weight, cosine, sine, d_middle, early, ada, about, out_grad = refs_in
    out_one, out_two, share = refs[3 * groups + 13 : 3 * groups + 16]
    grads = refs[3 * groups + 16 : -4]
    d_part, d_norm, whole_grad, held = refs[-4:]
    step = pl.program_id(0)
    part = one.shape[0]

    def lay(values):
        at = 0
        for value in values:
            d_part[:, at : at + value.shape[1]] = value.astype(BF16)
            at += value.shape[1]

    @pl.when(step == 0)
    def query():
        lay([ref[...] for ref in dq])

    @pl.when(step == 1)
    def key():
        lay([own[0] + ref[...].astype(F32) for own, ref in zip(d_own, dk)])

    @pl.when(step == 2)
    def value():
        lay([own[0] + ref[...].astype(F32) for own, ref in zip(d_own, dv)])

    @pl.when(step < 2)
    def turn():
        d_part[...] = rotate(d_part[...].astype(F32), cosine[...], -sine[...]).astype(BF16)

    norm_step = ndot(d_part[...], weight[...])
    gradient = dot(norm_t[...], d_part[...]).astype(BF16)
    width = gradient.shape[1]
    if len(grads) == 1:
        grads[0][0] = gradient
    else:
        for index in range(3):

            @pl.when(step == index)
            def keep_gradient(index=index):
                whole_grad[:, index * width : (index + 1) * width] = gradient

    @pl.when(step == 0)
    def assign():
        d_norm[...] = norm_step

    @pl.when(step > 0)
    def add():
        d_norm[...] += norm_step

    @pl.when(step == 2)
    def end():
        gain = gain_ref[...].astype(F32)
        scale = mod[1:2, :]
        plain = jnp.zeros_like(gain)
        both = jnp.zeros_like(gain)
        for index, (ref, out) in enumerate(((one, out_one), (two, out_two))):
            rows = slice(index * part, (index + 1) * part)
            xhat, inverse_std = normalize(ref[...].astype(F32))
            grad = d_norm[rows, :]
            back = normalize_back(grad * (gain * (1.0 + scale)), xhat, inverse_std)
            out[...] = (d_middle[rows, :] + back).astype(BF16)
            plain += jnp.sum(grad, axis=0, keepdims=True)
            both += jnp.sum(grad * xhat, axis=0, keepdims=True)
        share[0:1, :] = plain
        share[1:2, :] = both * gain
        share[2:7, :] = early[0:5, :]
        share[7:8, :] = both * (1.0 + scale)

        if len(grads) == 1:
            return
        core = core_ref[0]
        half, rows = held.shape[0], held.shape[2]
        blocks = 2 * half
        count = 3 * width // parts
        rest = width // parts
        for index in range(parts):
            for block in range(blocks):
                at = slice(block * rows, (block + 1) * rows)
                held[block // 2, block % 2, :, :count] = whole_grad[at, index * count : (index + 1) * count]
                held[block // 2, block % 2, :, count:] = out_grad[at, index * rest : (index + 1) * rest]
            grads[0][index] = held[:, core]
            grads[1][index] = held[:, 1 - core]
        flat = jnp.concatenate([share[index : index + 1, :] for index in range(6)], axis=1)
        depth = ada.shape[0]
        d_condition = jnp.sum(ada[...].astype(F32) * flat, axis=1, keepdims=True)
        embedded = about[:, :depth]
        gate = 1.0 / (1.0 + jnp.exp(-embedded))
        square = jnp.where(
            lax.broadcasted_iota(jnp.int32, (depth, depth), 0)
            == lax.broadcasted_iota(jnp.int32, (depth, depth), 1),
            d_condition,
            0.0,
        )
        d_embedded = jnp.sum(square, axis=0, keepdims=True) * gate * (1.0 + embedded * (1.0 - gate))
        count = flat.shape[1] // blocks
        place = lax.broadcasted_iota(jnp.int32, (EXTRA, width), 0)
        told_rest = width - about.shape[1] - 2 * rows
        for block in range(blocks):
            row = jnp.concatenate(
                [
                    flat[:, block * count : (block + 1) * count],
                    d_embedded,
                    jnp.zeros((1, width - count - depth), F32),
                ],
                axis=1,
            )
            told = jnp.concatenate(
                [
                    about[...],
                    share[7:8, block * rows : (block + 1) * rows],
                    share[6:7, block * rows : (block + 1) * rows],
                    jnp.zeros((1, told_rest), F32),
                ],
                axis=1,
            )
            mine = core_ref[1]
            value = jnp.where(place == mine, row, 0.0) + jnp.where(place == mine + blocks, told, 0.0)
            held[block // 2, block % 2, :EXTRA, :] = value.astype(BF16)
        grads[0][parts] = held[:, core]
        grads[1][parts] = held[:, 1 - core]


def project_back(
    core, dq, d_own, dk, dv, norm_t, one, two, mod, gain, weight, cosine, sine, d_middle, early, ada, about, out_grad, wide, narrow, split
):
    groups = len(dq)
    width, tokens = norm_t.shape
    part = tokens // 2
    small = whole((part, width))
    full = whole((tokens, width))
    later = [pl.BlockSpec((1,) + array.shape, lambda i: (jnp.maximum(i - 1, 0), 0, 0)) for array in dq]
    if split:
        half, rows = wide // 2, width // wide
        shape = (narrow + 1, half, rows, width)
        specs, shapes = [whole(shape)] * 2, [shape_of(shape, BF16)] * 2
        scratch = [pltpu.VMEM((width, 3 * width), BF16), pltpu.VMEM((half, 2, rows, width), BF16)]
    else:
        specs, shapes = grad_rows(3, width, wide, split)
        scratch = [pltpu.VMEM((16, 128), BF16)] * 2
    return pl.pallas_call(
        functools.partial(project_back_kernel, groups, narrow),
        grid=(3,),
        in_specs=[pl.BlockSpec(memory_space=pltpu.SMEM)]
        + [whole(array.shape) for array in dq]
        + later
        + [whole(array.shape) for array in dq] * 2
        + [
            whole((width, tokens)),
            small,
            small,
            whole(mod.shape),
            whole((1, width)),
            pl.BlockSpec((width, width), lambda i: (0, i)),
            whole(cosine.shape),
            whole(sine.shape),
            full,
            whole(early.shape),
            whole(ada.shape),
            whole(about.shape),
            whole(out_grad.shape),
        ],
        out_specs=[small, small, whole((8, width))] + specs,
        out_shape=[
            shape_of((part, width), BF16),
            shape_of((part, width), BF16),
            shape_of((8, width), F32),
        ]
        + shapes,
        scratch_shapes=[
            pltpu.VMEM((tokens, width), BF16),
            pltpu.VMEM((tokens, width), F32),
        ]
        + scratch,
        compiler_params=params(60),
        cost_estimate=LIGHT,
        name="project_back",
    )(core, *dq, *d_own, *dk, *dv, norm_t, one, two, mod, gain, weight, cosine, sine, d_middle, early, ada, about, out_grad)


def add(target, to, keep, received, at):
    target[to] = keep[at] + received[at]


def halve(kind, words, keep, received, stay, leave):
    entries, blocks = keep.shape[:2]
    if kind == "near":
        n = words[2]
        for target, index in ((stay, n), (leave, n ^ 1)):
            for entry in range(entries // 4 * 2):
                at = entry // 2 * 4 + (index if entry % 2 == 0 else 3 - index)
                for block in range(blocks):
                    add(target, (entry, block), keep, received, (at, block))
        if entries % 4:
            for block in range(blocks):
                total = keep[entries - 1, block] + received[entries - 1, block]
                stay[entries // 4 * 2, block] = total
                leave[entries // 4 * 2, block] = total
        return
    bit = words[0 if kind == "x" else 1]
    for target, mine in ((stay, bit), (leave, 1 - bit)):
        for entry in range(entries):
            for block in range(blocks // 2):
                if blocks == 2:
                    at = mine
                elif kind == "x":
                    at = 2 * block + mine
                else:
                    at = 2 * mine + block
                add(target, (entry, block), keep, received, (entry, at))


def first_kernel(count, words, *refs):
    pairs_in = [(refs[2 * index], refs[2 * index + 1]) for index in range(count)]
    a_stay, a_leave, b_stay, b_leave, c_stay, c_leave = refs[2 * count :]
    step = pl.program_id(0)
    y, x = step // 2, step % 2
    n = words[2]

    def third(target, part, extra):
        entry = 0
        for keep, received in pairs_in:
            for index in range(keep.shape[0] if extra else keep.shape[0] // 4 * 4):
                rows = slice(part * THIRD, (part + 1) * THIRD)
                target[entry, 0] = keep[index, 0, rows, :] + received[index, 0, rows, :]
                entry += 1

    for target, match in ((a_stay, x == words[0]), (a_leave, x != words[0])):
        pl.when(match)(functools.partial(third, target, 0, True))
    for target, match in ((b_stay, y == words[1]), (b_leave, y != words[1])):
        pl.when(match)(functools.partial(third, target, 1, False))
    rows = slice(2 * THIRD, 3 * THIRD)
    for target, index in ((c_stay, n), (c_leave, n ^ 1)):
        for item, (keep, received) in enumerate(pairs_in):
            target[2 * item, 0] = keep[index, 0, rows, :] + received[index, 0, rows, :]
            target[2 * item + 1, 0] = keep[3 - index, 0, rows, :] + received[3 - index, 0, rows, :]


def first_stage(name, words, items):
    count = len(items)
    width = items[0][0].shape[3]
    entries = sum(keep.shape[0] for keep, unused in items)
    blocks_a = (entries, 2, THIRD, width)
    blocks_b = (4 * count, 2, THIRD, width)
    blocks_c = (2 * count, 4, THIRD, width)

    def spec(shape, index):
        return pl.BlockSpec((shape[0], 1, THIRD, width), index)

    def by_y(i, words):
        return (0, i // 2, 0, 0)

    def stay_x(i, words):
        return (0, jnp.clip(i - 2 * words[1], 0, 1), 0, 0)

    def leave_x(i, words):
        return (0, jnp.clip(i - 2 * (1 - words[1]), 0, 1), 0, 0)

    def each(i, words):
        return (0, i, 0, 0)

    in_specs, operands = [], []
    for keep, received in items:
        block = (keep.shape[0], 1) + keep.shape[2:]
        in_specs += [pl.BlockSpec(block, each)] * 2
        operands += [keep, received]
    return pl.pallas_call(
        functools.partial(first_kernel, count),
        grid_spec=pltpu.PrefetchScalarGridSpec(
            num_scalar_prefetch=1,
            grid=(4,),
            in_specs=in_specs,
            out_specs=[
                spec(blocks_a, by_y),
                spec(blocks_a, by_y),
                spec(blocks_b, stay_x),
                spec(blocks_b, leave_x),
                spec(blocks_c, each),
                spec(blocks_c, each),
            ],
        ),
        out_shape=[shape_of(shape, BF16) for shape in (blocks_a, blocks_b, blocks_c) for unused in range(2)],
        compiler_params=params(16),
        cost_estimate=LIGHT,
        name=name,
    )(words, *operands)


def call(kernel, name, shapes, operands, scratch=(), estimate=None):
    vmem = pl.BlockSpec(memory_space=pltpu.VMEM)
    return pl.pallas_call(
        kernel,
        in_specs=[pl.BlockSpec(memory_space=pltpu.SMEM)] + [vmem] * (len(operands) - 1),
        out_specs=[vmem] * len(shapes),
        out_shape=shapes,
        scratch_shapes=list(scratch),
        compiler_params=params(16),
        cost_estimate=estimate or LIGHT,
        name=name,
    )(*operands)


def next_kernel(kinds, words, *refs):
    for index, kind in enumerate(kinds):
        keep, received = refs[2 * index], refs[2 * index + 1]
        stay, leave = refs[2 * len(kinds) + 2 * index], refs[2 * len(kinds) + 2 * index + 1]
        halve(kind, words, keep, received, stay, leave)


def next_stage(name, kinds, words, kept, got, estimate=None):
    shapes, operands = [], [words]
    for kind, keep, received in zip(kinds, kept, got):
        entries, blocks, rows, columns = keep.shape
        if kind == "near":
            shape = (entries // 4 * 2 + entries % 4, blocks, rows, columns)
        else:
            shape = (entries, blocks // 2, rows, columns)
        shapes += [shape_of(shape, BF16)] * 2
        operands += [keep, received]
    outs = call(functools.partial(next_kernel, kinds), name, shapes, operands, estimate=estimate)
    return outs[::2], outs[1::2]


def far_kernel(words, *refs):
    keeps, gots, (stay, leave, *held) = refs[:3], refs[3:6], refs[6:]
    for third, (keep, received) in enumerate(zip(keeps, gots)):
        rows = slice(third * THIRD, (third + 1) * THIRD)
        for item in range(keep.shape[0] // 2):
            stay[item, rows, :] = keep[2 * item, 0].astype(F32) + received[2 * item, 0].astype(F32)
            leave[item, rows, :] = keep[2 * item + 1, 0] + received[2 * item + 1, 0]
    if held:
        for index, ref in enumerate((keeps[0], gots[0])):
            rows = slice(3 * THIRD + index * SMALL, 3 * THIRD + (index + 1) * SMALL)
            leave[0, rows, :] = ref[2, 0, :SMALL, :]
            held[0][index * SMALL : (index + 1) * SMALL, :] = ref[2, 0, :SMALL, :]


def far_stage(name, words, kept, got):
    count = kept[1].shape[0] // 2
    width = kept[0].shape[3]
    extra = kept[0].shape[0] % 2
    rows = 3 * THIRD
    shapes = [
        shape_of((count, rows, width), F32),
        shape_of((count, rows + extra * 2 * SMALL, width), BF16),
    ]
    if extra:
        shapes.append(shape_of((2 * SMALL, width), BF16))
    return call(far_kernel, name, shapes, (words, *kept, *got))


def end_kernel(words, keep, received, up, down):
    up[...] = keep[0] + received[0].astype(F32)
    total = keep[1] + received[1].astype(F32)
    rows, columns = total.shape
    down[:, :rows] = total[:, : columns // 2].T
    down[:, rows:] = total[:, columns // 2 :].T


def last_kernel(words, own, got, held, qkv, out, ada, table, gain_one, gain_two, mods, about, wide):
    n, w = words[2], words[3]
    rows, first = qkv.shape
    total = own[0] + got[0, :rows, :].astype(F32)
    qkv[...] = total[:, :first]
    out[...] = total[:, first:]
    slots = mods.shape[0] // 4
    count = ada.shape[1]
    depth = wide.shape[0]
    part = ada.shape[0]
    for index in range(4):
        ref, at = (held, index * SMALL) if index < 2 else (got.at[0], rows + (index - 2) * SMALL)
        value = ref[at : at + 2 * slots, :].astype(F32)
        mods[index * slots : (index + 1) * slots, :] = value[:slots, :]
        about[index * slots : (index + 1) * slots, :] = value[slots:, :]
    gains = jnp.sum(about[:, 3 * depth : 3 * depth + 2 * rows], axis=0, keepdims=True)
    gain_one[...] = gains[:, :rows]
    gain_two[...] = gains[:, rows : 2 * rows]
    embedded = about[:, :depth]
    condition = (embedded / (1.0 + jnp.exp(-embedded))).astype(BF16)
    turned = (((0,), (0,)), ((), ()))
    wide[...] = lax.dot_general(
        condition, mods[:, :count].astype(BF16), turned, preferred_element_type=F32
    )
    ada[...] = wide[pl.ds(n * part, part), :]
    time = about[:, depth : depth + 1] * 32.0 + about[:, depth + 1 : depth + 2]
    times = table.shape[0]
    lane = lax.broadcasted_iota(jnp.int32, (mods.shape[0], times), 1) + w * times
    onehot = jnp.where(time.astype(jnp.int32) == lane, 1.0, 0.0).astype(BF16)
    grad = lax.dot_general(
        onehot, mods[:, count : count + depth].astype(BF16), turned, preferred_element_type=F32
    )
    value = grad[:, :part]
    for index in range(1, depth // part):
        value = jnp.where(n == index, grad[:, index * part : (index + 1) * part], value)
    table[...] = value


def last(words, own, got, held, qkv_shape, out_shape, ada_shape, table_shape, depth, wide):
    rows = qkv_shape[0]
    width = own.shape[2]
    return call(
        last_kernel,
        "last",
        [shape_of(qkv_shape, F32), shape_of(out_shape, F32), shape_of(ada_shape, F32), shape_of(table_shape, F32)]
        + [shape_of((1, rows), F32)] * 2,
        (words, own, got, held),
        [
            pltpu.VMEM((4 * wide, width), F32),
            pltpu.VMEM((4 * wide, width), F32),
            pltpu.VMEM((depth, ada_shape[1]), F32),
        ],
    )


def make(wide, narrow):
    wide_bits = wide.bit_length() - 1

    def first_message(w, n):
        p, c = w // 2, w % 2
        return 2 * p + n // 2, 2 * c + n % 2

    def second_message(w, n):
        p, c = w // 2, w % 2
        return 2 * p + n // 2, 2 * c + 1 - n % 2

    message_one = pairs(wide, narrow, first_message)
    message_two = pairs(wide, narrow, second_message)
    flip = [pairs(wide, narrow, lambda w, n, b=b: (w ^ (1 << b), n)) for b in range(wide_bits)]
    line = [pairs(wide, narrow, lambda w, n, m=m: (w, n ^ m)) for m in range(1, narrow)]
    split = wide == 8

    def on_device(
        hidden_in,
        positions,
        time_index,
        cond_table,
        ada_weight,
        norm1_gain,
        qkv_weight,
        out_weight,
        norm2_gain,
        up_weight,
        down_weight,
        cotangent,
    ):
        w = lax.axis_index("wide")
        n = lax.axis_index("narrow")
        core = w % 2
        core_word = jnp.stack([core, w]).astype(jnp.int32)
        words = jnp.stack([(w >> 1) & 1, (w >> 2) & 1, n, w]).astype(jnp.int32)
        width = hidden_in.shape[2]
        odd = n % 2

        def take(array, index):
            return lax.dynamic_index_in_dim(array, index, axis=0, keepdims=False)

        def spread(array):
            one = lax.ppermute(take(array, odd), AXES, message_one)
            two = lax.ppermute(take(array, 1 - odd), AXES, message_two)
            return one, two

        def permute(array, table):
            return lax.ppermute(array, AXES, table)

        def across(sends):
            return [permute(send, line[index]) for index, send in enumerate(sends)]

        def reduce_blocks(current):
            for bit in range(wide_bits):
                mine = (w >> bit) & 1
                current = current.reshape((-1, 2) + current.shape[1:])
                send = lax.dynamic_index_in_dim(current, 1 - mine, axis=1, keepdims=False)
                keep = lax.dynamic_index_in_dim(current, mine, axis=1, keepdims=False)
                received = permute(send, flip[bit])
                current = (keep.astype(F32) + received.astype(F32)).astype(BF16)
            current = current[0]
            total = take(current, n).astype(F32)
            for mask in range(1, narrow):
                total += permute(take(current, n ^ mask), line[mask - 1]).astype(F32)
            return total

        wait = lax.optimization_barrier
        hidden_one, hidden_two = spread(hidden_in)
        other_time = permute(time_index, flip[0])
        positions, other_time = wait((positions, other_time))
        place_one, place_two = spread(positions)
        row_time = jnp.where(n // 2 == core, time_index[n % 2], other_time[n % 2])
        embedded = lax.dynamic_slice_in_dim(cond_table, row_time, 1, axis=0).astype(F32)
        condition = (embedded * jax.nn.sigmoid(embedded)).astype(BF16)
        modulation = dot(condition, ada_weight).reshape(6, width)
        mod = jnp.concatenate([modulation, jnp.zeros((2, width), F32)])
        gain_one = norm1_gain.reshape(1, width)
        gain_two = norm2_gain.reshape(1, width)
        depth = cond_table.shape[1]
        pair = jnp.stack([row_time // 32, row_time % 32]).astype(F32).reshape(1, 2)
        about = jnp.concatenate(
            [embedded, pair, jnp.zeros((1, 2 * depth - 2), F32)], axis=1
        )

        place = jnp.concatenate([place_one, place_two]).astype(F32)
        lane = jnp.arange(128, dtype=jnp.int32)
        frequency = 10000.0 ** (-(lane % HALF).astype(F32) / HALF)
        angles = place[:, None] * frequency
        cosine = jnp.cos(angles)
        sine = jnp.sin(angles) * jnp.where(lane % HEAD_DIM < HALF, -1.0, 1.0)

        hidden_one, hidden_two, cotangent = wait((hidden_one, hidden_two, cotangent))
        cot_one, cot_two = spread(cotangent)
        q, kv, norm_t = project(hidden_one, hidden_two, mod, gain_one, qkv_weight, cosine, sine)
        kv_other = permute(kv, flip[0])
        attended, attended_t, log_total = attend(q, kv, kv_other)
        out_one, out_two, d_attended, d_middle, sums_two, out_grad, *grads = feed(
            core_word,
            attended,
            attended_t,
            hidden_one,
            hidden_two,
            cot_one,
            cot_two,
            mod,
            gain_two,
            out_weight,
            up_weight,
            down_weight,
            wide,
            narrow,
            split,
        )
        grads_feed = grads
        def back_groups(q, base, count):
            return attend_back(q, kv, kv_other, d_attended, attended_t, log_total, base, count)

        rows = width // wide
        if split:
            axes = {"x": flip[1], "y": flip[2], "near": line[0], "far": line[2]}

            def exchange(kinds, sends):
                return [permute(send, axes[kind]) for kind, send in zip(kinds, sends)]

            turns = [("x", "y", "near"), ("y", "near", "x"), ("near", "x", "y")]
            up_keep, up_send, down_keep, down_send = grads
            down_got = permute(down_send, flip[0])
            up_got = permute(up_send, flip[0])
            groups = width // (GROUP * HEAD_DIM)
            dq_first, own_first, dk_first, dv_first = back_groups(q, 0, 1)
            own_first, up_got, down_got = wait((own_first, up_got, down_got))
            stages = first_stage("first_feed", words, [(up_keep, up_got), (down_keep, down_got)])
            kept, sends = stages[::2], stages[1::2]
            got = exchange(turns[0], sends)
            out_one, out_two, dk_first, dv_first, q, *sends = wait((out_one, out_two, dk_first, dv_first, q, *sends))
            out_one = permute(out_one, inverse(message_one))
            dk_first, dv_first = permute(dk_first, flip[0]), permute(dv_first, flip[0])
            dq_second, own_second, dk_second, dv_second = back_groups(q, 1, groups - 1)
            dq_second, dk_first, dv_first = wait((dq_second, dk_first, dv_first))
            dk_second, dv_second = permute(dk_second, flip[0]), permute(dv_second, flip[0])
            dq_second, out_one, out_two, *got = wait((dq_second, out_one, out_two, *got))
            out_two = permute(out_two, inverse(message_two))
            kept, sends = next_stage("second_feed", turns[1], words, kept, got)
            got = exchange(turns[1], sends)
            dq_first, *sends = wait((dq_first, *sends))
            dq, d_own = [dq_first, dq_second], [own_first, own_second]
            dk, dv = [dk_first, dk_second], [dv_first, dv_second]
        else:
            out_one = permute(out_one, inverse(message_one))
            out_two = permute(out_two, inverse(message_two))
            first, second, third, fourth = back_groups(q, 0, width // (GROUP * HEAD_DIM))
            dq, d_own, dk, dv = [first], [second], [permute(third, flip[0])], [permute(fourth, flip[0])]

        grad_one, grad_two, share, *grads = project_back(
            core_word,
            dq,
            d_own,
            dk,
            dv,
            norm_t,
            hidden_one,
            hidden_two,
            mod,
            gain_one,
            qkv_weight,
            cosine,
            sine,
            d_middle,
            sums_two,
            ada_weight,
            about,
            out_grad,
            wide,
            narrow,
            split,
        )

        def join(one, two):
            return jnp.stack([jnp.where(odd == 0, one, two), jnp.where(odd == 0, two, one)])

        row_count = depth // narrow
        column_count = 6 * width // wide
        time_count = cond_table.shape[0] // wide
        if split:
            qkv_keep, qkv_send = grads
            qkv_got = permute(qkv_send, flip[0])
            out_two, grad_first = wait((out_two, grad_one))
            grad_one = permute(grad_one, inverse(message_one))
            grad_first, out_two, *got = wait((grad_first, out_two, *got))
            kept, sends = next_stage("third_feed", turns[2], words, kept, got, HEAVY)
            got = exchange(turns[2], sends)
            qkv_got, *sends = wait((qkv_got, *sends))
            stages = first_stage("first_qkv", words, [(qkv_keep, qkv_got)])
            kept_qkv, sends = stages[::2], stages[1::2]
            grad_one, grad_two, got[0], got[1], got[2], *sends = wait((grad_one, grad_two, *got, *sends))
            got_qkv = exchange(turns[0], sends)
            *got, sends[0] = wait((*got, sends[0]))
            own, send = far_stage("far_feed", words, kept, got)
            far_got = permute(send, axes["far"])
            *got_qkv, send = wait((*got_qkv, send))
            kept_qkv, sends = next_stage("second_qkv", turns[1], words, kept_qkv, got_qkv)
            got_qkv = exchange(turns[1], sends)
            far_got, grad_two, *sends = wait((far_got, grad_two, *sends))
            grad_two = permute(grad_two, inverse(message_two))
            grad_up, grad_down = call(
                end_kernel,
                "end_feed",
                [shape_of((rows, width), F32), shape_of((width // 2, width // narrow), F32)],
                (words, own, far_got),
            )
            *got_qkv, grad_up = wait((*got_qkv, grad_up))
            kept_qkv, sends = next_stage("third_qkv", turns[2], words, kept_qkv, got_qkv)
            got_qkv = exchange(turns[2], sends)
            own, send, held = far_stage("far_qkv", words, kept_qkv, got_qkv)
            far_got = permute(send, axes["far"])
            grad_one, grad_two, send = wait((grad_one, grad_two, send))
            hidden_grad = join(grad_one, grad_two)
            far_got, hidden_grad = wait((far_got, hidden_grad))
            grad_qkv, grad_out, grad_ada, grad_table, grad_gain_one, grad_gain_two = last(
                words,
                own,
                far_got,
                held,
                (rows, 3 * width // narrow),
                (rows, width // narrow),
                (row_count, column_count),
                (time_count, row_count),
                depth,
                wide,
            )
            gains = grad_gain_two.reshape(rows), grad_gain_one.reshape(rows)
        else:
            up_grad, down_grad = grads_feed
            (qkv_grad,) = grads
            grad_one = permute(grad_one, inverse(message_one))
            grad_two = permute(grad_two, inverse(message_two))
            hidden_grad = join(grad_one, grad_two)
            steps = down_grad.shape[0]
            grad_up = reduce_blocks(up_grad.reshape(narrow, wide, rows, width).transpose(1, 0, 2, 3))
            grad_down = reduce_blocks(
                down_grad.reshape(steps, narrow, width // narrow, wide // steps, -1)
                .transpose(0, 3, 1, 2, 4)
                .reshape(wide, narrow, width // narrow, -1)
            ).T

            def by_rows(grad):
                return reduce_blocks(
                    grad.transpose(1, 0, 2).reshape(wide, rows, narrow, -1).transpose(0, 2, 1, 3)
                )

            grad_out = by_rows(out_grad[None])
            grad_qkv = by_rows(qkv_grad)
            told = jnp.concatenate(
                [embedded, jnp.broadcast_to(row_time.astype(F32), (1, width - depth))], axis=1
            )
            share = jnp.concatenate([share, told])[None]
            for table in flip + [line[0], line[2]]:
                share = jnp.concatenate([share, permute(share, table)])
            all_mod = share[:, :6].reshape(-1, 6 * width)
            gains = jnp.sum(share[:, 6:8].reshape(-1, 2, wide, rows), axis=0)
            gains = lax.dynamic_index_in_dim(gains, w, axis=1, keepdims=False)
            my_embedded = lax.dynamic_slice_in_dim(share[:, 8, :depth], n * row_count, row_count, axis=1)
            times = share[:, 8, depth].astype(jnp.int32)
            my_gate = jax.nn.sigmoid(my_embedded)
            my_conditions = (my_embedded * my_gate).astype(BF16).astype(F32)
            my_mod = lax.dynamic_slice_in_dim(all_mod, w * column_count, column_count, axis=1)
            grad_ada = lax.dot_general(
                my_conditions,
                my_mod,
                (((0,), (0,)), ((), ())),
                precision=HIGHEST,
                preferred_element_type=F32,
            )
            my_ada = lax.dynamic_slice_in_dim(ada_weight, n * row_count, row_count, axis=0).astype(F32)
            d_condition = lax.dot_general(
                all_mod,
                my_ada,
                (((1,), (1,)), ((), ())),
                precision=HIGHEST,
                preferred_element_type=F32,
            )
            d_embedded = d_condition * my_gate * (1.0 + my_embedded * (1.0 - my_gate))
            my_times = w * time_count + jnp.arange(time_count, dtype=jnp.int32)
            onehot = (my_times[:, None] == times[None, :]).astype(F32)
            grad_table = jnp.dot(onehot, d_embedded, precision=HIGHEST, preferred_element_type=F32)
        return (
            join(out_one, out_two),
            hidden_grad,
            grad_table,
            grad_ada,
            gains[1],
            grad_qkv,
            grad_out,
            gains[0],
            grad_up,
            grad_down,
        )

    return on_device


def solution(mesh):
    in_specs = (
        P("wide", "narrow", None),
        P("wide", "narrow"),
        P("wide"),
        P(),
        P(),
        P(),
        P(),
        P(),
        P(),
        P(),
        P(),
        P("wide", "narrow", None),
    )
    out_specs = (
        P("wide", "narrow", None),
        P("wide", "narrow", None),
        P("wide", "narrow"),
        P("narrow", "wide"),
        P("wide"),
        P("wide", "narrow"),
        P("wide", "narrow"),
        P("wide"),
        P("wide", "narrow"),
        P("wide", "narrow"),
    )
    return jax.shard_map(
        make(mesh.shape["wide"], mesh.shape["narrow"]),
        mesh=mesh,
        in_specs=in_specs,
        out_specs=out_specs,
        check_vma=False,
    )
```

```python
import functools

import jax
import jax.numpy as jnp
from jax import lax
from jax.experimental import pallas as pl
from jax.experimental.pallas import tpu as pltpu
from jax.sharding import PartitionSpec as P

HEAD_DIM = 64
HALF = HEAD_DIM // 2
GROUP = 4
ONES = 16
LOG2E = 1.4426950408889634
SCALE = HEAD_DIM**-0.5
HIGHEST = lax.Precision.HIGHEST
norm_eps = 1e-05
AXES = ("wide", "narrow")
EXTRA = 32
SMALL = 32
THIRD = 32
F32 = jnp.float32
BF16 = jnp.bfloat16
MIB = 1 << 20


def cost(us):
    return pl.CostEstimate(flops=int(us * 1.15e9), bytes_accessed=int(us * 3.7e6), transcendentals=0)


LIGHT = cost(0.01)
HEAVY = cost(100)


def dot(left, right):
    return jnp.dot(left, right, preferred_element_type=F32)


def ndot(left, right):
    return lax.dot_general(left, right, (((1,), (1,)), ((), ())), preferred_element_type=F32)


def pairs(wide, narrow, target):
    result = []
    for w in range(wide):
        for n in range(narrow):
            w_to, n_to = target(w, n)
            result.append((w * narrow + n, w_to * narrow + n_to))
    return result


def inverse(table):
    return [(target, source) for source, target in table]


def normalize(hidden):
    center = hidden - jnp.mean(hidden, axis=-1, keepdims=True)
    variance = jnp.mean(center * center, axis=-1, keepdims=True)
    inverse_std = lax.rsqrt(variance + norm_eps)
    return center * inverse_std, inverse_std


def normalize_back(grad, xhat, inverse_std):
    mean_grad = jnp.mean(grad, axis=-1, keepdims=True)
    mean_both = jnp.mean(grad * xhat, axis=-1, keepdims=True)
    return (grad - mean_grad - xhat * mean_both) * inverse_std


def rotate(values, cosine, sine):
    width = values.shape[1]
    lane = lax.broadcasted_iota(jnp.int32, values.shape, 1)
    ahead = pltpu.roll(values, width - HALF, 1)
    behind = pltpu.roll(values, HALF, 1)
    swapped = jnp.where(lane % HEAD_DIM < HALF, ahead, behind)
    repeat = width // cosine.shape[1]
    cosine = jnp.concatenate([cosine] * repeat, axis=1)
    sine = jnp.concatenate([sine] * repeat, axis=1)
    return values * cosine + swapped * sine


def whole(shape):
    return pl.BlockSpec(shape, lambda *index: (0,) * len(shape))


def params(mib):
    return pltpu.CompilerParams(vmem_limit_bytes=mib * MIB)


def shape_of(shape, dtype):
    return jax.ShapeDtypeStruct(shape, dtype)


def project_kernel(one, two, mod, gain, weight, cosine, sine, q_out, kv_out, norm_t, norm):
    step = pl.program_id(0)
    part = one.shape[0]

    @pl.when(step == 0)
    def first():
        for index, ref in enumerate((one, two)):
            xhat, unused = normalize(ref[...].astype(F32))
            value = xhat * gain[...].astype(F32) * (1.0 + mod[1:2, :]) + mod[0:1, :]
            norm[index * part : (index + 1) * part, :] = value.astype(BF16)
        norm_t[...] = norm[...].T

    result = dot(norm[...], weight[...])

    @pl.when(step == 0)
    def query():
        q_out[...] = (rotate(result, cosine[...], sine[...]).astype(BF16).astype(F32) * SCALE).astype(BF16)

    @pl.when(step == 1)
    def key():
        kv_out[0] = rotate(result, cosine[...], sine[...]).astype(BF16)

    @pl.when(step == 2)
    def value():
        kv_out[0] = result.astype(BF16)


def project(one, two, mod, gain, weight, cosine, sine):
    part, width = one.shape
    tokens = 2 * part
    return pl.pallas_call(
        project_kernel,
        grid=(3,),
        in_specs=[
            whole((part, width)),
            whole((part, width)),
            whole(mod.shape),
            whole((1, width)),
            pl.BlockSpec((width, width), lambda i: (0, i)),
            whole(cosine.shape),
            whole(sine.shape),
        ],
        out_specs=[
            whole((tokens, width)),
            pl.BlockSpec((1, tokens, width), lambda i: (jnp.maximum(i - 1, 0), 0, 0)),
            whole((width, tokens)),
        ],
        out_shape=[
            shape_of((tokens, width), BF16),
            shape_of((2, tokens, width), BF16),
            shape_of((width, tokens), BF16),
        ],
        scratch_shapes=[pltpu.VMEM((tokens, width), BF16)],
        compiler_params=params(28),
        cost_estimate=LIGHT,
        name="project",
    )(one, two, mod, gain, weight, cosine, sine)


def attend_kernel(q, kv, kv_other, out, out_t, log_total, keys, values_t, scores):
    tokens, lanes = q.shape
    keys[:tokens, :] = kv[0]
    keys[tokens:, :] = kv_other[0]
    step = HEAD_DIM + ONES
    turned = kv[1].T, kv_other[1].T
    for head in range(GROUP):
        lane = slice(head * HEAD_DIM, (head + 1) * HEAD_DIM)
        rows = slice(head * step, head * step + HEAD_DIM)
        values_t[rows, :tokens] = turned[0][lane, :]
        values_t[rows, tokens:] = turned[1][lane, :]
        values_t[head * step + HEAD_DIM : (head + 1) * step, :] = jnp.ones((ONES, 2 * tokens), BF16)
    q_t = q[...].T
    row = lax.broadcasted_iota(jnp.int32, q_t.shape, 0) // HEAD_DIM
    log_total[...] = jnp.zeros_like(log_total)

    def score(head):
        scores[head % 2] = dot(keys[...], jnp.where(row == head, q_t, jnp.zeros_like(q_t)))

    score(0)
    for head in range(GROUP):
        if head + 1 < GROUP:
            score(head + 1)
        score_head = scores[head % 2]
        top = jnp.max(score_head, axis=0, keepdims=True)
        expo = jnp.exp2((score_head - top) * LOG2E).astype(BF16)
        rows = slice(head * HEAD_DIM, (head + 1) * HEAD_DIM)
        result = dot(values_t[head * step : (head + 1) * step, :], expo)
        total = result[HEAD_DIM : HEAD_DIM + 1, :]
        out_t[rows, :] = (result[:HEAD_DIM, :] / total).astype(BF16)
        log_total[0, head : head + 1, :] = top + jnp.log(total)
    out[...] = out_t[...].T


def attend(q, kv, kv_other):
    tokens, width = q.shape
    lanes = GROUP * HEAD_DIM
    groups = width // lanes
    pair = pl.BlockSpec((2, tokens, lanes), lambda g: (0, 0, g))
    flat = pl.BlockSpec((tokens, lanes), lambda g: (0, g))
    return pl.pallas_call(
        attend_kernel,
        grid=(groups,),
        in_specs=[flat, pair, pair],
        out_specs=[
            flat,
            pl.BlockSpec((lanes, tokens), lambda g: (g, 0)),
            pl.BlockSpec((1, 8, tokens), lambda g: (g, 0, 0)),
        ],
        out_shape=[
            shape_of((tokens, width), BF16),
            shape_of((width, tokens), BF16),
            shape_of((groups, 8, tokens), F32),
        ],
        scratch_shapes=[
            pltpu.VMEM((2 * tokens, lanes), BF16),
            pltpu.VMEM((lanes + GROUP * ONES, 2 * tokens), BF16),
            pltpu.VMEM((2, 2 * tokens, tokens), F32),
        ],
        compiler_params=params(28),
        cost_estimate=LIGHT,
        name="attend",
    )(q, kv, kv_other)


def attend_back_kernel(
    q, kv, kv_other, d_out, out_t, log_total, dq, d_own, d_other, keys_t, low, grad_low, dq_t, scores, grads
):
    tokens, lanes = q.shape
    chunk = low.shape[0]
    keys_t[:, :tokens] = kv[0].T
    keys_t[:, tokens:] = kv_other[0].T
    q_all = q[...]
    d_all = d_out[...]
    q_t = q_all.T
    d_t = d_all.T
    row = lax.broadcasted_iota(jnp.int32, q_t.shape, 0) // HEAD_DIM
    lane = lax.broadcasted_iota(jnp.int32, q_all.shape, 1) // HEAD_DIM
    product = d_t.astype(F32) * out_t[...].astype(F32)
    q_rows, d_rows = [], []
    for head in range(GROUP):
        q_rows.append(jnp.where(lane == head, q_all, jnp.zeros_like(q_all)))
        d_rows.append(jnp.where(lane == head, d_all, jnp.zeros_like(d_all)))
    q_stack = jnp.concatenate(q_rows, axis=0)
    d_stack = jnp.concatenate(d_rows, axis=0)
    items = [(index, head) for index in range(2 * tokens // chunk) for head in range(GROUP)]

    def products(item):
        index, head = items[item]
        source = kv if index * chunk < tokens else kv_other
        at = index * chunk % tokens
        q_head = jnp.where(row == head, q_t, jnp.zeros_like(q_t))
        d_head = jnp.where(row == head, d_t, jnp.zeros_like(d_t))
        scores[item % 2] = dot(source[0, at : at + chunk, :], q_head)
        grads[item % 2] = dot(source[1, at : at + chunk, :], d_head)

    products(0)
    for item, (index, head) in enumerate(items):
        if item + 1 < len(items):
            products(item + 1)
        rows = slice(head * HEAD_DIM, (head + 1) * HEAD_DIM)
        columns = slice(head * tokens, (head + 1) * tokens)
        center = jnp.sum(product[rows, :], axis=0, keepdims=True)
        offset = log_total[0, head : head + 1, :] * LOG2E
        probs = jnp.exp2(scores[item % 2] * LOG2E - offset)
        low[:, columns] = probs.astype(BF16)
        d_scores = (probs * (grads[item % 2] - center)).astype(BF16)
        grad_low[:, columns] = d_scores
        update = dot(keys_t[rows, index * chunk : (index + 1) * chunk], d_scores)
        if index == 0:
            dq_t[rows, :] = update
        else:
            dq_t[rows, :] += update
        if head < GROUP - 1:
            continue
        at = index * chunk % tokens
        d_keys = dot(grad_low[...], q_stack)
        d_values = dot(low[...], d_stack)
        if index * chunk < tokens:
            d_own[0, at : at + chunk, :] = d_keys
            d_own[1, at : at + chunk, :] = d_values
        else:
            d_other[0, at : at + chunk, :] = d_keys.astype(BF16)
            d_other[1, at : at + chunk, :] = d_values.astype(BF16)
    dq[...] = (dq_t[...] * SCALE).T.astype(BF16)


def attend_back(q, kv, kv_other, d_out, out_t, log_total, group):
    tokens, width = q.shape
    lanes = GROUP * HEAD_DIM
    chunk = min(256, tokens)
    pair = pl.BlockSpec((2, tokens, lanes), lambda g: (0, 0, group))
    flat = pl.BlockSpec((tokens, lanes), lambda g: (0, group))
    pair_out = whole((2, tokens, lanes))
    return pl.pallas_call(
        attend_back_kernel,
        grid=(1,),
        in_specs=[
            flat,
            pair,
            pair,
            flat,
            pl.BlockSpec((lanes, tokens), lambda g: (group, 0)),
            pl.BlockSpec((1, 8, tokens), lambda g: (group, 0, 0)),
        ],
        out_specs=[whole((tokens, lanes)), pair_out, pair_out],
        out_shape=[
            shape_of((tokens, lanes), BF16),
            shape_of((2, tokens, lanes), F32),
            shape_of((2, tokens, lanes), BF16),
        ],
        scratch_shapes=[
            pltpu.VMEM((lanes, 2 * tokens), BF16),
            pltpu.VMEM((chunk, GROUP * tokens), BF16),
            pltpu.VMEM((chunk, GROUP * tokens), BF16),
            pltpu.VMEM((lanes, tokens), F32),
            pltpu.VMEM((2, chunk, tokens), F32),
            pltpu.VMEM((2, chunk, tokens), F32),
        ],
        compiler_params=params(24),
        cost_estimate=LIGHT,
        name="attend_back",
    )(q, kv, kv_other, d_out, out_t, log_total)


def gelu_both(up):
    factor = 0.7978845608028654
    square = up * up
    angle = up * (factor + factor * 0.044715 * square)
    tanh = jnp.tanh(angle)
    half = 0.5 * (1.0 + tanh)
    slope = half + 0.5 * up * (1.0 - tanh * tanh) * (factor + 3.0 * factor * 0.044715 * square)
    return up * half, slope


def store_rows(value, targets, held, core):
    if len(targets) == 1:
        targets[0][0] = value.astype(BF16)
        return
    blocks, rows = held.shape[0] * 2, held.shape[2]
    for block in range(blocks):
        held[block // 2, block % 2] = value[block * rows : (block + 1) * rows, :].astype(BF16)
    targets[0][0] = held[:, core]
    targets[1][0] = held[:, 1 - core]


def store_columns(value, targets, core):
    value = value.astype(BF16)
    if len(targets) == 1:
        targets[0][0] = value
        return
    parts, unused, rows, columns = targets[0].shape
    columns = columns // 2
    first, second = value[:, :columns], value[:, columns:]
    stay = jnp.where(core == 0, first, second)
    leave = jnp.where(core == 0, second, first)
    for target, kept in zip(targets, (stay, leave)):
        for index in range(2 * parts):
            side = slice((index % 2) * columns, (index % 2 + 1) * columns)
            target[index // 2, 0, :, side] = kept[index * rows : (index + 1) * rows, :]


def feed_kernel(
    core_ref,
    attended,
    attended_t,
    one,
    two,
    cot_one,
    cot_two,
    mod,
    gain_ref,
    w_out,
    w_up,
    w_down,
    out_one,
    out_two,
    d_attended,
    d_middle_out,
    sums,
    out_grad,
    *rest,
):
    projected, middle, norm, norm_t, d_down, d_down_t, down, d_norm, held = rest[-9:]
    grads = rest[:-9]
    count = len(grads) // 2
    up_grad, down_grad = grads[:count], grads[count:]
    step = pl.program_id(0)
    last = pl.num_programs(0) - 1
    core = core_ref[0]
    part = one.shape[0]
    gate_one, shift, scale, gate_two = (mod[index : index + 1, :] for index in (2, 3, 4, 5))
    gain = gain_ref[...].astype(F32)

    @pl.when(step == 0)
    def begin():
        projected[...] = dot(attended[...], w_out[...])
        for index, (ref, cot) in enumerate(((one, cot_one), (two, cot_two))):
            rows = slice(index * part, (index + 1) * part)
            middle[rows, :] = ref[...].astype(F32) + gate_one * projected[rows, :]
            d_down[rows, :] = (cot[...].astype(F32) * gate_two).astype(BF16)
        xhat, unused = normalize(middle[...])
        norm[...] = (xhat * gain * (1.0 + scale) + shift).astype(BF16)
        norm_t[...] = norm[...].T
        d_down_t[...] = d_down[...].T

    @pl.when(step < last)
    def layer():
        up = dot(norm[...], w_up[...])
        activated, slope = gelu_both(up)
        activated = activated.astype(BF16)
        d_up = (ndot(d_down[...], w_down[...]) * slope).astype(BF16)
        down_step = dot(activated, w_down[...])
        norm_step = ndot(d_up, w_up[...])

        @pl.when(step == 0)
        def assign():
            down[...] = down_step
            d_norm[...] = norm_step

        @pl.when(step > 0)
        def add():
            down[...] += down_step
            d_norm[...] += norm_step

        store_rows(dot(norm_t[...], d_up), up_grad, held, core)
        store_columns(dot(d_down_t[...], activated), down_grad, core)

    @pl.when(step == last)
    def end():
        xhat, inverse_std = normalize(middle[...])
        grad = d_norm[...]
        back = normalize_back(grad * (gain * (1.0 + scale)), xhat, inverse_std)
        gate_sum = jnp.zeros_like(gate_two)
        for index, (cot, out) in enumerate(((cot_one, out_one), (cot_two, out_two))):
            rows = slice(index * part, (index + 1) * part)
            d_result = cot[...].astype(F32)
            out[...] = (middle[rows, :] + gate_two * down[rows, :]).astype(BF16)
            gate_sum += jnp.sum(d_result * down[rows, :], axis=0, keepdims=True)
            d_middle_out[rows, :] = d_result + back[rows, :]
        d_middle = d_middle_out[...]
        d_projected = (d_middle * gate_one).astype(BF16)
        both = jnp.sum(grad * xhat, axis=0, keepdims=True)
        sums[0:1, :] = jnp.sum(d_middle * projected[...], axis=0, keepdims=True)
        sums[1:2, :] = jnp.sum(grad, axis=0, keepdims=True)
        sums[2:3, :] = both * gain
        sums[3:4, :] = gate_sum
        sums[4:5, :] = both * (1.0 + scale)
        sums[5:8, :] = jnp.zeros((3, sums.shape[1]), F32)
        d_attended[...] = ndot(d_projected, w_out[...]).astype(BF16)
        out_grad[...] = dot(attended_t[...], d_projected).astype(BF16)


def grad_rows(steps, width, wide, split):
    at = lambda i: jnp.minimum(i, steps - 1)
    half, rows = wide // 2, width // wide
    if not split:
        return [pl.BlockSpec((1, width, width), lambda i: (at(i), 0, 0))], [shape_of((steps, width, width), BF16)]
    spec = pl.BlockSpec((1, half, rows, width), lambda i: (at(i), 0, 0, 0))
    return [spec] * 2, [shape_of((steps, half, rows, width), BF16)] * 2


def grad_columns(steps, width, narrow, split):
    at = lambda i: jnp.minimum(i, steps - 1)
    if not split:
        return [pl.BlockSpec((1, width, width), lambda i: (at(i), 0, 0))], [shape_of((steps, width, width), BF16)]
    rows = width // narrow // 2
    spec = pl.BlockSpec((narrow, 1, rows, width), lambda i: (0, at(i), 0, 0))
    return [spec] * 2, [shape_of((narrow, steps, rows, width), BF16)] * 2


def feed(core, attended, attended_t, one, two, cot_one, cot_two, mod, gain, w_out, w_up, w_down, wide, narrow, split):
    tokens, width = attended.shape
    part = tokens // 2
    hidden = w_up.shape[1]
    steps = hidden // width
    half, rows = (wide // 2, width // wide) if split else (1, 16)
    up_specs, up_shapes = grad_rows(steps, width, wide, split)
    down_specs, down_shapes = grad_columns(steps, width, narrow, split)
    small = whole((part, width))
    full = whole((tokens, width))
    return pl.pallas_call(
        feed_kernel,
        grid=(steps + 1,),
        in_specs=[
            pl.BlockSpec(memory_space=pltpu.SMEM),
            full,
            whole((width, tokens)),
            small,
            small,
            small,
            small,
            whole(mod.shape),
            whole((1, width)),
            whole((width, width)),
            pl.BlockSpec((width, width), lambda i: (0, jnp.minimum(i, steps - 1))),
            pl.BlockSpec((width, width), lambda i: (jnp.minimum(i, steps - 1), 0)),
        ],
        out_specs=[small, small, full, full, whole((8, width)), whole((width, width))]
        + up_specs
        + down_specs,
        out_shape=[
            shape_of((part, width), BF16),
            shape_of((part, width), BF16),
            shape_of((tokens, width), BF16),
            shape_of((tokens, width), F32),
            shape_of((8, width), F32),
            shape_of((width, width), BF16),
        ]
        + up_shapes
        + down_shapes,
        scratch_shapes=[
            pltpu.VMEM((tokens, width), F32),
            pltpu.VMEM((tokens, width), F32),
            pltpu.VMEM((tokens, width), BF16),
            pltpu.VMEM((width, tokens), BF16),
            pltpu.VMEM((tokens, width), BF16),
            pltpu.VMEM((width, tokens), BF16),
            pltpu.VMEM((tokens, width), F32),
            pltpu.VMEM((tokens, width), F32),
            pltpu.VMEM((half, 2, rows, width), BF16),
        ],
        compiler_params=params(44),
        cost_estimate=LIGHT,
        name="feed",
    )(core, attended, attended_t, one, two, cot_one, cot_two, mod, gain, w_out, w_up, w_down)


def project_back_kernel(groups, parts, core_ref, *refs):
    dq, d_own, received = refs[:groups], refs[groups : 2 * groups], refs[2 * groups : 3 * groups]
    refs_in = refs[3 * groups : 3 * groups + 13]
    norm_t, one, two, mod, gain_ref, weight, cosine, sine, d_middle, early, ada, about, out_grad = refs_in
    out_one, out_two, share = refs[3 * groups + 13 : 3 * groups + 16]
    grads = refs[3 * groups + 16 : -10]
    d_part, d_norm, whole_grad, held = refs[-10:-6]
    step = pl.program_id(0)
    late, done = refs[-6:-1], refs[-1]
    copies = [
        pltpu.make_async_copy(source, target, done.at[index])
        for index, (source, target) in enumerate(zip((one, two, d_middle, ada, out_grad), late))
    ]

    @pl.when(step == 0)
    def fetch():
        for copy in copies:
            copy.start()

    one, two, d_middle, ada, out_grad = late
    part = one.shape[0]
    lanes = dq[0].shape[1]

    @pl.when(step == 0)
    def query():
        value = jnp.concatenate([ref[...] for ref in dq], axis=1).astype(F32)
        d_part[...] = rotate(value, cosine[...], -sine[...]).astype(BF16)

    @pl.when(step > 0)
    def other():
        for group in range(groups):
            total = d_own[group][0] + received[group][0].astype(F32)
            d_part[:, group * lanes : (group + 1) * lanes] = total.astype(BF16)

    @pl.when(step == 1)
    def key():
        d_part[...] = rotate(d_part[...].astype(F32), cosine[...], -sine[...]).astype(BF16)

    norm_step = ndot(d_part[...], weight[...])
    gradient = dot(norm_t[...], d_part[...]).astype(BF16)
    width = gradient.shape[1]
    if len(grads) == 1:
        grads[0][0] = gradient
    else:
        for index in range(3):

            @pl.when(step == index)
            def keep_gradient(index=index):
                whole_grad[:, index * width : (index + 1) * width] = gradient

    @pl.when(step == 0)
    def assign():
        d_norm[...] = norm_step

    @pl.when(step > 0)
    def add():
        d_norm[...] += norm_step

    @pl.when(step == 2)
    def end():
        for copy in copies:
            copy.wait()
        gain = gain_ref[...].astype(F32)
        scale = mod[1:2, :]
        plain = jnp.zeros_like(gain)
        both = jnp.zeros_like(gain)
        for index, (ref, out) in enumerate(((one, out_one), (two, out_two))):
            rows = slice(index * part, (index + 1) * part)
            xhat, inverse_std = normalize(ref[...].astype(F32))
            grad = d_norm[rows, :]
            back = normalize_back(grad * (gain * (1.0 + scale)), xhat, inverse_std)
            out[...] = (d_middle[rows, :] + back).astype(BF16)
            plain += jnp.sum(grad, axis=0, keepdims=True)
            both += jnp.sum(grad * xhat, axis=0, keepdims=True)
        share[0:1, :] = plain
        share[1:2, :] = both * gain
        share[2:7, :] = early[0:5, :]
        share[7:8, :] = both * (1.0 + scale)

        if len(grads) == 1:
            return
        core = core_ref[0]
        half, rows = held.shape[0], held.shape[2]
        blocks = 2 * half
        count = 3 * width // parts
        rest = width // parts
        for index in range(parts):
            for block in range(blocks):
                at = slice(block * rows, (block + 1) * rows)
                held[block // 2, block % 2, :, :count] = whole_grad[at, index * count : (index + 1) * count]
                held[block // 2, block % 2, :, count:] = out_grad[at, index * rest : (index + 1) * rest]
            grads[0][index] = held[:, core]
            grads[1][index] = held[:, 1 - core]
        flat = jnp.concatenate([share[index : index + 1, :] for index in range(6)], axis=1)
        depth = ada.shape[0]
        d_condition = jnp.sum(ada[...].astype(F32) * flat, axis=1, keepdims=True)
        embedded = about[:, :depth]
        gate = 1.0 / (1.0 + jnp.exp(-embedded))
        square = jnp.where(
            lax.broadcasted_iota(jnp.int32, (depth, depth), 0)
            == lax.broadcasted_iota(jnp.int32, (depth, depth), 1),
            d_condition,
            0.0,
        )
        d_embedded = jnp.sum(square, axis=0, keepdims=True) * gate * (1.0 + embedded * (1.0 - gate))
        count = flat.shape[1] // blocks
        place = lax.broadcasted_iota(jnp.int32, (EXTRA, width), 0)
        told_rest = width - about.shape[1] - 2 * rows
        for block in range(blocks):
            row = jnp.concatenate(
                [
                    flat[:, block * count : (block + 1) * count],
                    d_embedded,
                    jnp.zeros((1, width - count - depth), F32),
                ],
                axis=1,
            )
            told = jnp.concatenate(
                [
                    about[...],
                    share[7:8, block * rows : (block + 1) * rows],
                    share[6:7, block * rows : (block + 1) * rows],
                    jnp.zeros((1, told_rest), F32),
                ],
                axis=1,
            )
            mine = core_ref[1]
            value = jnp.where(place == mine, row, 0.0) + jnp.where(place == mine + blocks, told, 0.0)
            held[block // 2, block % 2, :EXTRA, :] = value.astype(BF16)
        grads[0][parts] = held[:, core]
        grads[1][parts] = held[:, 1 - core]


def project_back(
    core, dq, d_own, received, norm_t, one, two, mod, gain, weight, cosine, sine, d_middle, early, ada, about, out_grad, wide, narrow, split
):
    groups = len(dq)
    tokens, lanes = dq[0].shape
    width = groups * lanes
    part = tokens // 2
    small = whole((part, width))
    away = pl.BlockSpec(memory_space=pl.ANY)
    later = pl.BlockSpec((1, tokens, lanes), lambda i: (jnp.maximum(i - 1, 0), 0, 0))
    if split:
        half, rows = wide // 2, width // wide
        shape = (narrow + 1, half, rows, width)
        specs, shapes = [whole(shape)] * 2, [shape_of(shape, BF16)] * 2
        scratch = [pltpu.VMEM((width, 3 * width), BF16), pltpu.VMEM((half, 2, rows, width), BF16)]
    else:
        specs, shapes = grad_rows(3, width, wide, split)
        scratch = [pltpu.VMEM((16, 128), BF16)] * 2
    return pl.pallas_call(
        functools.partial(project_back_kernel, groups, narrow),
        grid=(3,),
        in_specs=[pl.BlockSpec(memory_space=pltpu.SMEM)]
        + [whole((tokens, lanes))] * groups
        + [later] * (2 * groups)
        + [
            whole((width, tokens)),
            away,
            away,
            whole(mod.shape),
            whole((1, width)),
            pl.BlockSpec((width, width), lambda i: (0, i)),
            whole(cosine.shape),
            whole(sine.shape),
            away,
            whole(early.shape),
            away,
            whole(about.shape),
            away,
        ],
        out_specs=[small, small, whole((8, width))] + specs,
        out_shape=[
            shape_of((part, width), BF16),
            shape_of((part, width), BF16),
            shape_of((8, width), F32),
        ]
        + shapes,
        scratch_shapes=[
            pltpu.VMEM((tokens, width), BF16),
            pltpu.VMEM((tokens, width), F32),
        ]
        + scratch
        + [pltpu.VMEM(array.shape, array.dtype) for array in (one, two, d_middle, ada, out_grad)]
        + [pltpu.SemaphoreType.DMA((5,))],
        compiler_params=params(60),
        cost_estimate=LIGHT,
        name="project_back",
    )(core, *dq, *d_own, *received, norm_t, one, two, mod, gain, weight, cosine, sine, d_middle, early, ada, about, out_grad)


def add(target, to, keep, received, at):
    target[to] = keep[at] + received[at]


def halve(kind, words, keep, received, stay, leave):
    entries, blocks = keep.shape[:2]
    if kind == "near":
        n = words[2]
        for target, index in ((stay, n), (leave, n ^ 1)):
            for entry in range(entries // 4 * 2):
                at = entry // 2 * 4 + (index if entry % 2 == 0 else 3 - index)
                for block in range(blocks):
                    add(target, (entry, block), keep, received, (at, block))
        if entries % 4:
            for block in range(blocks):
                total = keep[entries - 1, block] + received[entries - 1, block]
                stay[entries // 4 * 2, block] = total
                leave[entries // 4 * 2, block] = total
        return
    bit = words[0 if kind == "x" else 1]
    for target, mine in ((stay, bit), (leave, 1 - bit)):
        for entry in range(entries):
            for block in range(blocks // 2):
                if blocks == 2:
                    at = mine
                elif kind == "x":
                    at = 2 * block + mine
                else:
                    at = 2 * mine + block
                add(target, (entry, block), keep, received, (entry, at))


def first_kernel(count, words, *refs):
    pairs_in = [(refs[2 * index], refs[2 * index + 1]) for index in range(count)]
    a_stay, a_leave, b_stay, b_leave, c_stay, c_leave = refs[2 * count :]
    step = pl.program_id(0)
    y, x = step // 2, step % 2
    n = words[2]

    def third(target, part, extra):
        entry = 0
        for keep, received in pairs_in:
            for index in range(keep.shape[0] if extra else keep.shape[0] // 4 * 4):
                rows = slice(part * THIRD, (part + 1) * THIRD)
                target[entry, 0] = keep[index, 0, rows, :] + received[index, 0, rows, :]
                entry += 1

    for target, match in ((a_stay, x == words[0]), (a_leave, x != words[0])):
        pl.when(match)(functools.partial(third, target, 0, True))
    for target, match in ((b_stay, y == words[1]), (b_leave, y != words[1])):
        pl.when(match)(functools.partial(third, target, 1, False))
    rows = slice(2 * THIRD, 3 * THIRD)
    for target, index in ((c_stay, n), (c_leave, n ^ 1)):
        for item, (keep, received) in enumerate(pairs_in):
            target[2 * item, 0] = keep[index, 0, rows, :] + received[index, 0, rows, :]
            target[2 * item + 1, 0] = keep[3 - index, 0, rows, :] + received[3 - index, 0, rows, :]


def first_stage(name, words, items):
    count = len(items)
    width = items[0][0].shape[3]
    entries = sum(keep.shape[0] for keep, unused in items)
    blocks_a = (entries, 2, THIRD, width)
    blocks_b = (4 * count, 2, THIRD, width)
    blocks_c = (2 * count, 4, THIRD, width)

    def spec(shape, index):
        return pl.BlockSpec((shape[0], 1, THIRD, width), index)

    def by_y(i, words):
        return (0, i // 2, 0, 0)

    def stay_x(i, words):
        return (0, jnp.clip(i - 2 * words[1], 0, 1), 0, 0)

    def leave_x(i, words):
        return (0, jnp.clip(i - 2 * (1 - words[1]), 0, 1), 0, 0)

    def each(i, words):
        return (0, i, 0, 0)

    in_specs, operands = [], []
    for keep, received in items:
        block = (keep.shape[0], 1) + keep.shape[2:]
        in_specs += [pl.BlockSpec(block, each)] * 2
        operands += [keep, received]
    return pl.pallas_call(
        functools.partial(first_kernel, count),
        grid_spec=pltpu.PrefetchScalarGridSpec(
            num_scalar_prefetch=1,
            grid=(4,),
            in_specs=in_specs,
            out_specs=[
                spec(blocks_a, by_y),
                spec(blocks_a, by_y),
                spec(blocks_b, stay_x),
                spec(blocks_b, leave_x),
                spec(blocks_c, each),
                spec(blocks_c, each),
            ],
        ),
        out_shape=[shape_of(shape, BF16) for shape in (blocks_a, blocks_b, blocks_c) for unused in range(2)],
        compiler_params=params(16),
        cost_estimate=LIGHT,
        name=name,
    )(words, *operands)


def call(kernel, name, shapes, operands, scratch=(), estimate=None):
    vmem = pl.BlockSpec(memory_space=pltpu.VMEM)
    return pl.pallas_call(
        kernel,
        in_specs=[pl.BlockSpec(memory_space=pltpu.SMEM)] + [vmem] * (len(operands) - 1),
        out_specs=[vmem] * len(shapes),
        out_shape=shapes,
        scratch_shapes=list(scratch),
        compiler_params=params(16),
        cost_estimate=estimate or LIGHT,
        name=name,
    )(*operands)


def next_kernel(kinds, words, *refs):
    for index, kind in enumerate(kinds):
        keep, received = refs[2 * index], refs[2 * index + 1]
        stay, leave = refs[2 * len(kinds) + 2 * index], refs[2 * len(kinds) + 2 * index + 1]
        halve(kind, words, keep, received, stay, leave)


def next_stage(name, kinds, words, kept, got, estimate=None):
    shapes, operands = [], [words]
    for kind, keep, received in zip(kinds, kept, got):
        entries, blocks, rows, columns = keep.shape
        if kind == "near":
            shape = (entries // 4 * 2 + entries % 4, blocks, rows, columns)
        else:
            shape = (entries, blocks // 2, rows, columns)
        shapes += [shape_of(shape, BF16)] * 2
        operands += [keep, received]
    outs = call(functools.partial(next_kernel, kinds), name, shapes, operands, estimate=estimate)
    return outs[::2], outs[1::2]


def far_kernel(words, *refs):
    keeps, gots, (stay, leave, *held) = refs[:3], refs[3:6], refs[6:]
    for third, (keep, received) in enumerate(zip(keeps, gots)):
        rows = slice(third * THIRD, (third + 1) * THIRD)
        for item in range(keep.shape[0] // 2):
            stay[item, rows, :] = keep[2 * item, 0].astype(F32) + received[2 * item, 0].astype(F32)
            leave[item, rows, :] = keep[2 * item + 1, 0] + received[2 * item + 1, 0]
    if held:
        for index, ref in enumerate((keeps[0], gots[0])):
            rows = slice(3 * THIRD + index * SMALL, 3 * THIRD + (index + 1) * SMALL)
            leave[0, rows, :] = ref[2, 0, :SMALL, :]
            held[0][index * SMALL : (index + 1) * SMALL, :] = ref[2, 0, :SMALL, :]


def far_stage(name, words, kept, got):
    count = kept[1].shape[0] // 2
    width = kept[0].shape[3]
    extra = kept[0].shape[0] % 2
    rows = 3 * THIRD
    shapes = [
        shape_of((count, rows, width), F32),
        shape_of((count, rows + extra * 2 * SMALL, width), BF16),
    ]
    if extra:
        shapes.append(shape_of((2 * SMALL, width), BF16))
    return call(far_kernel, name, shapes, (words, *kept, *got))


def end_kernel(words, keep, received, up, down):
    up[...] = keep[0] + received[0].astype(F32)
    total = keep[1] + received[1].astype(F32)
    rows, columns = total.shape
    down[:, :rows] = total[:, : columns // 2].T
    down[:, rows:] = total[:, columns // 2 :].T


def last_kernel(words, own, got, held, qkv, out, ada, table, gain_one, gain_two, mods, about, wide):
    n, w = words[2], words[3]
    rows, first = qkv.shape
    total = own[0] + got[0, :rows, :].astype(F32)
    qkv[...] = total[:, :first]
    out[...] = total[:, first:]
    slots = mods.shape[0] // 4
    count = ada.shape[1]
    depth = wide.shape[0]
    part = ada.shape[0]
    for index in range(4):
        ref, at = (held, index * SMALL) if index < 2 else (got.at[0], rows + (index - 2) * SMALL)
        value = ref[at : at + 2 * slots, :].astype(F32)
        mods[index * slots : (index + 1) * slots, :] = value[:slots, :]
        about[index * slots : (index + 1) * slots, :] = value[slots:, :]
    gains = jnp.sum(about[:, 3 * depth : 3 * depth + 2 * rows], axis=0, keepdims=True)
    gain_one[...] = gains[:, :rows]
    gain_two[...] = gains[:, rows : 2 * rows]
    embedded = about[:, :depth]
    condition = (embedded / (1.0 + jnp.exp(-embedded))).astype(BF16)
    turned = (((0,), (0,)), ((), ()))
    wide[...] = lax.dot_general(
        condition, mods[:, :count].astype(BF16), turned, preferred_element_type=F32
    )
    ada[...] = wide[pl.ds(n * part, part), :]
    time = about[:, depth : depth + 1] * 32.0 + about[:, depth + 1 : depth + 2]
    times = table.shape[0]
    lane = lax.broadcasted_iota(jnp.int32, (mods.shape[0], times), 1) + w * times
    onehot = jnp.where(time.astype(jnp.int32) == lane, 1.0, 0.0).astype(BF16)
    grad = lax.dot_general(
        onehot, mods[:, count : count + depth].astype(BF16), turned, preferred_element_type=F32
    )
    value = grad[:, :part]
    for index in range(1, depth // part):
        value = jnp.where(n == index, grad[:, index * part : (index + 1) * part], value)
    table[...] = value


def last(words, own, got, held, qkv_shape, out_shape, ada_shape, table_shape, depth, wide):
    rows = qkv_shape[0]
    width = own.shape[2]
    return call(
        last_kernel,
        "last",
        [shape_of(qkv_shape, F32), shape_of(out_shape, F32), shape_of(ada_shape, F32), shape_of(table_shape, F32)]
        + [shape_of((1, rows), F32)] * 2,
        (words, own, got, held),
        [
            pltpu.VMEM((4 * wide, width), F32),
            pltpu.VMEM((4 * wide, width), F32),
            pltpu.VMEM((depth, ada_shape[1]), F32),
        ],
    )


def make(wide, narrow):
    wide_bits = wide.bit_length() - 1

    def first_message(w, n):
        p, c = w // 2, w % 2
        return 2 * p + n // 2, 2 * c + n % 2

    def second_message(w, n):
        p, c = w // 2, w % 2
        return 2 * p + n // 2, 2 * c + 1 - n % 2

    message_one = pairs(wide, narrow, first_message)
    message_two = pairs(wide, narrow, second_message)
    flip = [pairs(wide, narrow, lambda w, n, b=b: (w ^ (1 << b), n)) for b in range(wide_bits)]
    line = [pairs(wide, narrow, lambda w, n, m=m: (w, n ^ m)) for m in range(1, narrow)]
    split = wide == 8

    def on_device(
        hidden_in,
        positions,
        time_index,
        cond_table,
        ada_weight,
        norm1_gain,
        qkv_weight,
        out_weight,
        norm2_gain,
        up_weight,
        down_weight,
        cotangent,
    ):
        w = lax.axis_index("wide")
        n = lax.axis_index("narrow")
        core = w % 2
        core_word = jnp.stack([core, w]).astype(jnp.int32)
        words = jnp.stack([(w >> 1) & 1, (w >> 2) & 1, n, w]).astype(jnp.int32)
        width = hidden_in.shape[2]
        odd = n % 2

        def take(array, index):
            return lax.dynamic_index_in_dim(array, index, axis=0, keepdims=False)

        def spread(array):
            one = lax.ppermute(take(array, odd), AXES, message_one)
            two = lax.ppermute(take(array, 1 - odd), AXES, message_two)
            return one, two

        def permute(array, table):
            return lax.ppermute(array, AXES, table)

        def across(sends):
            return [permute(send, line[index]) for index, send in enumerate(sends)]

        def reduce_blocks(current):
            for bit in range(wide_bits):
                mine = (w >> bit) & 1
                current = current.reshape((-1, 2) + current.shape[1:])
                send = lax.dynamic_index_in_dim(current, 1 - mine, axis=1, keepdims=False)
                keep = lax.dynamic_index_in_dim(current, mine, axis=1, keepdims=False)
                received = permute(send, flip[bit])
                current = (keep.astype(F32) + received.astype(F32)).astype(BF16)
            current = current[0]
            total = take(current, n).astype(F32)
            for mask in range(1, narrow):
                total += permute(take(current, n ^ mask), line[mask - 1]).astype(F32)
            return total

        wait = lax.optimization_barrier
        hidden_one, hidden_two = spread(hidden_in)
        other_time = permute(time_index, flip[0])
        positions, other_time = wait((positions, other_time))
        place_one, place_two = spread(positions)
        row_time = jnp.where(n // 2 == core, time_index[n % 2], other_time[n % 2])
        embedded = lax.dynamic_slice_in_dim(cond_table, row_time, 1, axis=0).astype(F32)
        condition = (embedded * jax.nn.sigmoid(embedded)).astype(BF16)
        modulation = dot(condition, ada_weight).reshape(6, width)
        mod = jnp.concatenate([modulation, jnp.zeros((2, width), F32)])
        gain_one = norm1_gain.reshape(1, width)
        gain_two = norm2_gain.reshape(1, width)
        depth = cond_table.shape[1]
        pair = jnp.stack([row_time // 32, row_time % 32]).astype(F32).reshape(1, 2)
        about = jnp.concatenate(
            [embedded, pair, jnp.zeros((1, 2 * depth - 2), F32)], axis=1
        )

        place = jnp.concatenate([place_one, place_two]).astype(F32)
        lane = jnp.arange(128, dtype=jnp.int32)
        frequency = 10000.0 ** (-(lane % HALF).astype(F32) / HALF)
        angles = place[:, None] * frequency
        cosine = jnp.cos(angles)
        sine = jnp.sin(angles) * jnp.where(lane % HEAD_DIM < HALF, -1.0, 1.0)

        hidden_one, hidden_two, cotangent = wait((hidden_one, hidden_two, cotangent))
        cot_one, cot_two = spread(cotangent)
        q, kv, norm_t = project(hidden_one, hidden_two, mod, gain_one, qkv_weight, cosine, sine)
        kv_other = permute(kv, flip[0])
        attended, attended_t, log_total = attend(q, kv, kv_other)
        out_one, out_two, d_attended, d_middle, sums_two, out_grad, *grads = feed(
            core_word,
            attended,
            attended_t,
            hidden_one,
            hidden_two,
            cot_one,
            cot_two,
            mod,
            gain_two,
            out_weight,
            up_weight,
            down_weight,
            wide,
            narrow,
            split,
        )
        grads_feed = grads
        dq, d_own, received = [], [], []

        def back_group(group, q):
            first, second, third = attend_back(q, kv, kv_other, d_attended, attended_t, log_total, group)
            dq.append(first)
            d_own.append(second)
            received.append(permute(third, flip[0]))

        rows = width // wide
        if split:
            axes = {"x": flip[1], "y": flip[2], "near": line[0], "far": line[2]}

            def exchange(kinds, sends):
                return [permute(send, axes[kind]) for kind, send in zip(kinds, sends)]

            turns = [("x", "y", "near"), ("y", "near", "x"), ("near", "x", "y")]
            up_keep, up_send, down_keep, down_send = grads
            down_got = permute(down_send, flip[0])
            up_got = permute(up_send, flip[0])
            back_group(0, q)
            d_own[0], up_got, down_got = wait((d_own[0], up_got, down_got))
            stages = first_stage("first_feed", words, [(up_keep, up_got), (down_keep, down_got)])
            kept, sends = stages[::2], stages[1::2]
            got = exchange(turns[0], sends)
            out_one, out_two, q, *sends = wait((out_one, out_two, q, *sends))
            out_one = permute(out_one, inverse(message_one))
            back_group(1, q)
            q, d_own[1], received[0] = wait((q, d_own[1], received[0]))
            back_group(2, q)
            dq[2], received[1], out_one, out_two, *got = wait((dq[2], received[1], out_one, out_two, *got))
            out_two = permute(out_two, inverse(message_two))
            kept, sends = next_stage("second_feed", turns[1], words, kept, got)
            got = exchange(turns[1], sends)
            dq[0], *sends = wait((dq[0], *sends))
        else:
            out_one = permute(out_one, inverse(message_one))
            out_two = permute(out_two, inverse(message_two))
            for group in range(width // (GROUP * HEAD_DIM)):
                back_group(group, q)

        grad_one, grad_two, share, *grads = project_back(
            core_word,
            dq,
            d_own,
            received,
            norm_t,
            hidden_one,
            hidden_two,
            mod,
            gain_one,
            qkv_weight,
            cosine,
            sine,
            d_middle,
            sums_two,
            ada_weight,
            about,
            out_grad,
            wide,
            narrow,
            split,
        )

        def join(one, two):
            return jnp.stack([jnp.where(odd == 0, one, two), jnp.where(odd == 0, two, one)])

        row_count = depth // narrow
        column_count = 6 * width // wide
        time_count = cond_table.shape[0] // wide
        if split:
            qkv_keep, qkv_send = grads
            qkv_got = permute(qkv_send, flip[0])
            out_two, grad_first = wait((out_two, grad_one))
            grad_one = permute(grad_one, inverse(message_one))
            grad_first, out_two, *got = wait((grad_first, out_two, *got))
            kept, sends = next_stage("third_feed", turns[2], words, kept, got, HEAVY)
            got = exchange(turns[2], sends)
            qkv_got, *sends = wait((qkv_got, *sends))
            stages = first_stage("first_qkv", words, [(qkv_keep, qkv_got)])
            kept_qkv, sends = stages[::2], stages[1::2]
            grad_one, grad_two, got[0], got[1], got[2], *sends = wait((grad_one, grad_two, *got, *sends))
            got_qkv = exchange(turns[0], sends)
            *got, sends[0] = wait((*got, sends[0]))
            own, send = far_stage("far_feed", words, kept, got)
            far_got = permute(send, axes["far"])
            *got_qkv, send = wait((*got_qkv, send))
            kept_qkv, sends = next_stage("second_qkv", turns[1], words, kept_qkv, got_qkv)
            got_qkv = exchange(turns[1], sends)
            far_got, grad_two, *sends = wait((far_got, grad_two, *sends))
            grad_two = permute(grad_two, inverse(message_two))
            grad_up, grad_down = call(
                end_kernel,
                "end_feed",
                [shape_of((rows, width), F32), shape_of((width // 2, width // narrow), F32)],
                (words, own, far_got),
            )
            *got_qkv, grad_up = wait((*got_qkv, grad_up))
            kept_qkv, sends = next_stage("third_qkv", turns[2], words, kept_qkv, got_qkv)
            got_qkv = exchange(turns[2], sends)
            own, send, held = far_stage("far_qkv", words, kept_qkv, got_qkv)
            far_got = permute(send, axes["far"])
            grad_one, grad_two, send = wait((grad_one, grad_two, send))
            hidden_grad = join(grad_one, grad_two)
            far_got, hidden_grad = wait((far_got, hidden_grad))
            grad_qkv, grad_out, grad_ada, grad_table, grad_gain_one, grad_gain_two = last(
                words,
                own,
                far_got,
                held,
                (rows, 3 * width // narrow),
                (rows, width // narrow),
                (row_count, column_count),
                (time_count, row_count),
                depth,
                wide,
            )
            gains = grad_gain_two.reshape(rows), grad_gain_one.reshape(rows)
        else:
            up_grad, down_grad = grads_feed
            (qkv_grad,) = grads
            grad_one = permute(grad_one, inverse(message_one))
            grad_two = permute(grad_two, inverse(message_two))
            hidden_grad = join(grad_one, grad_two)
            steps = down_grad.shape[0]
            grad_up = reduce_blocks(up_grad.reshape(narrow, wide, rows, width).transpose(1, 0, 2, 3))
            grad_down = reduce_blocks(
                down_grad.reshape(steps, narrow, width // narrow, wide // steps, -1)
                .transpose(0, 3, 1, 2, 4)
                .reshape(wide, narrow, width // narrow, -1)
            ).T

            def by_rows(grad):
                return reduce_blocks(
                    grad.transpose(1, 0, 2).reshape(wide, rows, narrow, -1).transpose(0, 2, 1, 3)
                )

            grad_out = by_rows(out_grad[None])
            grad_qkv = by_rows(qkv_grad)
            told = jnp.concatenate(
                [embedded, jnp.broadcast_to(row_time.astype(F32), (1, width - depth))], axis=1
            )
            share = jnp.concatenate([share, told])[None]
            for table in flip + [line[0], line[2]]:
                share = jnp.concatenate([share, permute(share, table)])
            all_mod = share[:, :6].reshape(-1, 6 * width)
            gains = jnp.sum(share[:, 6:8].reshape(-1, 2, wide, rows), axis=0)
            gains = lax.dynamic_index_in_dim(gains, w, axis=1, keepdims=False)
            my_embedded = lax.dynamic_slice_in_dim(share[:, 8, :depth], n * row_count, row_count, axis=1)
            times = share[:, 8, depth].astype(jnp.int32)
            my_gate = jax.nn.sigmoid(my_embedded)
            my_conditions = (my_embedded * my_gate).astype(BF16).astype(F32)
            my_mod = lax.dynamic_slice_in_dim(all_mod, w * column_count, column_count, axis=1)
            grad_ada = lax.dot_general(
                my_conditions,
                my_mod,
                (((0,), (0,)), ((), ())),
                precision=HIGHEST,
                preferred_element_type=F32,
            )
            my_ada = lax.dynamic_slice_in_dim(ada_weight, n * row_count, row_count, axis=0).astype(F32)
            d_condition = lax.dot_general(
                all_mod,
                my_ada,
                (((1,), (1,)), ((), ())),
                precision=HIGHEST,
                preferred_element_type=F32,
            )
            d_embedded = d_condition * my_gate * (1.0 + my_embedded * (1.0 - my_gate))
            my_times = w * time_count + jnp.arange(time_count, dtype=jnp.int32)
            onehot = (my_times[:, None] == times[None, :]).astype(F32)
            grad_table = jnp.dot(onehot, d_embedded, precision=HIGHEST, preferred_element_type=F32)
        return (
            join(out_one, out_two),
            hidden_grad,
            grad_table,
            grad_ada,
            gains[1],
            grad_qkv,
            grad_out,
            gains[0],
            grad_up,
            grad_down,
        )

    return on_device


def solution(mesh):
    in_specs = (
        P("wide", "narrow", None),
        P("wide", "narrow"),
        P("wide"),
        P(),
        P(),
        P(),
        P(),
        P(),
        P(),
        P(),
        P(),
        P("wide", "narrow", None),
    )
    out_specs = (
        P("wide", "narrow", None),
        P("wide", "narrow", None),
        P("wide", "narrow"),
        P("narrow", "wide"),
        P("wide"),
        P("wide", "narrow"),
        P("wide", "narrow"),
        P("wide"),
        P("wide", "narrow"),
        P("wide", "narrow"),
    )
    return jax.shard_map(
        make(mesh.shape["wide"], mesh.shape["narrow"]),
        mesh=mesh,
        in_specs=in_specs,
        out_specs=out_specs,
        check_vma=False,
    )
```

```python
import functools

import jax
import jax.numpy as jnp
from jax import lax
from jax.experimental import pallas as pl
from jax.experimental.pallas import tpu as pltpu
from jax.sharding import PartitionSpec as P

HEAD_DIM = 64
HALF = HEAD_DIM // 2
GROUP = 4
ONES = 16
LOG2E = 1.4426950408889634
SCALE = HEAD_DIM**-0.5
HIGHEST = lax.Precision.HIGHEST
norm_eps = 1e-05
AXES = ("wide", "narrow")
EXTRA = 32
SMALL = 32
THIRD = 32
F32 = jnp.float32
BF16 = jnp.bfloat16
MIB = 1 << 20


def cost(us):
    return pl.CostEstimate(flops=int(us * 1.15e9), bytes_accessed=int(us * 3.7e6), transcendentals=0)


LIGHT = cost(0.01)
HEAVY = cost(100)


def dot(left, right):
    return jnp.dot(left, right, preferred_element_type=F32)


def ndot(left, right):
    return lax.dot_general(left, right, (((1,), (1,)), ((), ())), preferred_element_type=F32)


def pairs(wide, narrow, target):
    result = []
    for w in range(wide):
        for n in range(narrow):
            w_to, n_to = target(w, n)
            result.append((w * narrow + n, w_to * narrow + n_to))
    return result


def inverse(table):
    return [(target, source) for source, target in table]


def normalize(hidden):
    center = hidden - jnp.mean(hidden, axis=-1, keepdims=True)
    variance = jnp.mean(center * center, axis=-1, keepdims=True)
    inverse_std = lax.rsqrt(variance + norm_eps)
    return center * inverse_std, inverse_std


def normalize_back(grad, xhat, inverse_std):
    mean_grad = jnp.mean(grad, axis=-1, keepdims=True)
    mean_both = jnp.mean(grad * xhat, axis=-1, keepdims=True)
    return (grad - mean_grad - xhat * mean_both) * inverse_std


def rotate(values, cosine, sine):
    width = values.shape[1]
    lane = lax.broadcasted_iota(jnp.int32, values.shape, 1)
    ahead = pltpu.roll(values, width - HALF, 1)
    behind = pltpu.roll(values, HALF, 1)
    swapped = jnp.where(lane % HEAD_DIM < HALF, ahead, behind)
    repeat = width // cosine.shape[1]
    cosine = jnp.concatenate([cosine] * repeat, axis=1)
    sine = jnp.concatenate([sine] * repeat, axis=1)
    return values * cosine + swapped * sine


def whole(shape):
    return pl.BlockSpec(shape, lambda *index: (0,) * len(shape))


def params(mib):
    return pltpu.CompilerParams(vmem_limit_bytes=mib * MIB)


def shape_of(shape, dtype):
    return jax.ShapeDtypeStruct(shape, dtype)


def project_kernel(one, two, mod, gain, weight, cosine, sine, q_out, kv_out, norm_t, norm):
    step = pl.program_id(0)
    part = one.shape[0]

    @pl.when(step == 0)
    def first():
        for index, ref in enumerate((one, two)):
            xhat, unused = normalize(ref[...].astype(F32))
            value = xhat * gain[...].astype(F32) * (1.0 + mod[1:2, :]) + mod[0:1, :]
            norm[index * part : (index + 1) * part, :] = value.astype(BF16)
        norm_t[...] = norm[...].T

    result = dot(norm[...], weight[...])

    @pl.when(step == 0)
    def query():
        q_out[...] = (rotate(result, cosine[...], sine[...]).astype(BF16).astype(F32) * SCALE).astype(BF16)

    @pl.when(step == 1)
    def key():
        kv_out[0] = rotate(result, cosine[...], sine[...]).astype(BF16)

    @pl.when(step == 2)
    def value():
        kv_out[0] = result.astype(BF16)


def project(one, two, mod, gain, weight, cosine, sine):
    part, width = one.shape
    tokens = 2 * part
    return pl.pallas_call(
        project_kernel,
        grid=(3,),
        in_specs=[
            whole((part, width)),
            whole((part, width)),
            whole(mod.shape),
            whole((1, width)),
            pl.BlockSpec((width, width), lambda i: (0, i)),
            whole(cosine.shape),
            whole(sine.shape),
        ],
        out_specs=[
            whole((tokens, width)),
            pl.BlockSpec((1, tokens, width), lambda i: (jnp.maximum(i - 1, 0), 0, 0)),
            whole((width, tokens)),
        ],
        out_shape=[
            shape_of((tokens, width), BF16),
            shape_of((2, tokens, width), BF16),
            shape_of((width, tokens), BF16),
        ],
        scratch_shapes=[pltpu.VMEM((tokens, width), BF16)],
        compiler_params=params(28),
        cost_estimate=LIGHT,
        name="project",
    )(one, two, mod, gain, weight, cosine, sine)


def attend_kernel(q, kv, kv_other, out, out_t, log_total, keys, values_t, scores):
    tokens, lanes = q.shape
    keys[:tokens, :] = kv[0]
    keys[tokens:, :] = kv_other[0]
    step = HEAD_DIM + ONES
    turned = kv[1].T, kv_other[1].T
    for head in range(GROUP):
        lane = slice(head * HEAD_DIM, (head + 1) * HEAD_DIM)
        rows = slice(head * step, head * step + HEAD_DIM)
        values_t[rows, :tokens] = turned[0][lane, :]
        values_t[rows, tokens:] = turned[1][lane, :]
        values_t[head * step + HEAD_DIM : (head + 1) * step, :] = jnp.ones((ONES, 2 * tokens), BF16)
    q_t = q[...].T
    row = lax.broadcasted_iota(jnp.int32, q_t.shape, 0) // HEAD_DIM
    log_total[...] = jnp.zeros_like(log_total)

    def score(head):
        scores[head % 2] = dot(keys[...], jnp.where(row == head, q_t, jnp.zeros_like(q_t)))

    score(0)
    for head in range(GROUP):
        if head + 1 < GROUP:
            score(head + 1)
        score_head = scores[head % 2]
        top = jnp.max(score_head, axis=0, keepdims=True)
        expo = jnp.exp2((score_head - top) * LOG2E).astype(BF16)
        rows = slice(head * HEAD_DIM, (head + 1) * HEAD_DIM)
        result = dot(values_t[head * step : (head + 1) * step, :], expo)
        total = result[HEAD_DIM : HEAD_DIM + 1, :]
        out_t[rows, :] = (result[:HEAD_DIM, :] / total).astype(BF16)
        log_total[0, head : head + 1, :] = top + jnp.log(total)
    out[...] = out_t[...].T


def attend(q, kv, kv_other):
    tokens, width = q.shape
    lanes = GROUP * HEAD_DIM
    groups = width // lanes
    pair = pl.BlockSpec((2, tokens, lanes), lambda g: (0, 0, g))
    flat = pl.BlockSpec((tokens, lanes), lambda g: (0, g))
    return pl.pallas_call(
        attend_kernel,
        grid=(groups,),
        in_specs=[flat, pair, pair],
        out_specs=[
            flat,
            pl.BlockSpec((lanes, tokens), lambda g: (g, 0)),
            pl.BlockSpec((1, 8, tokens), lambda g: (g, 0, 0)),
        ],
        out_shape=[
            shape_of((tokens, width), BF16),
            shape_of((width, tokens), BF16),
            shape_of((groups, 8, tokens), F32),
        ],
        scratch_shapes=[
            pltpu.VMEM((2 * tokens, lanes), BF16),
            pltpu.VMEM((lanes + GROUP * ONES, 2 * tokens), BF16),
            pltpu.VMEM((2, 2 * tokens, tokens), F32),
        ],
        compiler_params=params(28),
        cost_estimate=LIGHT,
        name="attend",
    )(q, kv, kv_other)


def attend_back_kernel(
    q, kv, kv_other, d_out, out_t, log_total, dq, d_own, d_other, keys_t, low, grad_low, dq_t, scores, grads
):
    tokens, lanes = q.shape
    chunk = low.shape[0]
    keys_t[:, :tokens] = kv[0].T
    keys_t[:, tokens:] = kv_other[0].T
    q_all = q[...]
    d_all = d_out[...]
    q_t = q_all.T
    d_t = d_all.T
    row = lax.broadcasted_iota(jnp.int32, q_t.shape, 0) // HEAD_DIM
    lane = lax.broadcasted_iota(jnp.int32, q_all.shape, 1) // HEAD_DIM
    product = d_t.astype(F32) * out_t[...].astype(F32)
    q_rows, d_rows = [], []
    for head in range(GROUP):
        q_rows.append(jnp.where(lane == head, q_all, jnp.zeros_like(q_all)))
        d_rows.append(jnp.where(lane == head, d_all, jnp.zeros_like(d_all)))
    q_stack = jnp.concatenate(q_rows, axis=0)
    d_stack = jnp.concatenate(d_rows, axis=0)
    items = [(index, head) for index in range(2 * tokens // chunk) for head in range(GROUP)]

    def products(item):
        index, head = items[item]
        source = kv if index * chunk < tokens else kv_other
        at = index * chunk % tokens
        q_head = jnp.where(row == head, q_t, jnp.zeros_like(q_t))
        d_head = jnp.where(row == head, d_t, jnp.zeros_like(d_t))
        scores[item % 2] = dot(source[0, at : at + chunk, :], q_head)
        grads[item % 2] = dot(source[1, at : at + chunk, :], d_head)

    products(0)
    for item, (index, head) in enumerate(items):
        if item + 1 < len(items):
            products(item + 1)
        rows = slice(head * HEAD_DIM, (head + 1) * HEAD_DIM)
        columns = slice(head * tokens, (head + 1) * tokens)
        center = jnp.sum(product[rows, :], axis=0, keepdims=True)
        offset = log_total[0, head : head + 1, :] * LOG2E
        probs = jnp.exp2(scores[item % 2] * LOG2E - offset)
        low[:, columns] = probs.astype(BF16)
        d_scores = (probs * (grads[item % 2] - center)).astype(BF16)
        grad_low[:, columns] = d_scores
        update = dot(keys_t[rows, index * chunk : (index + 1) * chunk], d_scores)
        if index == 0:
            dq_t[rows, :] = update
        else:
            dq_t[rows, :] += update
        if head < GROUP - 1:
            continue
        at = index * chunk % tokens
        d_keys = dot(grad_low[...], q_stack)
        d_values = dot(low[...], d_stack)
        if index * chunk < tokens:
            d_own[0, at : at + chunk, :] = d_keys
            d_own[1, at : at + chunk, :] = d_values
        else:
            d_other[0, at : at + chunk, :] = d_keys.astype(BF16)
            d_other[1, at : at + chunk, :] = d_values.astype(BF16)
    dq[...] = (dq_t[...] * SCALE).T.astype(BF16)


def attend_back(q, kv, kv_other, d_out, out_t, log_total, group):
    tokens, width = q.shape
    lanes = GROUP * HEAD_DIM
    chunk = min(256, tokens)
    pair = pl.BlockSpec((2, tokens, lanes), lambda g: (0, 0, group))
    flat = pl.BlockSpec((tokens, lanes), lambda g: (0, group))
    pair_out = whole((2, tokens, lanes))
    return pl.pallas_call(
        attend_back_kernel,
        grid=(1,),
        in_specs=[
            flat,
            pair,
            pair,
            flat,
            pl.BlockSpec((lanes, tokens), lambda g: (group, 0)),
            pl.BlockSpec((1, 8, tokens), lambda g: (group, 0, 0)),
        ],
        out_specs=[whole((tokens, lanes)), pair_out, pair_out],
        out_shape=[
            shape_of((tokens, lanes), BF16),
            shape_of((2, tokens, lanes), F32),
            shape_of((2, tokens, lanes), BF16),
        ],
        scratch_shapes=[
            pltpu.VMEM((lanes, 2 * tokens), BF16),
            pltpu.VMEM((chunk, GROUP * tokens), BF16),
            pltpu.VMEM((chunk, GROUP * tokens), BF16),
            pltpu.VMEM((lanes, tokens), F32),
            pltpu.VMEM((2, chunk, tokens), F32),
            pltpu.VMEM((2, chunk, tokens), F32),
        ],
        compiler_params=params(24),
        cost_estimate=LIGHT,
        name="attend_back",
    )(q, kv, kv_other, d_out, out_t, log_total)


def gelu_both(up):
    factor = 0.7978845608028654
    square = up * up
    angle = up * (factor + factor * 0.044715 * square)
    tanh = jnp.tanh(angle)
    half = 0.5 * (1.0 + tanh)
    slope = half + 0.5 * up * (1.0 - tanh * tanh) * (factor + 3.0 * factor * 0.044715 * square)
    return up * half, slope


def store_rows(value, targets, held, core):
    if len(targets) == 1:
        targets[0][0] = value.astype(BF16)
        return
    blocks, rows = held.shape[0] * 2, held.shape[2]
    for block in range(blocks):
        held[block // 2, block % 2] = value[block * rows : (block + 1) * rows, :].astype(BF16)
    targets[0][0] = held[:, core]
    targets[1][0] = held[:, 1 - core]


def store_columns(value, targets, core):
    value = value.astype(BF16)
    if len(targets) == 1:
        targets[0][0] = value
        return
    parts, unused, rows, columns = targets[0].shape
    columns = columns // 2
    first, second = value[:, :columns], value[:, columns:]
    stay = jnp.where(core == 0, first, second)
    leave = jnp.where(core == 0, second, first)
    for target, kept in zip(targets, (stay, leave)):
        for index in range(2 * parts):
            side = slice((index % 2) * columns, (index % 2 + 1) * columns)
            target[index // 2, 0, :, side] = kept[index * rows : (index + 1) * rows, :]


def feed_kernel(
    core_ref,
    attended,
    attended_t,
    one,
    two,
    cot_one,
    cot_two,
    mod,
    gain_ref,
    w_out,
    w_up,
    w_down,
    out_one,
    out_two,
    d_attended,
    d_middle_out,
    sums,
    out_grad,
    *rest,
):
    projected, middle, norm, norm_t, d_down, d_down_t, down, d_norm, held = rest[-9:]
    grads = rest[:-9]
    count = len(grads) // 2
    up_grad, down_grad = grads[:count], grads[count:]
    step = pl.program_id(0)
    last = pl.num_programs(0) - 1
    core = core_ref[0]
    part = one.shape[0]
    gate_one, shift, scale, gate_two = (mod[index : index + 1, :] for index in (2, 3, 4, 5))
    gain = gain_ref[...].astype(F32)

    @pl.when(step == 0)
    def begin():
        projected[...] = dot(attended[...], w_out[...])
        for index, (ref, cot) in enumerate(((one, cot_one), (two, cot_two))):
            rows = slice(index * part, (index + 1) * part)
            middle[rows, :] = ref[...].astype(F32) + gate_one * projected[rows, :]
            d_down[rows, :] = (cot[...].astype(F32) * gate_two).astype(BF16)
        xhat, unused = normalize(middle[...])
        norm[...] = (xhat * gain * (1.0 + scale) + shift).astype(BF16)
        norm_t[...] = norm[...].T
        d_down_t[...] = d_down[...].T

    @pl.when(step < last)
    def layer():
        up = dot(norm[...], w_up[...])
        activated, slope = gelu_both(up)
        activated = activated.astype(BF16)
        d_up = (ndot(d_down[...], w_down[...]) * slope).astype(BF16)
        down_step = dot(activated, w_down[...])
        norm_step = ndot(d_up, w_up[...])

        @pl.when(step == 0)
        def assign():
            down[...] = down_step
            d_norm[...] = norm_step

        @pl.when(step > 0)
        def add():
            down[...] += down_step
            d_norm[...] += norm_step

        store_rows(dot(norm_t[...], d_up), up_grad, held, core)
        store_columns(dot(d_down_t[...], activated), down_grad, core)

    @pl.when(step == last)
    def end():
        xhat, inverse_std = normalize(middle[...])
        grad = d_norm[...]
        back = normalize_back(grad * (gain * (1.0 + scale)), xhat, inverse_std)
        gate_sum = jnp.zeros_like(gate_two)
        for index, (cot, out) in enumerate(((cot_one, out_one), (cot_two, out_two))):
            rows = slice(index * part, (index + 1) * part)
            d_result = cot[...].astype(F32)
            out[...] = (middle[rows, :] + gate_two * down[rows, :]).astype(BF16)
            gate_sum += jnp.sum(d_result * down[rows, :], axis=0, keepdims=True)
            d_middle_out[rows, :] = d_result + back[rows, :]
        d_middle = d_middle_out[...]
        d_projected = (d_middle * gate_one).astype(BF16)
        both = jnp.sum(grad * xhat, axis=0, keepdims=True)
        sums[0:1, :] = jnp.sum(d_middle * projected[...], axis=0, keepdims=True)
        sums[1:2, :] = jnp.sum(grad, axis=0, keepdims=True)
        sums[2:3, :] = both * gain
        sums[3:4, :] = gate_sum
        sums[4:5, :] = both * (1.0 + scale)
        sums[5:8, :] = jnp.zeros((3, sums.shape[1]), F32)
        d_attended[...] = ndot(d_projected, w_out[...]).astype(BF16)
        out_grad[...] = dot(attended_t[...], d_projected).astype(BF16)


def grad_rows(steps, width, wide, split):
    at = lambda i: jnp.minimum(i, steps - 1)
    half, rows = wide // 2, width // wide
    if not split:
        return [pl.BlockSpec((1, width, width), lambda i: (at(i), 0, 0))], [shape_of((steps, width, width), BF16)]
    spec = pl.BlockSpec((1, half, rows, width), lambda i: (at(i), 0, 0, 0))
    return [spec] * 2, [shape_of((steps, half, rows, width), BF16)] * 2


def grad_columns(steps, width, narrow, split):
    at = lambda i: jnp.minimum(i, steps - 1)
    if not split:
        return [pl.BlockSpec((1, width, width), lambda i: (at(i), 0, 0))], [shape_of((steps, width, width), BF16)]
    rows = width // narrow // 2
    spec = pl.BlockSpec((narrow, 1, rows, width), lambda i: (0, at(i), 0, 0))
    return [spec] * 2, [shape_of((narrow, steps, rows, width), BF16)] * 2


def feed(core, attended, attended_t, one, two, cot_one, cot_two, mod, gain, w_out, w_up, w_down, wide, narrow, split):
    tokens, width = attended.shape
    part = tokens // 2
    hidden = w_up.shape[1]
    steps = hidden // width
    half, rows = (wide // 2, width // wide) if split else (1, 16)
    up_specs, up_shapes = grad_rows(steps, width, wide, split)
    down_specs, down_shapes = grad_columns(steps, width, narrow, split)
    small = whole((part, width))
    full = whole((tokens, width))
    return pl.pallas_call(
        feed_kernel,
        grid=(steps + 1,),
        in_specs=[
            pl.BlockSpec(memory_space=pltpu.SMEM),
            full,
            whole((width, tokens)),
            small,
            small,
            small,
            small,
            whole(mod.shape),
            whole((1, width)),
            whole((width, width)),
            pl.BlockSpec((width, width), lambda i: (0, jnp.minimum(i, steps - 1))),
            pl.BlockSpec((width, width), lambda i: (jnp.minimum(i, steps - 1), 0)),
        ],
        out_specs=[small, small, full, full, whole((8, width)), whole((width, width))]
        + up_specs
        + down_specs,
        out_shape=[
            shape_of((part, width), BF16),
            shape_of((part, width), BF16),
            shape_of((tokens, width), BF16),
            shape_of((tokens, width), F32),
            shape_of((8, width), F32),
            shape_of((width, width), BF16),
        ]
        + up_shapes
        + down_shapes,
        scratch_shapes=[
            pltpu.VMEM((tokens, width), F32),
            pltpu.VMEM((tokens, width), F32),
            pltpu.VMEM((tokens, width), BF16),
            pltpu.VMEM((width, tokens), BF16),
            pltpu.VMEM((tokens, width), BF16),
            pltpu.VMEM((width, tokens), BF16),
            pltpu.VMEM((tokens, width), F32),
            pltpu.VMEM((tokens, width), F32),
            pltpu.VMEM((half, 2, rows, width), BF16),
        ],
        compiler_params=params(44),
        cost_estimate=LIGHT,
        name="feed",
    )(core, attended, attended_t, one, two, cot_one, cot_two, mod, gain, w_out, w_up, w_down)


def project_back_kernel(groups, parts, core_ref, *refs):
    dq, d_own, received = refs[:groups], refs[groups : 2 * groups], refs[2 * groups : 3 * groups]
    refs_in = refs[3 * groups : 3 * groups + 13]
    norm_t, one, two, mod, gain_ref, weight, cosine, sine, d_middle, early, ada, about, out_grad = refs_in
    out_one, out_two, share = refs[3 * groups + 13 : 3 * groups + 16]
    grads = refs[3 * groups + 16 : -13]
    d_part, d_norm, whole_grad, held = refs[-13:-9]
    staged, sent = refs[-9:-7], refs[-7]
    step = pl.program_id(0)
    late, done = refs[-6:-1], refs[-1]
    copies = [
        pltpu.make_async_copy(source, target, done.at[index])
        for index, (source, target) in enumerate(zip((one, two, d_middle, ada, out_grad), late))
    ]

    @pl.when(step == 0)
    def fetch():
        for copy in copies:
            copy.start()

    one, two, d_middle, ada, out_grad = late
    part = one.shape[0]
    lanes = dq[0].shape[1]

    @pl.when(step == 0)
    def query():
        value = jnp.concatenate([ref[...] for ref in dq], axis=1).astype(F32)
        d_part[...] = rotate(value, cosine[...], -sine[...]).astype(BF16)

    @pl.when(step > 0)
    def other():
        for group in range(groups):
            total = d_own[group][0] + received[group][0].astype(F32)
            d_part[:, group * lanes : (group + 1) * lanes] = total.astype(BF16)

    @pl.when(step == 1)
    def key():
        d_part[...] = rotate(d_part[...].astype(F32), cosine[...], -sine[...]).astype(BF16)

    norm_step = ndot(d_part[...], weight[...])
    gradient = dot(norm_t[...], d_part[...]).astype(BF16)
    width = gradient.shape[1]
    if len(grads) == 1:
        grads[0][0] = gradient
    else:
        for index in range(3):

            @pl.when(step == index)
            def keep_gradient(index=index):
                whole_grad[:, index * width : (index + 1) * width] = gradient

    @pl.when(step == 0)
    def assign():
        d_norm[...] = norm_step

    @pl.when(step > 0)
    def add():
        d_norm[...] += norm_step

    def out_copies(index):
        return [
            pltpu.make_async_copy(staged[side].at[index], grads[side].at[index], sent.at[side, index])
            for side in range(2)
        ]

    def leave(index, core):
        staged[0][index] = held[:, core]
        staged[1][index] = held[:, 1 - core]
        for copy in out_copies(index):
            copy.start()

    @pl.when(step == 2)
    def end():
        for copy in copies:
            copy.wait()
        if len(grads) == 2:
            core = core_ref[0]
            half, rows = held.shape[0], held.shape[2]
            blocks = 2 * half
            count = 3 * width // parts
            rest = width // parts
            for index in range(parts):
                for block in range(blocks):
                    at = slice(block * rows, (block + 1) * rows)
                    held[block // 2, block % 2, :, :count] = whole_grad[at, index * count : (index + 1) * count]
                    held[block // 2, block % 2, :, count:] = out_grad[at, index * rest : (index + 1) * rest]
                leave(index, core)
        gain = gain_ref[...].astype(F32)
        scale = mod[1:2, :]
        plain = jnp.zeros_like(gain)
        both = jnp.zeros_like(gain)
        for index, (ref, out) in enumerate(((one, out_one), (two, out_two))):
            rows = slice(index * part, (index + 1) * part)
            xhat, inverse_std = normalize(ref[...].astype(F32))
            grad = d_norm[rows, :]
            back = normalize_back(grad * (gain * (1.0 + scale)), xhat, inverse_std)
            out[...] = (d_middle[rows, :] + back).astype(BF16)
            plain += jnp.sum(grad, axis=0, keepdims=True)
            both += jnp.sum(grad * xhat, axis=0, keepdims=True)
        share[0:1, :] = plain
        share[1:2, :] = both * gain
        share[2:7, :] = early[0:5, :]
        share[7:8, :] = both * (1.0 + scale)

        if len(grads) == 1:
            return
        blocks, rows = 2 * held.shape[0], held.shape[2]
        core = core_ref[0]
        flat = jnp.concatenate([share[index : index + 1, :] for index in range(6)], axis=1)
        depth = ada.shape[0]
        d_condition = jnp.sum(ada[...].astype(F32) * flat, axis=1, keepdims=True)
        embedded = about[:, :depth]
        gate = 1.0 / (1.0 + jnp.exp(-embedded))
        square = jnp.where(
            lax.broadcasted_iota(jnp.int32, (depth, depth), 0)
            == lax.broadcasted_iota(jnp.int32, (depth, depth), 1),
            d_condition,
            0.0,
        )
        d_embedded = jnp.sum(square, axis=0, keepdims=True) * gate * (1.0 + embedded * (1.0 - gate))
        count = flat.shape[1] // blocks
        place = lax.broadcasted_iota(jnp.int32, (EXTRA, width), 0)
        told_rest = width - about.shape[1] - 2 * rows
        for block in range(blocks):
            row = jnp.concatenate(
                [
                    flat[:, block * count : (block + 1) * count],
                    d_embedded,
                    jnp.zeros((1, width - count - depth), F32),
                ],
                axis=1,
            )
            told = jnp.concatenate(
                [
                    about[...],
                    share[7:8, block * rows : (block + 1) * rows],
                    share[6:7, block * rows : (block + 1) * rows],
                    jnp.zeros((1, told_rest), F32),
                ],
                axis=1,
            )
            mine = core_ref[1]
            value = jnp.where(place == mine, row, 0.0) + jnp.where(place == mine + blocks, told, 0.0)
            held[block // 2, block % 2, :EXTRA, :] = value.astype(BF16)
        leave(parts, core)
        for index in range(parts + 1):
            for copy in out_copies(index):
                copy.wait()


def project_back(
    core, dq, d_own, received, norm_t, one, two, mod, gain, weight, cosine, sine, d_middle, early, ada, about, out_grad, wide, narrow, split
):
    groups = len(dq)
    tokens, lanes = dq[0].shape
    width = groups * lanes
    part = tokens // 2
    small = whole((part, width))
    away = pl.BlockSpec(memory_space=pl.ANY)
    later = pl.BlockSpec((1, tokens, lanes), lambda i: (jnp.maximum(i - 1, 0), 0, 0))
    if split:
        half, rows = wide // 2, width // wide
        shape = (narrow + 1, half, rows, width)
        specs, shapes = [away] * 2, [shape_of(shape, BF16)] * 2
        scratch = [pltpu.VMEM((width, 3 * width), BF16), pltpu.VMEM((half, 2, rows, width), BF16)]
    else:
        specs, shapes = grad_rows(3, width, wide, split)
        scratch = [pltpu.VMEM((16, 128), BF16)] * 2
    return pl.pallas_call(
        functools.partial(project_back_kernel, groups, narrow),
        grid=(3,),
        in_specs=[pl.BlockSpec(memory_space=pltpu.SMEM)]
        + [whole((tokens, lanes))] * groups
        + [later] * (2 * groups)
        + [
            whole((width, tokens)),
            away,
            away,
            whole(mod.shape),
            whole((1, width)),
            pl.BlockSpec((width, width), lambda i: (0, i)),
            whole(cosine.shape),
            whole(sine.shape),
            away,
            whole(early.shape),
            away,
            whole(about.shape),
            away,
        ],
        out_specs=[small, small, whole((8, width))] + specs,
        out_shape=[
            shape_of((part, width), BF16),
            shape_of((part, width), BF16),
            shape_of((8, width), F32),
        ]
        + shapes,
        scratch_shapes=[
            pltpu.VMEM((tokens, width), BF16),
            pltpu.VMEM((tokens, width), F32),
        ]
        + scratch
        + ([pltpu.VMEM(shape, BF16)] * 2 if split else [pltpu.VMEM((16, 128), BF16)] * 2)
        + [pltpu.SemaphoreType.DMA((2, narrow + 1))]
        + [pltpu.VMEM(array.shape, array.dtype) for array in (one, two, d_middle, ada, out_grad)]
        + [pltpu.SemaphoreType.DMA((5,))],
        compiler_params=params(60),
        cost_estimate=LIGHT,
        name="project_back",
    )(core, *dq, *d_own, *received, norm_t, one, two, mod, gain, weight, cosine, sine, d_middle, early, ada, about, out_grad)


def add(target, to, keep, received, at):
    target[to] = keep[at] + received[at]


def halve(kind, words, keep, received, stay, leave):
    entries, blocks = keep.shape[:2]
    if kind == "near":
        n = words[2]
        for target, index in ((stay, n), (leave, n ^ 1)):
            for entry in range(entries // 4 * 2):
                at = entry // 2 * 4 + (index if entry % 2 == 0 else 3 - index)
                for block in range(blocks):
                    add(target, (entry, block), keep, received, (at, block))
        if entries % 4:
            for block in range(blocks):
                total = keep[entries - 1, block] + received[entries - 1, block]
                stay[entries // 4 * 2, block] = total
                leave[entries // 4 * 2, block] = total
        return
    bit = words[0 if kind == "x" else 1]
    for target, mine in ((stay, bit), (leave, 1 - bit)):
        for entry in range(entries):
            for block in range(blocks // 2):
                if blocks == 2:
                    at = mine
                elif kind == "x":
                    at = 2 * block + mine
                else:
                    at = 2 * mine + block
                add(target, (entry, block), keep, received, (entry, at))


def first_kernel(count, words, *refs):
    pairs_in = [(refs[2 * index], refs[2 * index + 1]) for index in range(count)]
    a_stay, a_leave, b_stay, b_leave, c_stay, c_leave = refs[2 * count :]
    step = pl.program_id(0)
    y, x = step // 2, step % 2
    n = words[2]

    def third(target, part, extra):
        entry = 0
        for keep, received in pairs_in:
            for index in range(keep.shape[0] if extra else keep.shape[0] // 4 * 4):
                rows = slice(part * THIRD, (part + 1) * THIRD)
                target[entry, 0] = keep[index, 0, rows, :] + received[index, 0, rows, :]
                entry += 1

    for target, match in ((a_stay, x == words[0]), (a_leave, x != words[0])):
        pl.when(match)(functools.partial(third, target, 0, True))
    for target, match in ((b_stay, y == words[1]), (b_leave, y != words[1])):
        pl.when(match)(functools.partial(third, target, 1, False))
    rows = slice(2 * THIRD, 3 * THIRD)
    for target, index in ((c_stay, n), (c_leave, n ^ 1)):
        for item, (keep, received) in enumerate(pairs_in):
            target[2 * item, 0] = keep[index, 0, rows, :] + received[index, 0, rows, :]
            target[2 * item + 1, 0] = keep[3 - index, 0, rows, :] + received[3 - index, 0, rows, :]


def first_stage(name, words, items):
    count = len(items)
    width = items[0][0].shape[3]
    entries = sum(keep.shape[0] for keep, unused in items)
    blocks_a = (entries, 2, THIRD, width)
    blocks_b = (4 * count, 2, THIRD, width)
    blocks_c = (2 * count, 4, THIRD, width)

    def spec(shape, index):
        return pl.BlockSpec((shape[0], 1, THIRD, width), index)

    def by_y(i, words):
        return (0, i // 2, 0, 0)

    def stay_x(i, words):
        return (0, jnp.clip(i - 2 * words[1], 0, 1), 0, 0)

    def leave_x(i, words):
        return (0, jnp.clip(i - 2 * (1 - words[1]), 0, 1), 0, 0)

    def each(i, words):
        return (0, i, 0, 0)

    in_specs, operands = [], []
    for keep, received in items:
        block = (keep.shape[0], 1) + keep.shape[2:]
        in_specs += [pl.BlockSpec(block, each)] * 2
        operands += [keep, received]
    return pl.pallas_call(
        functools.partial(first_kernel, count),
        grid_spec=pltpu.PrefetchScalarGridSpec(
            num_scalar_prefetch=1,
            grid=(4,),
            in_specs=in_specs,
            out_specs=[
                spec(blocks_a, by_y),
                spec(blocks_a, by_y),
                spec(blocks_b, stay_x),
                spec(blocks_b, leave_x),
                spec(blocks_c, each),
                spec(blocks_c, each),
            ],
        ),
        out_shape=[shape_of(shape, BF16) for shape in (blocks_a, blocks_b, blocks_c) for unused in range(2)],
        compiler_params=params(16),
        cost_estimate=LIGHT,
        name=name,
    )(words, *operands)


def call(kernel, name, shapes, operands, scratch=(), estimate=None):
    vmem = pl.BlockSpec(memory_space=pltpu.VMEM)
    return pl.pallas_call(
        kernel,
        in_specs=[pl.BlockSpec(memory_space=pltpu.SMEM)] + [vmem] * (len(operands) - 1),
        out_specs=[vmem] * len(shapes),
        out_shape=shapes,
        scratch_shapes=list(scratch),
        compiler_params=params(16),
        cost_estimate=estimate or LIGHT,
        name=name,
    )(*operands)


def next_kernel(kinds, words, *refs):
    for index, kind in enumerate(kinds):
        keep, received = refs[2 * index], refs[2 * index + 1]
        stay, leave = refs[2 * len(kinds) + 2 * index], refs[2 * len(kinds) + 2 * index + 1]
        halve(kind, words, keep, received, stay, leave)


def next_stage(name, kinds, words, kept, got, estimate=None):
    shapes, operands = [], [words]
    for kind, keep, received in zip(kinds, kept, got):
        entries, blocks, rows, columns = keep.shape
        if kind == "near":
            shape = (entries // 4 * 2 + entries % 4, blocks, rows, columns)
        else:
            shape = (entries, blocks // 2, rows, columns)
        shapes += [shape_of(shape, BF16)] * 2
        operands += [keep, received]
    outs = call(functools.partial(next_kernel, kinds), name, shapes, operands, estimate=estimate)
    return outs[::2], outs[1::2]


def far_kernel(words, *refs):
    keeps, gots, (stay, leave, *held) = refs[:3], refs[3:6], refs[6:]
    for third, (keep, received) in enumerate(zip(keeps, gots)):
        rows = slice(third * THIRD, (third + 1) * THIRD)
        for item in range(keep.shape[0] // 2):
            stay[item, rows, :] = keep[2 * item, 0].astype(F32) + received[2 * item, 0].astype(F32)
            leave[item, rows, :] = keep[2 * item + 1, 0] + received[2 * item + 1, 0]
    if held:
        for index, ref in enumerate((keeps[0], gots[0])):
            rows = slice(3 * THIRD + index * SMALL, 3 * THIRD + (index + 1) * SMALL)
            leave[0, rows, :] = ref[2, 0, :SMALL, :]
            held[0][index * SMALL : (index + 1) * SMALL, :] = ref[2, 0, :SMALL, :]


def far_stage(name, words, kept, got):
    count = kept[1].shape[0] // 2
    width = kept[0].shape[3]
    extra = kept[0].shape[0] % 2
    rows = 3 * THIRD
    shapes = [
        shape_of((count, rows, width), F32),
        shape_of((count, rows + extra * 2 * SMALL, width), BF16),
    ]
    if extra:
        shapes.append(shape_of((2 * SMALL, width), BF16))
    return call(far_kernel, name, shapes, (words, *kept, *got))


def end_kernel(words, keep, received, up, down):
    up[...] = keep[0] + received[0].astype(F32)
    total = keep[1] + received[1].astype(F32)
    rows, columns = total.shape
    down[:, :rows] = total[:, : columns // 2].T
    down[:, rows:] = total[:, columns // 2 :].T


def last_kernel(words, own, got, held, qkv, out, ada, table, gain_one, gain_two, mods, about, wide):
    n, w = words[2], words[3]
    rows, first = qkv.shape
    total = own[0] + got[0, :rows, :].astype(F32)
    qkv[...] = total[:, :first]
    out[...] = total[:, first:]
    slots = mods.shape[0] // 4
    count = ada.shape[1]
    depth = wide.shape[0]
    part = ada.shape[0]
    for index in range(4):
        ref, at = (held, index * SMALL) if index < 2 else (got.at[0], rows + (index - 2) * SMALL)
        value = ref[at : at + 2 * slots, :].astype(F32)
        mods[index * slots : (index + 1) * slots, :] = value[:slots, :]
        about[index * slots : (index + 1) * slots, :] = value[slots:, :]
    gains = jnp.sum(about[:, 3 * depth : 3 * depth + 2 * rows], axis=0, keepdims=True)
    gain_one[...] = gains[:, :rows]
    gain_two[...] = gains[:, rows : 2 * rows]
    embedded = about[:, :depth]
    condition = (embedded / (1.0 + jnp.exp(-embedded))).astype(BF16)
    turned = (((0,), (0,)), ((), ()))
    wide[...] = lax.dot_general(
        condition, mods[:, :count].astype(BF16), turned, preferred_element_type=F32
    )
    ada[...] = wide[pl.ds(n * part, part), :]
    time = about[:, depth : depth + 1] * 32.0 + about[:, depth + 1 : depth + 2]
    times = table.shape[0]
    lane = lax.broadcasted_iota(jnp.int32, (mods.shape[0], times), 1) + w * times
    onehot = jnp.where(time.astype(jnp.int32) == lane, 1.0, 0.0).astype(BF16)
    grad = lax.dot_general(
        onehot, mods[:, count : count + depth].astype(BF16), turned, preferred_element_type=F32
    )
    value = grad[:, :part]
    for index in range(1, depth // part):
        value = jnp.where(n == index, grad[:, index * part : (index + 1) * part], value)
    table[...] = value


def last(words, own, got, held, qkv_shape, out_shape, ada_shape, table_shape, depth, wide):
    rows = qkv_shape[0]
    width = own.shape[2]
    return call(
        last_kernel,
        "last",
        [shape_of(qkv_shape, F32), shape_of(out_shape, F32), shape_of(ada_shape, F32), shape_of(table_shape, F32)]
        + [shape_of((1, rows), F32)] * 2,
        (words, own, got, held),
        [
            pltpu.VMEM((4 * wide, width), F32),
            pltpu.VMEM((4 * wide, width), F32),
            pltpu.VMEM((depth, ada_shape[1]), F32),
        ],
    )


def make(wide, narrow):
    wide_bits = wide.bit_length() - 1

    def first_message(w, n):
        p, c = w // 2, w % 2
        return 2 * p + n // 2, 2 * c + n % 2

    def second_message(w, n):
        p, c = w // 2, w % 2
        return 2 * p + n // 2, 2 * c + 1 - n % 2

    message_one = pairs(wide, narrow, first_message)
    message_two = pairs(wide, narrow, second_message)
    flip = [pairs(wide, narrow, lambda w, n, b=b: (w ^ (1 << b), n)) for b in range(wide_bits)]
    line = [pairs(wide, narrow, lambda w, n, m=m: (w, n ^ m)) for m in range(1, narrow)]
    split = wide == 8

    def on_device(
        hidden_in,
        positions,
        time_index,
        cond_table,
        ada_weight,
        norm1_gain,
        qkv_weight,
        out_weight,
        norm2_gain,
        up_weight,
        down_weight,
        cotangent,
    ):
        w = lax.axis_index("wide")
        n = lax.axis_index("narrow")
        core = w % 2
        core_word = jnp.stack([core, w]).astype(jnp.int32)
        words = jnp.stack([(w >> 1) & 1, (w >> 2) & 1, n, w]).astype(jnp.int32)
        width = hidden_in.shape[2]
        odd = n % 2

        def take(array, index):
            return lax.dynamic_index_in_dim(array, index, axis=0, keepdims=False)

        def spread(array):
            one = lax.ppermute(take(array, odd), AXES, message_one)
            two = lax.ppermute(take(array, 1 - odd), AXES, message_two)
            return one, two

        def permute(array, table):
            return lax.ppermute(array, AXES, table)

        def across(sends):
            return [permute(send, line[index]) for index, send in enumerate(sends)]

        def reduce_blocks(current):
            for bit in range(wide_bits):
                mine = (w >> bit) & 1
                current = current.reshape((-1, 2) + current.shape[1:])
                send = lax.dynamic_index_in_dim(current, 1 - mine, axis=1, keepdims=False)
                keep = lax.dynamic_index_in_dim(current, mine, axis=1, keepdims=False)
                received = permute(send, flip[bit])
                current = (keep.astype(F32) + received.astype(F32)).astype(BF16)
            current = current[0]
            total = take(current, n).astype(F32)
            for mask in range(1, narrow):
                total += permute(take(current, n ^ mask), line[mask - 1]).astype(F32)
            return total

        wait = lax.optimization_barrier
        hidden_one, hidden_two = spread(hidden_in)
        other_time = permute(time_index, flip[0])
        positions, other_time = wait((positions, other_time))
        place_one, place_two = spread(positions)
        row_time = jnp.where(n // 2 == core, time_index[n % 2], other_time[n % 2])
        embedded = lax.dynamic_slice_in_dim(cond_table, row_time, 1, axis=0).astype(F32)
        condition = (embedded * jax.nn.sigmoid(embedded)).astype(BF16)
        modulation = dot(condition, ada_weight).reshape(6, width)
        mod = jnp.concatenate([modulation, jnp.zeros((2, width), F32)])
        gain_one = norm1_gain.reshape(1, width)
        gain_two = norm2_gain.reshape(1, width)
        depth = cond_table.shape[1]
        pair = jnp.stack([row_time // 32, row_time % 32]).astype(F32).reshape(1, 2)
        about = jnp.concatenate(
            [embedded, pair, jnp.zeros((1, 2 * depth - 2), F32)], axis=1
        )

        place = jnp.concatenate([place_one, place_two]).astype(F32)
        lane = jnp.arange(128, dtype=jnp.int32)
        frequency = 10000.0 ** (-(lane % HALF).astype(F32) / HALF)
        angles = place[:, None] * frequency
        cosine = jnp.cos(angles)
        sine = jnp.sin(angles) * jnp.where(lane % HEAD_DIM < HALF, -1.0, 1.0)

        hidden_one, hidden_two, cotangent = wait((hidden_one, hidden_two, cotangent))
        cot_one, cot_two = spread(cotangent)
        q, kv, norm_t = project(hidden_one, hidden_two, mod, gain_one, qkv_weight, cosine, sine)
        kv_other = permute(kv, flip[0])
        attended, attended_t, log_total = attend(q, kv, kv_other)
        out_one, out_two, d_attended, d_middle, sums_two, out_grad, *grads = feed(
            core_word,
            attended,
            attended_t,
            hidden_one,
            hidden_two,
            cot_one,
            cot_two,
            mod,
            gain_two,
            out_weight,
            up_weight,
            down_weight,
            wide,
            narrow,
            split,
        )
        grads_feed = grads
        dq, d_own, received = [], [], []

        def back_group(group, q):
            first, second, third = attend_back(q, kv, kv_other, d_attended, attended_t, log_total, group)
            dq.append(first)
            d_own.append(second)
            received.append(permute(third, flip[0]))

        rows = width // wide
        if split:
            axes = {"x": flip[1], "y": flip[2], "near": line[0], "far": line[2]}

            def exchange(kinds, sends):
                return [permute(send, axes[kind]) for kind, send in zip(kinds, sends)]

            turns = [("x", "y", "near"), ("y", "near", "x"), ("near", "x", "y")]
            up_keep, up_send, down_keep, down_send = grads
            down_got = permute(down_send, flip[0])
            up_got = permute(up_send, flip[0])
            back_group(0, q)
            d_own[0], up_got, down_got = wait((d_own[0], up_got, down_got))
            stages = first_stage("first_feed", words, [(up_keep, up_got), (down_keep, down_got)])
            kept, sends = stages[::2], stages[1::2]
            got = exchange(turns[0], sends)
            out_one, out_two, q, *sends = wait((out_one, out_two, q, *sends))
            out_one = permute(out_one, inverse(message_one))
            back_group(1, q)
            q, d_own[1], received[0] = wait((q, d_own[1], received[0]))
            back_group(2, q)
            dq[2], received[1], out_one, out_two, *got = wait((dq[2], received[1], out_one, out_two, *got))
            out_two = permute(out_two, inverse(message_two))
            kept, sends = next_stage("second_feed", turns[1], words, kept, got)
            got = exchange(turns[1], sends)
            dq[0], *sends = wait((dq[0], *sends))
        else:
            out_one = permute(out_one, inverse(message_one))
            out_two = permute(out_two, inverse(message_two))
            for group in range(width // (GROUP * HEAD_DIM)):
                back_group(group, q)

        grad_one, grad_two, share, *grads = project_back(
            core_word,
            dq,
            d_own,
            received,
            norm_t,
            hidden_one,
            hidden_two,
            mod,
            gain_one,
            qkv_weight,
            cosine,
            sine,
            d_middle,
            sums_two,
            ada_weight,
            about,
            out_grad,
            wide,
            narrow,
            split,
        )

        def join(one, two):
            return jnp.stack([jnp.where(odd == 0, one, two), jnp.where(odd == 0, two, one)])

        row_count = depth // narrow
        column_count = 6 * width // wide
        time_count = cond_table.shape[0] // wide
        if split:
            qkv_keep, qkv_send = grads
            qkv_got = permute(qkv_send, flip[0])
            out_two, grad_first = wait((out_two, grad_one))
            grad_one = permute(grad_one, inverse(message_one))
            grad_first, out_two, *got = wait((grad_first, out_two, *got))
            kept, sends = next_stage("third_feed", turns[2], words, kept, got, HEAVY)
            got = exchange(turns[2], sends)
            qkv_got, *sends = wait((qkv_got, *sends))
            stages = first_stage("first_qkv", words, [(qkv_keep, qkv_got)])
            kept_qkv, sends = stages[::2], stages[1::2]
            got[0], got[1], got[2], *sends = wait((*got, *sends))
            grad_one, grad_two, sends[2] = wait((grad_one, grad_two, sends[2]))
            got_qkv = exchange(turns[0], sends)
            *got, sends[0] = wait((*got, sends[0]))
            own, send = far_stage("far_feed", words, kept, got)
            far_got = permute(send, axes["far"])
            *got_qkv, send = wait((*got_qkv, send))
            kept_qkv, sends = next_stage("second_qkv", turns[1], words, kept_qkv, got_qkv)
            got_qkv = exchange(turns[1], sends)
            far_got, grad_two, *sends = wait((far_got, grad_two, *sends))
            grad_two = permute(grad_two, inverse(message_two))
            grad_up, grad_down = call(
                end_kernel,
                "end_feed",
                [shape_of((rows, width), F32), shape_of((width // 2, width // narrow), F32)],
                (words, own, far_got),
            )
            *got_qkv, grad_up = wait((*got_qkv, grad_up))
            kept_qkv, sends = next_stage("third_qkv", turns[2], words, kept_qkv, got_qkv)
            got_qkv = exchange(turns[2], sends)
            own, send, held = far_stage("far_qkv", words, kept_qkv, got_qkv)
            far_got = permute(send, axes["far"])
            grad_one, grad_two, send = wait((grad_one, grad_two, send))
            hidden_grad = join(grad_one, grad_two)
            far_got, hidden_grad = wait((far_got, hidden_grad))
            grad_qkv, grad_out, grad_ada, grad_table, grad_gain_one, grad_gain_two = last(
                words,
                own,
                far_got,
                held,
                (rows, 3 * width // narrow),
                (rows, width // narrow),
                (row_count, column_count),
                (time_count, row_count),
                depth,
                wide,
            )
            gains = grad_gain_two.reshape(rows), grad_gain_one.reshape(rows)
        else:
            up_grad, down_grad = grads_feed
            (qkv_grad,) = grads
            grad_one = permute(grad_one, inverse(message_one))
            grad_two = permute(grad_two, inverse(message_two))
            hidden_grad = join(grad_one, grad_two)
            steps = down_grad.shape[0]
            grad_up = reduce_blocks(up_grad.reshape(narrow, wide, rows, width).transpose(1, 0, 2, 3))
            grad_down = reduce_blocks(
                down_grad.reshape(steps, narrow, width // narrow, wide // steps, -1)
                .transpose(0, 3, 1, 2, 4)
                .reshape(wide, narrow, width // narrow, -1)
            ).T

            def by_rows(grad):
                return reduce_blocks(
                    grad.transpose(1, 0, 2).reshape(wide, rows, narrow, -1).transpose(0, 2, 1, 3)
                )

            grad_out = by_rows(out_grad[None])
            grad_qkv = by_rows(qkv_grad)
            told = jnp.concatenate(
                [embedded, jnp.broadcast_to(row_time.astype(F32), (1, width - depth))], axis=1
            )
            share = jnp.concatenate([share, told])[None]
            for table in flip + [line[0], line[2]]:
                share = jnp.concatenate([share, permute(share, table)])
            all_mod = share[:, :6].reshape(-1, 6 * width)
            gains = jnp.sum(share[:, 6:8].reshape(-1, 2, wide, rows), axis=0)
            gains = lax.dynamic_index_in_dim(gains, w, axis=1, keepdims=False)
            my_embedded = lax.dynamic_slice_in_dim(share[:, 8, :depth], n * row_count, row_count, axis=1)
            times = share[:, 8, depth].astype(jnp.int32)
            my_gate = jax.nn.sigmoid(my_embedded)
            my_conditions = (my_embedded * my_gate).astype(BF16).astype(F32)
            my_mod = lax.dynamic_slice_in_dim(all_mod, w * column_count, column_count, axis=1)
            grad_ada = lax.dot_general(
                my_conditions,
                my_mod,
                (((0,), (0,)), ((), ())),
                precision=HIGHEST,
                preferred_element_type=F32,
            )
            my_ada = lax.dynamic_slice_in_dim(ada_weight, n * row_count, row_count, axis=0).astype(F32)
            d_condition = lax.dot_general(
                all_mod,
                my_ada,
                (((1,), (1,)), ((), ())),
                precision=HIGHEST,
                preferred_element_type=F32,
            )
            d_embedded = d_condition * my_gate * (1.0 + my_embedded * (1.0 - my_gate))
            my_times = w * time_count + jnp.arange(time_count, dtype=jnp.int32)
            onehot = (my_times[:, None] == times[None, :]).astype(F32)
            grad_table = jnp.dot(onehot, d_embedded, precision=HIGHEST, preferred_element_type=F32)
        return (
            join(out_one, out_two),
            hidden_grad,
            grad_table,
            grad_ada,
            gains[1],
            grad_qkv,
            grad_out,
            gains[0],
            grad_up,
            grad_down,
        )

    return on_device


def solution(mesh):
    in_specs = (
        P("wide", "narrow", None),
        P("wide", "narrow"),
        P("wide"),
        P(),
        P(),
        P(),
        P(),
        P(),
        P(),
        P(),
        P(),
        P("wide", "narrow", None),
    )
    out_specs = (
        P("wide", "narrow", None),
        P("wide", "narrow", None),
        P("wide", "narrow"),
        P("narrow", "wide"),
        P("wide"),
        P("wide", "narrow"),
        P("wide", "narrow"),
        P("wide"),
        P("wide", "narrow"),
        P("wide", "narrow"),
    )
    return jax.shard_map(
        make(mesh.shape["wide"], mesh.shape["narrow"]),
        mesh=mesh,
        in_specs=in_specs,
        out_specs=out_specs,
        check_vma=False,
    )
```
